128 devices in a mesh: group: 16 (over y, x_lo, core), fsdp: 8 (over x_hi, z).
Axes of the slice: x: 4 (x_hi: 2, x_lo: 2; x = x_hi * 2 + x_lo), y: 4, z: 4, core: 2. Of those that a mesh axis runs over, the one named last changes fastest.
Arguments:
- query_embeddings: bfloat16 [512, 4096], P(('group', 'fsdp')), may hold values from -4 to 4
- passage_embeddings: bfloat16 [512, 4096], P(('group', 'fsdp')), may hold values from -4 to 4
- positives: int32 [512], P(('group', 'fsdp')), may hold values from 0 to 511, each once
- logarithm_scale: float32 [], replicated, may hold values from 2.4 to 2.8
- residual_input: bfloat16 [128, 256, 4096], P(('group', 'fsdp')), may hold values from -6 to 6
- attention_head_outputs: bfloat16 [128, 256, 4096], P(('group', 'fsdp')), may hold values from -6 to 6
- output_weight: bfloat16 [4096, 4096], P('fsdp'), may hold values from -0.09375 to 0.09375
- adapter_down_weight: bfloat16 [4096, 16], replicated, may hold values from -0.09375 to 0.09375
- adapter_up_weight: bfloat16 [16, 4096], replicated, may hold values from -0.375 to 0.375
- final_norm_weight: float32 [4096], replicated, may hold values from 0.5 to 1.5
- lengths: int32 [128], P(('group', 'fsdp')), may hold values from 64 to 256
Outputs:
- loss: float32 [], replicated
- scale_grad: float32 [], replicated
- query_grad: float32 [512, 4096], P(('group', 'fsdp'))
- passage_grad: float32 [512, 4096], P(('group', 'fsdp'))
- attn_grad: bfloat16 [128, 256, 4096], P(('group', 'fsdp'))
- residual_grad: bfloat16 [128, 256, 4096], P(('group', 'fsdp'))
- lora_down_grad: float32 [4096, 16], replicated
- lora_up_grad: float32 [16, 4096], replicated
The draws below stay inside these ranges and needn't reach their ends.
All inputs are finite; a program needn't handle non-finite values.
Results may differ from the reference program's by a relative error of at most 0.01.
Values may be sent and summed in bfloat16 or wider, within the bound.
No kernel may reach another device: no remote copies, remote signals or barrier semaphores. Data moves between devices by JAX's collectives and lax.ppermute only.
A program may use at most 128 MiB of HBM per device.

```python
import jax
import jax.numpy as jnp
from jax import lax

MODEL_DIMENSION = 4096
HEAD_FEATURES = 4096
ADAPTER_RANK = 16
SEQ = 256
ROWS_DEV = 1
Q_DEV = 4
B = 512
SEQS = 128


def draw_pair(key):
    base = jax.random.fold_in(key, 17)
    keys = jax.random.split(base, 2)
    queries = 0.06 * jax.random.normal(keys[0], (B, MODEL_DIMENSION), jnp.float32)
    passages = 0.06 * jax.random.normal(keys[1], (B, MODEL_DIMENSION), jnp.float32)
    return (jnp.clip(queries, -4.0, 4.0), jnp.clip(passages, -4.0, 4.0))


def draw_query_embeddings(key, part):
    return draw_pair(key)[0].astype(jnp.bfloat16)


def draw_passage_embeddings(key, part):
    return draw_pair(key)[1].astype(jnp.bfloat16)


def touch_ends(result, stream_key, smallest, high):
    longest = result.shape.index(max(result.shape))
    spots = []
    for shift in (0, 1):
        where = [jax.random.randint(jax.random.fold_in(stream_key, axis), (), 0, length) for axis, length in enumerate(result.shape)]
        where[longest] = (where[longest] + shift) % result.shape[longest]
        spots.append(tuple(where))
    return result.at[spots[0]].set(smallest).at[spots[1]].set(high)


def block_scale(stream_key, extent, shards, smallest, high):
    def one(dim, parts):
        steps = jax.random.uniform(jax.random.fold_in(jax.random.fold_in(stream_key, 6), dim), (parts,), jnp.float32, smallest / len(shards), high / len(shards))
        return jnp.repeat(jnp.exp(steps), extent[dim] // parts).reshape((-1,) + (1,) * (len(extent) - dim - 1))

    gain = one(*shards[0])
    for cut in shards[1:]:
        gain = gain * one(*cut)
    return gain


def noise(key, extent, width, limit, cuts=(), kind=jnp.bfloat16):
    entries = jax.random.normal(key, extent, jnp.float32) * width
    if len(cuts) > 0:
        entries = block_scale(key, extent, cuts, -0.22, 0.18) * entries
    return jnp.clip(entries, min=-limit, max=limit).astype(kind)


def setup_inputs(seed: int = 0) -> dict:
    streams_of = jax.random.split(jax.random.key(seed), 12)
    query_embeddings = draw_query_embeddings(jax.random.fold_in(streams_of[11], 71), 0)
    passage_embeddings = draw_passage_embeddings(jax.random.fold_in(streams_of[11], 71), 0)
    positives = jax.random.permutation(streams_of[2], B).astype(jnp.int32)
    logarithm_scale = jnp.clip(jax.random.uniform(streams_of[3], (), jnp.float32, 2.4, 2.8), 2.4, 2.8)
    residual_input = noise(streams_of[4], (SEQS, SEQ, MODEL_DIMENSION), 1.0, 6.0, ((0, 128),))
    attention_head_outputs = noise(streams_of[5], (SEQS, SEQ, HEAD_FEATURES), 1.0, 6.0, ((0, 128),))
    output_weight = noise(streams_of[6], (HEAD_FEATURES, MODEL_DIMENSION), HEAD_FEATURES ** -0.5, 0.09375, ((0, 8),))
    adapter_down_weight = noise(streams_of[7], (HEAD_FEATURES, ADAPTER_RANK), HEAD_FEATURES ** -0.5, 0.09375)
    adapter_up_weight = noise(streams_of[8], (ADAPTER_RANK, MODEL_DIMENSION), (ADAPTER_RANK * 16) ** -0.5, 0.375)
    final_norm_weight = jnp.clip(1.0 + 0.1 * jax.random.normal(streams_of[9], (MODEL_DIMENSION,), jnp.float32), 0.5, 1.5)
    lengths = touch_ends(jax.random.randint(streams_of[10], (SEQS,), SEQ // 4, SEQ + 1), jax.random.fold_in(streams_of[10], 1), SEQ // 4, SEQ).astype(jnp.int32)
    return dict(query_embeddings=query_embeddings, passage_embeddings=passage_embeddings, positives=positives, logarithm_scale=logarithm_scale, residual_input=residual_input, attention_head_outputs=attention_head_outputs, output_weight=output_weight, adapter_down_weight=adapter_down_weight, adapter_up_weight=adapter_up_weight, final_norm_weight=final_norm_weight, lengths=lengths)


grad_scale = 512.0
adapter_scale = 2.0
epsilon = 1e-05

def reference(query_embeddings, passage_embeddings, positives, logarithm_scale, residual_input, attention_head_outputs, output_weight, adapter_down_weight, adapter_up_weight, final_norm_weight, lengths):
    logit_scale = jnp.exp(logarithm_scale)
    logits = logit_scale * jnp.dot(query_embeddings, passage_embeddings.T, preferred_element_type=jnp.float32)
    row_max = lax.optimization_barrier(jnp.max(logits, axis=1))
    log_norm = row_max + jnp.log(lax.optimization_barrier(jnp.sum(jnp.exp(logits - row_max[:, None]), axis=1)))
    column = jnp.arange(B, dtype=jnp.int32)
    onehot = (column[None, :] == positives[:, None]).astype(jnp.float32)
    pos_logit = lax.optimization_barrier(jnp.sum(onehot * logits, axis=1))
    loss = jnp.mean(log_norm - pos_logit)
    weights = jnp.exp(logits - log_norm[:, None])
    scale_grad = jnp.mean(lax.optimization_barrier(jnp.sum(weights * logits, axis=1)) - pos_logit)
    weight_half = weights.astype(jnp.bfloat16)
    hot_half = onehot.astype(jnp.bfloat16)
    query_grad = logit_scale * (jnp.dot(weight_half, passage_embeddings, preferred_element_type=jnp.float32) - jnp.dot(hot_half, passage_embeddings, preferred_element_type=jnp.float32))
    passage_grad = logit_scale * (jnp.dot(weight_half.T, query_embeddings, preferred_element_type=jnp.float32) - jnp.dot(hot_half.T, query_embeddings, preferred_element_type=jnp.float32))
    row_grads = query_grad.reshape(B // Q_DEV, Q_DEV, MODEL_DIMENSION)[:, :ROWS_DEV].reshape(SEQS, MODEL_DIMENSION)
    position = jnp.arange(SEQ, dtype=jnp.int32)

    def per_sequence(carried_state, sequence_items):
        residual_vector_row, head_feature_row, row_grad, length = sequence_items
        projected_output = jnp.dot(head_feature_row, output_weight, preferred_element_type=jnp.float32)
        reduced_activation = jnp.dot(head_feature_row, adapter_down_weight, preferred_element_type=jnp.float32).astype(jnp.bfloat16)
        hidden_state = residual_vector_row.astype(jnp.float32) + projected_output + adapter_scale * jnp.dot(reduced_activation, adapter_up_weight, preferred_element_type=jnp.float32)
        inv_rms = lax.rsqrt(lax.optimization_barrier(jnp.mean(hidden_state * hidden_state, axis=1)) + epsilon)
        weight = grad_scale * (position < length).astype(jnp.float32) / length.astype(jnp.float32)
        gained = weight[:, None] * row_grad[None, :] * final_norm_weight[None, :]
        hidden_grad = inv_rms[:, None] * gained - hidden_state * (inv_rms * inv_rms * inv_rms * lax.optimization_barrier(jnp.mean(gained * hidden_state, axis=1)))[:, None]
        gradient_portion = hidden_grad.astype(jnp.bfloat16)
        reduced_gradient = (adapter_scale * jnp.dot(gradient_portion, adapter_up_weight.T, preferred_element_type=jnp.float32)).astype(jnp.bfloat16)
        head_gradient = (jnp.dot(gradient_portion, output_weight.T, preferred_element_type=jnp.float32) + jnp.dot(reduced_gradient, adapter_down_weight.T, preferred_element_type=jnp.float32)).astype(jnp.bfloat16)
        down_acc = carried_state[0] + jnp.dot(head_feature_row.T, reduced_gradient, preferred_element_type=jnp.float32)
        up_weight_accumulator = carried_state[1] + adapter_scale * jnp.dot(reduced_activation.T, gradient_portion, preferred_element_type=jnp.float32)
        return ((down_acc, up_weight_accumulator), (head_gradient, gradient_portion))
    initial = (jnp.zeros((HEAD_FEATURES, ADAPTER_RANK), jnp.float32), jnp.zeros((ADAPTER_RANK, MODEL_DIMENSION), jnp.float32))
    sums, grads = lax.scan(per_sequence, initial, (residual_input, attention_head_outputs, row_grads, lengths))
    return (loss, scale_grad, query_grad, passage_grad, grads[0], grads[1], sums[0] / SEQS, sums[1] / SEQS)
```

```python
import functools

import jax
import jax.numpy as jnp
from jax import lax
from jax.experimental import pallas as pl
from jax.experimental.pallas import tpu as pltpu
from jax.sharding import PartitionSpec as P

grad_scale = 512.0
adapter_scale = 2.0
epsilon = 1e-05
AX = ("group", "fsdp")
NT = (((1,), (1,)), ((), ()))
TN = (((0,), (0,)), ((), ()))
f32 = jnp.float32
bf16 = jnp.bfloat16


def coords(i):
    g, f = divmod(i, 8)
    return (f // 4) * 2 + (g // 2) % 2, g // 4, f % 4, g % 2


def device(x, y, z, c):
    x, y, z = x % 4, y % 4, z % 4
    return ((y * 2 + x % 2) * 2 + c) * 8 + (x // 2) * 4 + z


def table(move):
    return [(i, device(*move(*coords(i)))) for i in range(128)]


MOVES = {
    "core": table(lambda x, y, z, c: (x, y, z, 1 - c)),
    "xnear": table(lambda x, y, z, c: (x ^ 1, y, z, c)),
    "xflip": table(lambda x, y, z, c: (3 - x, y, z, c)),
    "ynear": table(lambda x, y, z, c: (x, y ^ 1, z, c)),
    "yflip": table(lambda x, y, z, c: (x, 3 - y, z, c)),
    "znear": table(lambda x, y, z, c: (x, y, z ^ 1, c)),
    "zflip": table(lambda x, y, z, c: (x, y, 3 - z, c)),
    "yup": table(lambda x, y, z, c: (x, y + 1, z, c)),
    "ydown": table(lambda x, y, z, c: (x, y - 1, z, c)),
    "zup": table(lambda x, y, z, c: (x, y, z + 1, c)),
    "zdown": table(lambda x, y, z, c: (x, y, z - 1, c)),
    "zfar": table(lambda x, y, z, c: (x, y, z + 2, c)),
}


def send(value, move, name):
    with jax.named_scope(name):
        return lax.ppermute(value, AX, MOVES[move])


def ordered(bit, mine, other, axis=0):
    return jnp.where(
        bit == 0,
        jnp.concatenate([mine, other], axis=axis),
        jnp.concatenate([other, mine], axis=axis),
    )


def pick(value, start, size, axis=0):
    return lax.dynamic_slice_in_dim(value, start, size, axis=axis)


def block_kernel(copies, n, has_y, last, scal, *refs):
    refs = list(refs)
    n_src = 1 + max(src for src, *_ in copies)
    srcs = refs[:n_src]
    a_own, a_par, res, low, up, q_rows, q_f = refs[n_src : n_src + 7]
    pos = n_src + 7
    y_in = None
    if has_y:
        y_in, st_in = refs[pos : pos + 2]
        pos += 2
    if last:
        hid_out, st_out, y_own, y_par, y_q = refs[pos : pos + 5]
        pos += 5
    else:
        hid_out, st_out, y_out = refs[pos : pos + 3]
        pos += 3
    w_s, a_s, y_s, hb_s, w_sem, a_sem, y_sem = refs[pos : pos + 7]

    started = []
    for k, (src, src_row, src_col, rows, shard, dst_row, dst_col, cols) in enumerate(copies):
        ref = srcs[src]
        if src_col is None:
            view = ref.at[pl.ds(src_row, rows), :]
        else:
            view = ref.at[pl.ds(src_row, rows), pl.ds(pl.multiple_of(scal[src_col], 256), cols)]
        first = pl.multiple_of(scal[shard] * 512 + dst_row, 256)
        if isinstance(dst_col, tuple):
            col = pl.multiple_of(scal[dst_col[0]] * 256, 256)
        else:
            col = dst_col
        copy = pltpu.make_async_copy(view, w_s.at[pl.ds(first, rows), pl.ds(col, cols)], w_sem.at[k])
        copy.start()
        started.append((shard, copy))
    ca = pltpu.make_async_copy(a_own, a_s.at[pl.ds(0, 256), :], a_sem.at[0])
    cp = pltpu.make_async_copy(a_par, a_s.at[pl.ds(256, 256), :], a_sem.at[1])
    ca.start()
    cp.start()
    if has_y:
        cy = pltpu.make_async_copy(y_in, y_s, y_sem.at[8])
        cy.start()
    ca.wait()
    cp.wait()
    hid_out[...] = res[...].astype(f32) + adapter_scale * jnp.dot(
        low[...], up[...], preferred_element_type=f32
    )
    for shard in range(8):
        for owner, copy in started:
            if owner == shard:
                copy.wait()
        first = pl.multiple_of(scal[shard] * 512, 512)
        hid_out[...] += jnp.dot(
            a_s[:, pl.ds(first, 512)], w_s[pl.ds(first, 512), :], preferred_element_type=f32
        )
    hid = hid_out[...]
    hb_s[pl.ds(0, 512), :] = hid.astype(bf16)
    hb_s[pl.ds(512, 16), :] = q_rows[...]
    sumsq = jnp.sum(hid * hid, axis=1, keepdims=True)
    dot_own = jnp.sum(hid[:256] * q_f[0:1, :], axis=1, keepdims=True)
    dot_par = jnp.sum(hid[256:] * q_f[1:2, :], axis=1, keepdims=True)
    down = lax.dot_general(hb_s[...], up[...], NT, preferred_element_type=f32)
    if has_y:
        st_out[...] = st_in[...]
    else:
        st_out[...] = jnp.zeros_like(st_out)
    st_out[:, 0:16] += down
    st_out[0:512, 16:17] += sumsq
    st_out[0:256, 17:18] += dot_own
    st_out[256:512, 17:18] += dot_par
    if has_y:
        cy.wait()
    outs = []
    for shard in range(8):
        first = pl.multiple_of(scal[shard] * 512, 512)
        part = lax.dot_general(
            hb_s[...], w_s[pl.ds(first, 512), :], NT, preferred_element_type=f32
        )
        if has_y:
            part += y_s[:, pl.ds(first, 512)]
        if last:
            y_own[:, pl.ds(first, 512)] = part[:256]
            y_par[:, pl.ds(first, 512)] = part[256:512].astype(bf16)
            y_q[:, pl.ds(first, 512)] = part[512:]
        else:
            y_s[:, pl.ds(first, 512)] = part
            out = pltpu.make_async_copy(
                y_s.at[:, pl.ds(first, 512)], y_out.at[:, pl.ds(first, 512)], y_sem.at[shard]
            )
            out.start()
            outs.append(out)
    for out in outs:
        out.wait()


def block_call(copies, srcs, scal, a_own, a_par, res, low, up, q_rows, q_f, carry, last, name):
    n = res.shape[1]
    has_y = carry is not None
    vm = pl.BlockSpec(memory_space=pltpu.VMEM)
    anyspace = pl.BlockSpec(memory_space=pl.ANY)
    in_specs = [pl.BlockSpec(memory_space=pltpu.SMEM)] + [anyspace] * (len(srcs) + 2) + [vm] * 5
    args = [scal, *srcs, a_own, a_par, res, low, up, q_rows, q_f]
    if has_y:
        in_specs += [anyspace, vm]
        args += list(carry)
    shapes = [jax.ShapeDtypeStruct((512, n), f32), jax.ShapeDtypeStruct((528, 128), f32)]
    out_specs = [vm, vm]
    if last:
        shapes += [
            jax.ShapeDtypeStruct((256, 4096), f32),
            jax.ShapeDtypeStruct((256, 4096), bf16),
            jax.ShapeDtypeStruct((16, 4096), f32),
        ]
        out_specs += [vm, vm, vm]
    else:
        shapes += [jax.ShapeDtypeStruct((528, 4096), f32)]
        out_specs += [anyspace]
    return pl.pallas_call(
        functools.partial(block_kernel, copies, n, has_y, last),
        out_shape=shapes,
        in_specs=in_specs,
        out_specs=out_specs,
        scratch_shapes=[
            pltpu.VMEM((4096, n), bf16),
            pltpu.VMEM((512, 4096), bf16),
            pltpu.VMEM((528, 4096), f32),
            pltpu.VMEM((528, n), bf16),
            pltpu.SemaphoreType.DMA((len(copies),)),
            pltpu.SemaphoreType.DMA((2,)),
            pltpu.SemaphoreType.DMA((9,)),
        ],
        compiler_params=pltpu.CompilerParams(vmem_limit_bytes=56 * 1024 * 1024),
        cost_estimate=pl.CostEstimate(
            flops=4 * 512 * 4096 * n, transcendentals=0, bytes_accessed=8192 * n + (20 << 20)
        ),
        name=name,
    )(*args)


REL = [(0, 0), (0, -1), (0, 1), (0, 2), (1, 0), (1, -1), (1, 1), (1, 2)]


def on_device(
    query_embeddings,
    passage_embeddings,
    positives,
    logarithm_scale,
    residual_input,
    attention_head_outputs,
    output_weight,
    adapter_down_weight,
    adapter_up_weight,
    final_norm_weight,
    lengths,
):
    group = lax.axis_index("group")
    fsdp = lax.axis_index("fsdp")
    y, x_lo, c = group // 4, (group // 2) % 2, group % 2
    x_hi, z = fsdp // 4, fsdp % 4
    x = x_hi * 2 + x_lo
    half = c * 2048
    other_half = 2048 - half
    logit_scale = jnp.exp(logarithm_scale)
    a_own = attention_head_outputs.reshape(256, 4096)
    res_own = residual_input.reshape(256, 4096)

    extras = jnp.concatenate(
        [
            (positives // 16).astype(bf16)[:, None],
            (positives % 16).astype(bf16)[:, None],
            jnp.broadcast_to(lengths.astype(bf16)[:, None], (4, 1)),
            jnp.zeros((4, 125), bf16),
        ],
        axis=1,
    )
    both = jnp.concatenate([query_embeddings, passage_embeddings], axis=0)
    tags = jnp.concatenate([extras, extras], axis=0)
    mine = jnp.concatenate([pick(both, half, 2048, 1), tags], axis=1)
    theirs = send(
        jnp.concatenate([pick(both, other_half, 2048, 1), tags], axis=1), "core", "s_pair"
    )
    q_chip = ordered(c, mine[:4], theirs[:4])
    p_chip = ordered(c, mine[4:, :2048], theirs[4:, :2048])
    len_par = theirs[0, 2050].astype(f32)

    quarter = y * 256
    s_g = pick(output_weight, half + quarter, 256, 1)
    s_b = pick(output_weight, half + 1024, 1024, 1)
    o_g = send(s_g, "xflip", "w_g_x")
    o_b = send(s_b, "xflip", "w_b_x")

    p_blk = ordered(z % 2, p_chip, send(p_chip, "znear", "p_z0"))
    p_blk = ordered(z // 2, p_blk, send(p_blk, "zflip", "p_z1"))
    p_blk = ordered(y % 2, p_blk, send(p_blk, "ynear", "p_y0"))
    p_blk = ordered(y // 2, p_blk, send(p_blk, "yflip", "p_y1"))
    q_blk = ordered(x % 2, q_chip, send(q_chip, "xnear", "q_x0"))
    q_blk = ordered(x // 2, q_blk, send(q_blk, "xflip", "q_x1"))

    g0 = jnp.concatenate([s_g, o_g], axis=0)
    g_up = send(g0, "zup", "w_g_z0u")
    g_dn = send(g0, "zdown", "w_g_z0d")
    g_far0 = send(g_up[:512], "zup", "w_g_z1u")
    g_far1 = send(g_dn[512:], "zdown", "w_g_z1d")
    y0 = jnp.concatenate([g_up[:512], g_dn[:512], g_far0, o_g, g_up[512:], g_dn[512:], g_far1], 0)
    y_up = send(y0, "yup", "w_g_y0u")
    y_dn = send(y0, "ydown", "w_g_y0d")
    y_far0 = send(y_up[:1792], "yup", "w_g_y1u")
    y_far1 = send(y_dn[1792:], "ydown", "w_g_y1d")
    b0 = jnp.concatenate([s_b, o_b], axis=0)
    b_up = send(b0, "zup", "w_b_z0u")
    b_dn = send(b0, "zdown", "w_b_z0d")
    b_far0 = send(b_up[:512], "zup", "w_b_z1u")
    b_far1 = send(b_dn[512:], "zdown", "w_b_z1d")

    q_feat = q_blk[:, :2048]
    positive = (q_blk[:, 2048].astype(f32) * 16 + q_blk[:, 2049].astype(f32)).astype(jnp.int32)
    row = jnp.arange(128, dtype=jnp.int32)
    row_c, row_z, row_y = (row // 4) % 2, (row // 8) % 4, row // 32
    passage_id = (((row_y * 2 + x_lo) * 2 + row_c) * 8 + x_hi * 4 + row_z) * 4 + row % 4
    partial = lax.dot_general(q_feat, p_blk, NT, preferred_element_type=f32)
    logits = logit_scale * (partial + send(partial, "core", "s_logit"))
    hit = positive[:, None] == passage_id[None, :]
    m = jnp.max(logits, axis=1)
    e = jnp.exp(logits - m[:, None])
    stats = jnp.stack(
        [m, jnp.sum(e, 1), jnp.sum(e * logits, 1), jnp.sum(jnp.where(hit, logits, 0.0), 1)]
    )
    for move, name in (("xnear", "l_x0"), ("xflip", "l_x1")):
        got = send(stats, move, name)
        top = jnp.maximum(stats[0], got[0])
        fa, fb = jnp.exp(stats[0] - top), jnp.exp(got[0] - top)
        stats = jnp.stack(
            [
                top,
                stats[1] * fa + got[1] * fb,
                stats[2] * fa + got[2] * fb,
                stats[3] + got[3],
            ]
        )
    log_norm = stats[0] + jnp.log(stats[1])
    loss_rows = log_norm - stats[3]
    scale_rows = stats[2] / stats[1] - stats[3]
    weight_half = jnp.exp(logits - log_norm[:, None]).astype(bf16)
    hot = hit.astype(bf16)
    q_part = jnp.dot(weight_half, p_blk, preferred_element_type=f32) - jnp.dot(
        hot, p_blk, preferred_element_type=f32
    )
    p_part = lax.dot_general(weight_half, q_feat, TN, preferred_element_type=f32) - lax.dot_general(
        hot, q_feat, TN, preferred_element_type=f32
    )
    xh, xl = x // 2, x % 2
    q_sum = pick(q_part, 16 * xh, 16) + send(pick(q_part, 16 * (1 - xh), 16), "xflip", "r_x0")
    q_sum = pick(q_sum, 8 * xl, 8) + send(pick(q_sum, 8 * (1 - xl), 8), "xnear", "r_x1")
    q_sum = logit_scale * q_sum

    a_par = send(a_own, "core", "s_a")
    r_par = send(pick(res_own, other_half, 2048, 1), "core", "s_r")
    r_own = pick(res_own, half, 2048, 1)
    low = jnp.concatenate(
        [
            jnp.dot(a_own, adapter_down_weight, preferred_element_type=f32),
            jnp.dot(a_par, adapter_down_weight, preferred_element_type=f32),
        ],
        axis=0,
    ).astype(bf16)
    up_half = pick(adapter_up_weight, half, 2048, 1)
    gain = pick(final_norm_weight, half, 2048)
    q_own = pick(q_sum, 4 * c, 1) * gain[None]
    q_par = pick(q_sum, 4 * (1 - c), 1) * gain[None]
    q_f = jnp.concatenate([q_own, q_par, jnp.zeros((6, 2048), f32)], axis=0)
    q_hi = q_f[:2].astype(bf16)
    q_lo = (q_f[:2] - q_hi.astype(f32)).astype(bf16)
    q_rows = jnp.concatenate([q_hi, q_lo, jnp.zeros((12, 2048), bf16)], axis=0)

    shard_ids = [(x_hi ^ du) * 4 + (z + dz) % 4 for du, dz in REL]
    scal = jnp.stack(
        shard_ids + [(y + dy) % 4 for dy in (0, -1, 1, 2)] + [half, half + 1024]
    ).astype(jnp.int32)
    order = [1, 2, 3, 4, 5, 6, 7]
    g_copies = [(0, 0, 12, 512, 0, 0, 0, 1024)]
    for j, shard in enumerate(order):
        for src, quarter_of in ((1, 8), (2, 9), (3, 10)):
            g_copies.append((src, j * 512, None, 512, shard, 0, (quarter_of,), 256))
        if j < 3:
            g_copies.append((4, j * 512, None, 512, shard, 0, (11,), 256))
        elif j == 3:
            g_copies.append((4, 1536, None, 256, shard, 0, (11,), 256))
            g_copies.append((5, 0, None, 256, shard, 256, (11,), 256))
        else:
            g_copies.append((5, j * 512 - 1792, None, 512, shard, 0, (11,), 256))
    b_copies = [
        (0, 0, 13, 512, 0, 0, 0, 1024),
        (1, 0, None, 512, 4, 0, 0, 1024),
        (2, 0, None, 512, 1, 0, 0, 1024),
        (2, 512, None, 512, 5, 0, 0, 1024),
        (3, 0, None, 512, 2, 0, 0, 1024),
        (3, 512, None, 512, 6, 0, 0, 1024),
        (4, 0, None, 512, 3, 0, 0, 1024),
        (5, 0, None, 512, 7, 0, 0, 1024),
    ]
    hid_g, st_g, yacc = block_call(
        g_copies,
        [output_weight, y0, y_up, y_dn, y_far0, y_far1],
        scal,
        a_own,
        a_par,
        jnp.concatenate([r_own[:, :1024], r_par[:, :1024]], axis=0),
        low,
        up_half[:, :1024],
        q_rows[:, :1024],
        q_f[:, :1024],
        None,
        False,
        "block_g",
    )
    hid_b, stats_own, y_own, y_par, y_q = block_call(
        b_copies,
        [output_weight, o_b, b_up, b_dn, b_far0, b_far1],
        scal,
        a_own,
        a_par,
        jnp.concatenate([r_own[:, 1024:], r_par[:, 1024:]], axis=0),
        low,
        up_half[:, 1024:],
        q_rows[:, 1024:],
        q_f[:, 1024:],
        (yacc, st_g),
        True,
        "block_b",
    )

    v_own, v_par = y_q[0:1] + y_q[2:3], y_q[1:2] + y_q[3:4]
    packed = jnp.concatenate([stats_own, v_par.reshape(32, 128)], axis=0)
    got = send(packed, "core", "s_stat")
    y_got = send(y_par, "core", "s_y")
    tok = stats_own[:512] + jnp.concatenate([got[256:512], got[:256]], axis=0)
    qu_own = stats_own[512, :16] + stats_own[514, :16] + got[513, :16] + got[515, :16]
    qu_par = stats_own[513, :16] + stats_own[515, :16] + got[512, :16] + got[514, :16]
    v = v_own + got[528:].reshape(1, 4096)
    position = jnp.arange(256, dtype=jnp.int32).astype(f32)
    len_own = lengths[0].astype(f32)
    w_tok = jnp.concatenate(
        [
            grad_scale * (position < len_own).astype(f32) / len_own,
            grad_scale * (position < len_par).astype(f32) / len_par,
        ]
    )
    inv = lax.rsqrt(tok[:, 16] / 4096 + epsilon)
    lead = inv * w_tok
    back = inv * inv * inv * (w_tok * tok[:, 17] / 4096)
    qu = jnp.concatenate(
        [jnp.broadcast_to(qu_own[None], (256, 16)), jnp.broadcast_to(qu_par[None], (256, 16))], 0
    )
    low_grad = (adapter_scale * (lead[:, None] * qu - back[:, None] * tok[:, :16])).astype(bf16)
    hidden = jnp.concatenate([hid_g, hid_b], axis=1)
    q_tok = jnp.concatenate(
        [jnp.broadcast_to(q_own, (256, 2048)), jnp.broadcast_to(q_par, (256, 2048))], axis=0
    )
    res_grad = (lead[:, None] * q_tok - back[:, None] * hidden).astype(bf16)
    r_got = send(res_grad[256:], "core", "s_rg")
    residual_grad = ordered(c, res_grad[:256], r_got, axis=1)
    attn_grad = (
        lead[:256, None] * v
        - back[:256, None] * (y_own + y_got.astype(f32))
        + lax.dot_general(low_grad[:256], adapter_down_weight, NT, preferred_element_type=f32)
    ).astype(bf16)

    up_part = adapter_scale * lax.dot_general(low, res_grad, TN, preferred_element_type=f32)
    down_part = lax.dot_general(
        low_grad[:256], pick(a_own, half, 2048, 1), TN, preferred_element_type=f32
    ) + lax.dot_general(low_grad[256:], pick(a_par, half, 2048, 1), TN, preferred_element_type=f32)
    my_row = (x * 2 + c) * 4
    sums = jnp.stack([jnp.sum(pick(loss_rows, my_row, 4)), jnp.sum(pick(scale_rows, my_row, 4))])
    tail = jnp.pad(sums[None], ((0, 7), (0, 2046)))
    total = jnp.concatenate([down_part, up_part, tail], axis=0)
    chunk = lambda step: pick(total, ((z + step) % 4) * 512, 512, 1)
    part = (
        chunk(0)
        + send(chunk(1), "zup", "t_z0")
        + send(chunk(-1), "zdown", "t_z1")
        + send(chunk(2), "zfar", "t_z2")
    )
    for move, name in (("ynear", "t_y0"), ("yflip", "t_y1"), ("xnear", "t_x0"), ("xflip", "t_x1")):
        part = part + send(part, move, name)
    from_dn = send(part, "zup", "t_g0")
    from_up = send(part, "zdown", "t_g1")
    from_far = send(part, "zfar", "t_g2")
    total = jnp.zeros((40, 2048), f32)
    for value, step in ((part, 0), (from_dn, -1), (from_up, 1), (from_far, 2)):
        total = lax.dynamic_update_slice(total, value, (0, ((z + step) % 4) * 512))
    mate = send(total, "core", "t_core")
    full = ordered(c, total[:32], mate[:32], axis=1)
    loss = (total[32, 0] + mate[32, 0]) / 512
    scale_grad = (total[32, 1] + mate[32, 1]) / 512
    lora_down = full[:16].T / 128
    lora_up = full[16:] / 128

    p_sum = p_part
    for bit, n, move, name in (
        (y // 2, 64, "yflip", "r_y0"),
        (y % 2, 32, "ynear", "r_y1"),
        (z // 2, 16, "zflip", "r_z0"),
        (z % 2, 8, "znear", "r_z1"),
    ):
        p_sum = pick(p_sum, n * bit, n) + send(pick(p_sum, n * (1 - bit), n), move, name)
    p_sum = logit_scale * p_sum
    keep = jnp.concatenate([pick(q_sum, 4 * c, 4), pick(p_sum, 4 * c, 4)], axis=0)
    give = jnp.concatenate([pick(q_sum, 4 * (1 - c), 4), pick(p_sum, 4 * (1 - c), 4)], axis=0)
    grads = ordered(c, keep, send(give, "core", "s_qp"), axis=1)
    return (
        loss,
        scale_grad,
        grads[:4],
        grads[4:],
        attn_grad[None],
        residual_grad[None],
        lora_down,
        lora_up,
    )


def solution(mesh):
    placed = (
        P(AX, None),
        P(AX, None),
        P(AX),
        P(),
        P(AX, None, None),
        P(AX, None, None),
        P("fsdp", None),
        P(),
        P(),
        P(),
        P(AX),
    )
    return jax.shard_map(
        on_device,
        mesh=mesh,
        in_specs=placed,
        out_specs=(
            P(),
            P(),
            P(AX, None),
            P(AX, None),
            P(AX, None, None),
            P(AX, None, None),
            P(),
            P(),
        ),
        check_vma=False,
    )
```

```python
import functools

import jax
import jax.numpy as jnp
from jax import lax
from jax.experimental import pallas as pl
from jax.experimental.pallas import tpu as pltpu
from jax.sharding import PartitionSpec as P


grad_scale = 512.0
adapter_scale = 2.0
epsilon = 1e-05
AX = ("group", "fsdp")
NT = (((1,), (1,)), ((), ()))
TN = (((0,), (0,)), ((), ()))
f32 = jnp.float32
bf16 = jnp.bfloat16


def coords(i):
    g, f = divmod(i, 8)
    return (f // 4) * 2 + (g // 2) % 2, g // 4, f % 4, g % 2


def device(x, y, z, c):
    x, y, z = x % 4, y % 4, z % 4
    return ((y * 2 + x % 2) * 2 + c) * 8 + (x // 2) * 4 + z


def table(move):
    return [(i, device(*move(*coords(i)))) for i in range(128)]


MOVES = {
    "core": table(lambda x, y, z, c: (x, y, z, 1 - c)),
    "xnear": table(lambda x, y, z, c: (x ^ 1, y, z, c)),
    "xflip": table(lambda x, y, z, c: (3 - x, y, z, c)),
    "ynear": table(lambda x, y, z, c: (x, y ^ 1, z, c)),
    "yflip": table(lambda x, y, z, c: (x, 3 - y, z, c)),
    "znear": table(lambda x, y, z, c: (x, y, z ^ 1, c)),
    "zflip": table(lambda x, y, z, c: (x, y, 3 - z, c)),
    "yup": table(lambda x, y, z, c: (x, y + 1, z, c)),
    "ydown": table(lambda x, y, z, c: (x, y - 1, z, c)),
    "zup": table(lambda x, y, z, c: (x, y, z + 1, c)),
    "zdown": table(lambda x, y, z, c: (x, y, z - 1, c)),
    "zfar": table(lambda x, y, z, c: (x, y, z + 2, c)),
}


def send(value, move):
    return lax.ppermute(value, AX, MOVES[move])


def ordered(bit, mine, other, axis=0):
    return jnp.where(
        bit == 0,
        jnp.concatenate([mine, other], axis=axis),
        jnp.concatenate([other, mine], axis=axis),
    )


def pick(value, start, size, axis=0):
    return lax.dynamic_slice_in_dim(value, start, size, axis=axis)


def block_kernel(copies, scal, *refs):
    n_src = 1 + max(src for src, *_ in copies)
    srcs = refs[:n_src]
    a_own, a_par, r_own, r_par, low, up, q_rows, q_f = refs[n_src : n_src + 8]
    hid_out, st_out, y_own, y_par, y_q = refs[n_src + 8 : n_src + 13]
    w_s, a_s, r_s, hid, hb_s, yo_s, yp_s, w_sem, in_sem, out_sem = refs[n_src + 13 :]
    half = pl.multiple_of(scal[12], 2048)
    inputs = [
        pltpu.make_async_copy(a_own, a_s.at[pl.ds(0, 256), :], in_sem.at[0]),
        pltpu.make_async_copy(a_par, a_s.at[pl.ds(256, 256), :], in_sem.at[1]),
        pltpu.make_async_copy(r_own.at[:, pl.ds(half, 2048)], r_s.at[pl.ds(0, 256), :], in_sem.at[2]),
        pltpu.make_async_copy(r_par, r_s.at[pl.ds(256, 256), :], in_sem.at[3]),
    ]
    for copy in inputs:
        copy.start()
    started = []
    for k, (src, src_row, src_col, rows, shard, dst_row, dst_col, cols) in enumerate(copies):
        ref = srcs[src]
        if src_col is None:
            view = ref.at[pl.ds(src_row, rows), :]
        else:
            view = ref.at[pl.ds(src_row, rows), pl.ds(pl.multiple_of(scal[src_col], 256), cols)]
        first = pl.multiple_of(scal[shard] * 512 + dst_row, 256)
        if isinstance(dst_col, tuple):
            col = pl.multiple_of(scal[dst_col[0]] * 256, 256)
        else:
            col = dst_col
        copy = pltpu.make_async_copy(view, w_s.at[pl.ds(first, rows), pl.ds(col, cols)], w_sem.at[k])
        copy.start()
        started.append((shard, copy))
    for copy in inputs:
        copy.wait()
    hid[...] = r_s[...].astype(f32) + adapter_scale * jnp.dot(
        low[...], up[...], preferred_element_type=f32
    )
    for shard in range(8):
        for owner, copy in started:
            if owner == shard:
                copy.wait()
        first = pl.multiple_of(scal[shard] * 512, 512)
        hid[...] += jnp.dot(
            a_s[:, pl.ds(first, 512)], w_s[pl.ds(first, 512), :], preferred_element_type=f32
        )
    outs = [pltpu.make_async_copy(hid, hid_out, out_sem.at[16])]
    outs[0].start()
    value = hid[...]
    hb_s[pl.ds(0, 512), :] = value.astype(bf16)
    hb_s[pl.ds(512, 16), :] = q_rows[...]
    st_out[...] = jnp.zeros_like(st_out)
    st_out[:, 0:16] = lax.dot_general(hb_s[...], up[...], NT, preferred_element_type=f32)
    st_out[0:512, 16:17] = jnp.sum(value * value, axis=1, keepdims=True)
    st_out[0:256, 17:18] = jnp.sum(value[:256] * q_f[0:1, :], axis=1, keepdims=True)
    st_out[256:512, 17:18] = jnp.sum(value[256:] * q_f[1:2, :], axis=1, keepdims=True)
    for shard in range(8):
        columns = pl.ds(pl.multiple_of(scal[shard] * 512, 512), 512)
        part = lax.dot_general(hb_s[...], w_s[columns, :], NT, preferred_element_type=f32)
        yo_s[:, columns] = part[:256]
        yp_s[:, columns] = part[256:512].astype(bf16)
        y_q[:, columns] = part[512:]
        for k, (src, dst) in enumerate(((yo_s, y_own), (yp_s, y_par))):
            out = pltpu.make_async_copy(
                src.at[:, columns], dst.at[:, columns], out_sem.at[2 * shard + k]
            )
            out.start()
            outs.append(out)
    for out in outs:
        out.wait()


def block_call(copies, srcs, scal, a_own, a_par, r_own, r_par, low, up, q_rows, q_f):
    vm = pl.BlockSpec(memory_space=pltpu.VMEM)
    anyspace = pl.BlockSpec(memory_space=pl.ANY)
    return pl.pallas_call(
        functools.partial(block_kernel, copies),
        out_shape=[
            jax.ShapeDtypeStruct((512, 2048), f32),
            jax.ShapeDtypeStruct((528, 128), f32),
            jax.ShapeDtypeStruct((256, 4096), f32),
            jax.ShapeDtypeStruct((256, 4096), bf16),
            jax.ShapeDtypeStruct((16, 4096), f32),
        ],
        in_specs=[pl.BlockSpec(memory_space=pltpu.SMEM)] + [anyspace] * (len(srcs) + 4) + [vm] * 4,
        out_specs=[anyspace, vm, anyspace, anyspace, vm],
        scratch_shapes=[
            pltpu.VMEM((4096, 2048), bf16),
            pltpu.VMEM((512, 4096), bf16),
            pltpu.VMEM((512, 2048), bf16),
            pltpu.VMEM((512, 2048), f32),
            pltpu.VMEM((528, 2048), bf16),
            pltpu.VMEM((256, 4096), f32),
            pltpu.VMEM((256, 4096), bf16),
            pltpu.SemaphoreType.DMA((len(copies),)),
            pltpu.SemaphoreType.DMA((4,)),
            pltpu.SemaphoreType.DMA((17,)),
        ],
        compiler_params=pltpu.CompilerParams(vmem_limit_bytes=48 * 1024 * 1024),
        cost_estimate=pl.CostEstimate(
            flops=4 * 512 * 4096 * 2048, transcendentals=0, bytes_accessed=32 << 20
        ),
        name="block",
    )(scal, *srcs, a_own, a_par, r_own, r_par, low, up, q_rows, q_f)


REL = [(0, 0), (0, -1), (0, 1), (0, 2), (1, 0), (1, -1), (1, 1), (1, 2)]


def compute(
    query_embeddings,
    passage_embeddings,
    positives,
    logarithm_scale,
    residual_input,
    attention_head_outputs,
    output_weight,
    adapter_down_weight,
    adapter_up_weight,
    final_norm_weight,
    lengths,
):
    group = lax.axis_index("group")
    fsdp = lax.axis_index("fsdp")
    y, x_lo, c = group // 4, (group // 2) % 2, group % 2
    x_hi, z = fsdp // 4, fsdp % 4
    x = x_hi * 2 + x_lo
    half = c * 2048
    other_half = 2048 - half
    logit_scale = jnp.exp(logarithm_scale)
    a_own = attention_head_outputs.reshape(256, 4096)
    res_own = residual_input.reshape(256, 4096)

    extras = jnp.concatenate(
        [
            (positives // 16).astype(bf16)[:, None],
            (positives % 16).astype(bf16)[:, None],
            jnp.broadcast_to(lengths.astype(bf16)[:, None], (4, 1)),
            jnp.zeros((4, 125), bf16),
        ],
        axis=1,
    )
    both = jnp.concatenate([query_embeddings, passage_embeddings], axis=0)
    tags = jnp.concatenate([extras, extras], axis=0)
    mine = jnp.concatenate([pick(both, half, 2048, 1), tags], axis=1)
    theirs = send(jnp.concatenate([pick(both, other_half, 2048, 1), tags], axis=1), "core")
    q_chip = ordered(c, mine[:4], theirs[:4])
    p_chip = ordered(c, mine[4:, :2048], theirs[4:, :2048])
    len_par = theirs[0, 2050].astype(f32)

    s_g = pick(output_weight, half + y * 256, 256, 1)
    s_a = pick(output_weight, half + 1024, 512, 1)
    s_b = pick(output_weight, half + 1536, 512, 1)
    o_g = send(s_g, "xflip")
    o_b = send(s_b, "xflip")
    o_a = send(s_a, "xflip")

    p_blk = ordered(z % 2, p_chip, send(p_chip, "znear"))
    p_blk = ordered(z // 2, p_blk, send(p_blk, "zflip"))
    p_blk = ordered(y % 2, p_blk, send(p_blk, "ynear"))
    p_blk = ordered(y // 2, p_blk, send(p_blk, "yflip"))
    q_blk = ordered(x % 2, q_chip, send(q_chip, "xnear"))
    q_blk = ordered(x // 2, q_blk, send(q_blk, "xflip"))

    g0 = jnp.concatenate([s_g, o_g], axis=0)
    g_up = send(g0, "zup")
    g_dn = send(g0, "zdown")
    g_far0 = send(g_up[:512], "zup")
    g_far1 = send(g_dn[512:], "zdown")
    yb = jnp.concatenate([g_up, g_dn], axis=0)
    yc = jnp.concatenate([g_far0, g_far1], axis=0)
    ya_u, ya_d = send(o_g, "yup"), send(o_g, "ydown")
    yb_u, yb_d = send(yb, "yup"), send(yb, "ydown")
    yc_u, yc_d = send(yc, "yup"), send(yc, "ydown")
    y1b_u = send(yb_u[:1024], "yup")
    y1b_d = send(yb_d[1024:], "ydown")
    y1c_u = send(jnp.concatenate([ya_u, yc_u[:256]], axis=0), "yup")
    y1c_d = send(yc_d[256:], "ydown")
    a_up = send(s_a, "zup")
    a_dn = send(s_a, "zdown")
    a_far_u = send(a_up[:256], "zup")
    a_far_d = send(a_dn[256:], "zdown")
    a_x1 = send(jnp.concatenate([a_up, a_dn], axis=0), "xflip")
    a_x2 = send(jnp.concatenate([a_far_u, a_far_d], axis=0), "xflip")
    b0 = jnp.concatenate([s_b, o_b], axis=0)
    b_up = send(b0, "zup")
    b_dn = send(b0, "zdown")
    b_far0 = send(b_up[:512], "zup")
    b_far1 = send(b_dn[512:], "zdown")

    q_feat = q_blk[:, :2048]
    positive = (q_blk[:, 2048].astype(f32) * 16 + q_blk[:, 2049].astype(f32)).astype(jnp.int32)
    row = jnp.arange(128, dtype=jnp.int32)
    row_c, row_z, row_y = (row // 4) % 2, (row // 8) % 4, row // 32
    passage_id = (((row_y * 2 + x_lo) * 2 + row_c) * 8 + x_hi * 4 + row_z) * 4 + row % 4
    partial = lax.dot_general(q_feat, p_blk, NT, preferred_element_type=f32)
    logits = logit_scale * (partial + send(partial, "core"))
    hit = positive[:, None] == passage_id[None, :]
    m = jnp.max(logits, axis=1)
    e = jnp.exp(logits - m[:, None])
    stats = jnp.stack(
        [m, jnp.sum(e, 1), jnp.sum(e * logits, 1), jnp.sum(jnp.where(hit, logits, 0.0), 1)]
    )
    for move in ("xnear", "xflip"):
        got = send(stats, move)
        top = jnp.maximum(stats[0], got[0])
        fa, fb = jnp.exp(stats[0] - top), jnp.exp(got[0] - top)
        stats = jnp.stack(
            [
                top,
                stats[1] * fa + got[1] * fb,
                stats[2] * fa + got[2] * fb,
                stats[3] + got[3],
            ]
        )
    log_norm = stats[0] + jnp.log(stats[1])
    loss_rows = log_norm - stats[3]
    scale_rows = stats[2] / stats[1] - stats[3]
    weight_half = jnp.exp(logits - log_norm[:, None]).astype(bf16)
    hot = hit.astype(bf16)
    q_part = jnp.dot(weight_half, p_blk, preferred_element_type=f32) - jnp.dot(
        hot, p_blk, preferred_element_type=f32
    )
    p_part = lax.dot_general(weight_half, q_feat, TN, preferred_element_type=f32) - lax.dot_general(
        hot, q_feat, TN, preferred_element_type=f32
    )
    xh, xl = x // 2, x % 2
    q_sum = pick(q_part, 16 * xh, 16) + send(pick(q_part, 16 * (1 - xh), 16), "xflip")
    q_sum = pick(q_sum, 8 * xl, 8) + send(pick(q_sum, 8 * (1 - xl), 8), "xnear")
    q_sum = logit_scale * q_sum

    a_par = send(a_own, "core")
    r_par = send(pick(res_own, other_half, 2048, 1), "core")
    low = jnp.concatenate(
        [
            jnp.dot(a_own, adapter_down_weight, preferred_element_type=f32),
            jnp.dot(a_par, adapter_down_weight, preferred_element_type=f32),
        ],
        axis=0,
    ).astype(bf16)
    up_half = pick(adapter_up_weight, half, 2048, 1)
    gain = pick(final_norm_weight, half, 2048)
    q_own = pick(q_sum, 4 * c, 1) * gain[None]
    q_par = pick(q_sum, 4 * (1 - c), 1) * gain[None]
    q_f = jnp.concatenate([q_own, q_par, jnp.zeros((6, 2048), f32)], axis=0)
    q_hi = q_f[:2].astype(bf16)
    q_lo = (q_f[:2] - q_hi.astype(f32)).astype(bf16)
    q_rows = jnp.concatenate([q_hi, q_lo, jnp.zeros((12, 2048), bf16)], axis=0)

    shard_ids = [(x_hi ^ du) * 4 + (z + dz) % 4 for du, dz in REL]
    scal = jnp.stack(shard_ids + [(y + dy) % 4 for dy in (0, -1, 1, 2)] + [half]).astype(jnp.int32)
    srcs, copies = [output_weight], [(0, 0, 12, 512, 0, 0, 0, 2048)]

    def land(value, shards, dst_col, cols):
        srcs.append(value)
        at = 0
        for shard, dst_row, rows in shards:
            copies.append((len(srcs) - 1, at, None, rows, shard, dst_row, dst_col, cols))
            at += rows

    for k, (va, vb, vc) in enumerate(((o_g, yb, yc), (ya_u, yb_u, yc_u), (ya_d, yb_d, yc_d))):
        land(va, [(4, 0, 512)], (8 + k,), 256)
        land(vb, [(1, 0, 512), (5, 0, 512), (2, 0, 512), (6, 0, 512)], (8 + k,), 256)
        land(vc, [(3, 0, 512), (7, 0, 512)], (8 + k,), 256)
    land(y1b_u, [(1, 0, 512), (5, 0, 512)], (11,), 256)
    land(y1b_d, [(2, 0, 512), (6, 0, 512)], (11,), 256)
    land(y1c_u, [(4, 0, 512), (3, 0, 256)], (11,), 256)
    land(y1c_d, [(3, 256, 256), (7, 0, 512)], (11,), 256)
    land(o_a, [(4, 0, 512)], 1024, 512)
    land(a_up, [(1, 0, 512)], 1024, 512)
    land(a_dn, [(2, 0, 512)], 1024, 512)
    land(a_far_u, [(3, 0, 256)], 1024, 512)
    land(a_far_d, [(3, 256, 256)], 1024, 512)
    land(a_x1, [(5, 0, 512), (6, 0, 512)], 1024, 512)
    land(a_x2, [(7, 0, 512)], 1024, 512)
    land(o_b, [(4, 0, 512)], 1536, 512)
    land(b_up, [(1, 0, 512), (5, 0, 512)], 1536, 512)
    land(b_dn, [(2, 0, 512), (6, 0, 512)], 1536, 512)
    land(b_far0, [(3, 0, 512)], 1536, 512)
    land(b_far1, [(7, 0, 512)], 1536, 512)
    hidden, stats_own, y_own, y_par, y_q = block_call(
        copies, srcs, scal, a_own, a_par, res_own, r_par, low, up_half, q_rows, q_f
    )

    v_own, v_par = y_q[0:1] + y_q[2:3], y_q[1:2] + y_q[3:4]
    packed = jnp.concatenate([stats_own, v_par.reshape(32, 128)], axis=0)
    got = send(packed, "core")
    y_got = send(y_par, "core")
    tok = stats_own[:512] + jnp.concatenate([got[256:512], got[:256]], axis=0)
    qu_own = stats_own[512, :16] + stats_own[514, :16] + got[513, :16] + got[515, :16]
    qu_par = stats_own[513, :16] + stats_own[515, :16] + got[512, :16] + got[514, :16]
    v = v_own + got[528:].reshape(1, 4096)
    position = jnp.arange(256, dtype=jnp.int32).astype(f32)
    len_own = lengths[0].astype(f32)
    w_tok = jnp.concatenate(
        [
            grad_scale * (position < len_own).astype(f32) / len_own,
            grad_scale * (position < len_par).astype(f32) / len_par,
        ]
    )
    inv = lax.rsqrt(tok[:, 16] / 4096 + epsilon)
    lead = inv * w_tok
    back = inv * inv * inv * (w_tok * tok[:, 17] / 4096)
    qu = jnp.concatenate(
        [jnp.broadcast_to(qu_own[None], (256, 16)), jnp.broadcast_to(qu_par[None], (256, 16))], 0
    )
    low_grad = (adapter_scale * (lead[:, None] * qu - back[:, None] * tok[:, :16])).astype(bf16)
    q_tok = jnp.concatenate(
        [jnp.broadcast_to(q_own, (256, 2048)), jnp.broadcast_to(q_par, (256, 2048))], axis=0
    )
    res_grad = (lead[:, None] * q_tok - back[:, None] * hidden).astype(bf16)
    r_got = send(res_grad[256:], "core")
    residual_grad = ordered(c, res_grad[:256], r_got, axis=1)
    attn_grad = (
        lead[:256, None] * v
        - back[:256, None] * (y_own + y_got.astype(f32))
        + lax.dot_general(low_grad[:256], adapter_down_weight, NT, preferred_element_type=f32)
    ).astype(bf16)

    up_part = adapter_scale * lax.dot_general(low, res_grad, TN, preferred_element_type=f32)
    down_part = lax.dot_general(
        low_grad[:256], pick(a_own, half, 2048, 1), TN, preferred_element_type=f32
    ) + lax.dot_general(low_grad[256:], pick(a_par, half, 2048, 1), TN, preferred_element_type=f32)
    my_row = (x * 2 + c) * 4
    sums = jnp.stack([jnp.sum(pick(loss_rows, my_row, 4)), jnp.sum(pick(scale_rows, my_row, 4))])
    tail = jnp.pad(sums[None], ((0, 7), (0, 2046)))
    total = jnp.concatenate([down_part, up_part, tail], axis=0)
    sides = [[i for i in range(128) if coords(i)[3] == side] for side in range(2)]
    swap = lambda value: lax.all_to_all(
        value, AX, 0, 0, axis_index_groups=sides, tiled=True
    )
    part = jnp.sum(swap(total.reshape(64, 1280)), axis=0, keepdims=True)
    total = swap(jnp.broadcast_to(part, (64, 1280))).reshape(40, 2048)
    mate = send(total, "core")
    full = ordered(c, total[:32], mate[:32], axis=1)
    loss = (total[32, 0] + mate[32, 0]) / 512
    scale_grad = (total[32, 1] + mate[32, 1]) / 512
    lora_down = full[:16].T / 128
    lora_up = full[16:] / 128

    p_sum = p_part
    for bit, n, move in (
        (y // 2, 64, "yflip"), (y % 2, 32, "ynear"), (z // 2, 16, "zflip"), (z % 2, 8, "znear")
    ):
        p_sum = pick(p_sum, n * bit, n) + send(pick(p_sum, n * (1 - bit), n), move)
    p_sum = logit_scale * p_sum
    keep = jnp.concatenate([pick(q_sum, 4 * c, 4), pick(p_sum, 4 * c, 4)], axis=0)
    give = jnp.concatenate([pick(q_sum, 4 * (1 - c), 4), pick(p_sum, 4 * (1 - c), 4)], axis=0)
    grads = ordered(c, keep, send(give, "core"), axis=1)
    return (
        loss,
        scale_grad,
        grads[:4],
        grads[4:],
        attn_grad[None],
        residual_grad[None],
        lora_down,
        lora_up,
    )


def solution(mesh):
    placed = (
        P(AX, None),
        P(AX, None),
        P(AX),
        P(),
        P(AX, None, None),
        P(AX, None, None),
        P("fsdp", None),
        P(),
        P(),
        P(),
        P(AX),
    )
    return jax.shard_map(
        compute,
        mesh=mesh,
        in_specs=placed,
        out_specs=(
            P(),
            P(),
            P(AX, None),
            P(AX, None),
            P(AX, None, None),
            P(AX, None, None),
            P(),
            P(),
        ),
        check_vma=False,
    )
```

```python
import functools

import jax
import jax.numpy as jnp
from jax import lax
from jax.experimental import pallas as pl
from jax.experimental.pallas import tpu as pltpu
from jax.sharding import PartitionSpec as P


grad_scale = 512.0
adapter_scale = 2.0
epsilon = 1e-05
AX = ("group", "fsdp")
NT = (((1,), (1,)), ((), ()))
TN = (((0,), (0,)), ((), ()))
f32 = jnp.float32
bf16 = jnp.bfloat16


def coords(i):
    g, f = divmod(i, 8)
    return (f // 4) * 2 + (g // 2) % 2, g // 4, f % 4, g % 2


def device(x, y, z, c):
    x, y, z = x % 4, y % 4, z % 4
    return ((y * 2 + x % 2) * 2 + c) * 8 + (x // 2) * 4 + z


def table(move):
    return [(i, device(*move(*coords(i)))) for i in range(128)]


MOVES = {
    "core": table(lambda x, y, z, c: (x, y, z, 1 - c)),
    "xnear": table(lambda x, y, z, c: (x ^ 1, y, z, c)),
    "xflip": table(lambda x, y, z, c: (3 - x, y, z, c)),
    "ynear": table(lambda x, y, z, c: (x, y ^ 1, z, c)),
    "yflip": table(lambda x, y, z, c: (x, 3 - y, z, c)),
    "znear": table(lambda x, y, z, c: (x, y, z ^ 1, c)),
    "zflip": table(lambda x, y, z, c: (x, y, 3 - z, c)),
    "yup": table(lambda x, y, z, c: (x, y + 1, z, c)),
    "ydown": table(lambda x, y, z, c: (x, y - 1, z, c)),
    "zup": table(lambda x, y, z, c: (x, y, z + 1, c)),
    "zdown": table(lambda x, y, z, c: (x, y, z - 1, c)),
    "zfar": table(lambda x, y, z, c: (x, y, z + 2, c)),
}


def send(value, move):
    return lax.ppermute(value, AX, MOVES[move])


def ordered(bit, mine, other, axis=0):
    return jnp.where(
        bit == 0,
        jnp.concatenate([mine, other], axis=axis),
        jnp.concatenate([other, mine], axis=axis),
    )


def pick(value, start, size, axis=0):
    return lax.dynamic_slice_in_dim(value, start, size, axis=axis)


def block_kernel(copies, scal, *refs):
    n_src = 1 + max(src for src, *_ in copies)
    srcs = refs[:n_src]
    a_own, a_par, r_own, r_par, low, up, q_rows, q_f = refs[n_src : n_src + 8]
    hid_out, st_out, y_own, y_par, y_q = refs[n_src + 8 : n_src + 13]
    w_s, a_s, r_s, hid, hb_s, yo_s, yp_s, w_sem, in_sem, out_sem = refs[n_src + 13 :]
    half = pl.multiple_of(scal[12], 2048)
    inputs = [
        pltpu.make_async_copy(a_own, a_s.at[pl.ds(0, 256), :], in_sem.at[0]),
        pltpu.make_async_copy(a_par, a_s.at[pl.ds(256, 256), :], in_sem.at[1]),
        pltpu.make_async_copy(r_own.at[:, pl.ds(half, 2048)], r_s.at[pl.ds(0, 256), :], in_sem.at[2]),
        pltpu.make_async_copy(r_par, r_s.at[pl.ds(256, 256), :], in_sem.at[3]),
    ]
    for copy in inputs:
        copy.start()
    for src, src_row, src_col, rows, shard, dst_row, dst_col, cols in copies:
        ref = srcs[src]
        if src_col is None:
            view = ref.at[pl.ds(src_row, rows), :]
        else:
            view = ref.at[pl.ds(src_row, rows), pl.ds(pl.multiple_of(scal[src_col], 256), cols)]
        first = pl.multiple_of(scal[shard] * 512 + dst_row, 256)
        if isinstance(dst_col, tuple):
            col = pl.multiple_of(scal[dst_col[0]] * 256, 256)
        else:
            col = dst_col
        pltpu.make_async_copy(
            view, w_s.at[pl.ds(first, rows), pl.ds(col, cols)], w_sem.at[shard]
        ).start()
    for copy in inputs:
        copy.wait()
    hid[...] = r_s[...].astype(f32) + adapter_scale * jnp.dot(
        low[...], up[...], preferred_element_type=f32
    )

    def forward(shard, carry):
        rows = pl.ds(pl.multiple_of(scal[shard] * 512, 512), 512)
        pltpu.make_async_copy(w_s.at[rows, :], w_s.at[rows, :], w_sem.at[shard]).wait()
        hid[...] += jnp.dot(a_s[:, rows], w_s[rows, :], preferred_element_type=f32)
        return carry

    lax.fori_loop(0, 8, forward, 0)
    hid_copy = pltpu.make_async_copy(hid, hid_out, out_sem.at[2])
    hid_copy.start()
    value = hid[...]
    hb_s[pl.ds(0, 512), :] = value.astype(bf16)
    hb_s[pl.ds(512, 16), :] = q_rows[...]
    st_out[...] = jnp.zeros_like(st_out)
    st_out[:, 0:16] = lax.dot_general(hb_s[...], up[...], NT, preferred_element_type=f32)
    st_out[0:512, 16:17] = jnp.sum(value * value, axis=1, keepdims=True)
    st_out[0:256, 17:18] = jnp.sum(value[:256] * q_f[0:1, :], axis=1, keepdims=True)
    st_out[256:512, 17:18] = jnp.sum(value[256:] * q_f[1:2, :], axis=1, keepdims=True)

    def backward(shard, carry):
        columns = pl.ds(pl.multiple_of(scal[shard] * 512, 512), 512)
        part = lax.dot_general(hb_s[...], w_s[columns, :], NT, preferred_element_type=f32)
        yo_s[:, columns] = part[:256]
        yp_s[:, columns] = part[256:512].astype(bf16)
        y_q[:, columns] = part[512:]
        pltpu.make_async_copy(yo_s.at[:, columns], y_own.at[:, columns], out_sem.at[0]).start()
        pltpu.make_async_copy(yp_s.at[:, columns], y_par.at[:, columns], out_sem.at[1]).start()
        return carry

    lax.fori_loop(0, 8, backward, 0)
    pltpu.make_async_copy(yo_s, y_own, out_sem.at[0]).wait()
    pltpu.make_async_copy(yp_s, y_par, out_sem.at[1]).wait()
    hid_copy.wait()


def block_call(copies, srcs, scal, a_own, a_par, r_own, r_par, low, up, q_rows, q_f):
    vm = pl.BlockSpec(memory_space=pltpu.VMEM)
    anyspace = pl.BlockSpec(memory_space=pl.ANY)
    return pl.pallas_call(
        functools.partial(block_kernel, copies),
        out_shape=[
            jax.ShapeDtypeStruct((512, 2048), f32),
            jax.ShapeDtypeStruct((528, 128), f32),
            jax.ShapeDtypeStruct((256, 4096), f32),
            jax.ShapeDtypeStruct((256, 4096), bf16),
            jax.ShapeDtypeStruct((16, 4096), f32),
        ],
        in_specs=[pl.BlockSpec(memory_space=pltpu.SMEM)] + [anyspace] * (len(srcs) + 4) + [vm] * 4,
        out_specs=[anyspace, vm, anyspace, anyspace, vm],
        scratch_shapes=[
            pltpu.VMEM((4096, 2048), bf16),
            pltpu.VMEM((512, 4096), bf16),
            pltpu.VMEM((512, 2048), bf16),
            pltpu.VMEM((512, 2048), f32),
            pltpu.VMEM((528, 2048), bf16),
            pltpu.VMEM((256, 4096), f32),
            pltpu.VMEM((256, 4096), bf16),
            pltpu.SemaphoreType.DMA((8,)),
            pltpu.SemaphoreType.DMA((4,)),
            pltpu.SemaphoreType.DMA((3,)),
        ],
        compiler_params=pltpu.CompilerParams(vmem_limit_bytes=48 * 1024 * 1024),
        cost_estimate=pl.CostEstimate(
            flops=4 * 512 * 4096 * 2048, transcendentals=0, bytes_accessed=32 << 20
        ),
        name="block",
    )(scal, *srcs, a_own, a_par, r_own, r_par, low, up, q_rows, q_f)


REL = [(0, 0), (0, -1), (0, 1), (0, 2), (1, 0), (1, -1), (1, 1), (1, 2)]


def compute(
    query_embeddings,
    passage_embeddings,
    positives,
    logarithm_scale,
    residual_input,
    attention_head_outputs,
    output_weight,
    adapter_down_weight,
    adapter_up_weight,
    final_norm_weight,
    lengths,
):
    group = lax.axis_index("group")
    fsdp = lax.axis_index("fsdp")
    y, x_lo, c = group // 4, (group // 2) % 2, group % 2
    x_hi, z = fsdp // 4, fsdp % 4
    x = x_hi * 2 + x_lo
    half = c * 2048
    other_half = 2048 - half
    logit_scale = jnp.exp(logarithm_scale)
    a_own = attention_head_outputs.reshape(256, 4096)
    res_own = residual_input.reshape(256, 4096)

    extras = jnp.concatenate(
        [
            (positives // 16).astype(bf16)[:, None],
            (positives % 16).astype(bf16)[:, None],
            jnp.broadcast_to(lengths.astype(bf16)[:, None], (4, 1)),
            jnp.zeros((4, 125), bf16),
        ],
        axis=1,
    )
    both = jnp.concatenate([query_embeddings, passage_embeddings], axis=0)
    tags = jnp.concatenate([extras, extras], axis=0)
    mine = jnp.concatenate([pick(both, half, 2048, 1), tags], axis=1)
    theirs = send(jnp.concatenate([pick(both, other_half, 2048, 1), tags], axis=1), "core")
    q_chip = ordered(c, mine[:4], theirs[:4])
    p_chip = ordered(c, mine[4:, :2048], theirs[4:, :2048])
    len_par = theirs[0, 2050].astype(f32)

    s_g = pick(output_weight, half + y * 256, 256, 1)
    s_ab = pick(output_weight, half + 1024, 1024, 1)
    o_g = send(s_g, "xflip")
    o_ab = send(s_ab, "xflip")

    p_blk = ordered(z % 2, p_chip, send(p_chip, "znear"))
    p_blk = ordered(z // 2, p_blk, send(p_blk, "zflip"))
    p_blk = ordered(y % 2, p_blk, send(p_blk, "ynear"))
    p_blk = ordered(y // 2, p_blk, send(p_blk, "yflip"))
    q_blk = ordered(x % 2, q_chip, send(q_chip, "xnear"))
    q_blk = ordered(x // 2, q_blk, send(q_blk, "xflip"))

    ga = jnp.concatenate([s_g, o_g, s_ab[:, :256]], axis=0)
    up0 = send(ga, "zup")
    dn0 = send(ga, "zdown")
    up1 = send(jnp.concatenate([up0[:512], up0[1024:1280]], axis=0), "zup")
    dn1 = send(jnp.concatenate([dn0[512:1024], dn0[1280:]], axis=0), "zdown")
    y0 = jnp.concatenate([o_g, up0[:1024], dn0[:1024], up1[:512], dn1[:512]], axis=0)
    y_up = send(y0, "yup")
    y_dn = send(y0, "ydown")
    y_far0 = send(y_up[:1792], "yup")
    y_far1 = send(y_dn[1792:], "ydown")
    a_x = send(jnp.concatenate([up0[1024:], dn0[1024:], up1[512:], dn1[512:]], axis=0), "xflip")
    b0 = jnp.concatenate([s_ab[:, 256:], o_ab[:, 256:]], axis=0)
    b_up = send(b0, "zup")
    b_dn = send(b0, "zdown")
    b_far0 = send(b_up[:512], "zup")
    b_far1 = send(b_dn[512:], "zdown")

    q_feat = q_blk[:, :2048]
    positive = (q_blk[:, 2048].astype(f32) * 16 + q_blk[:, 2049].astype(f32)).astype(jnp.int32)
    row = jnp.arange(128, dtype=jnp.int32)
    row_c, row_z, row_y = (row // 4) % 2, (row // 8) % 4, row // 32
    passage_id = (((row_y * 2 + x_lo) * 2 + row_c) * 8 + x_hi * 4 + row_z) * 4 + row % 4
    partial = lax.dot_general(q_feat, p_blk, NT, preferred_element_type=f32)
    logits = logit_scale * (partial + send(partial, "core"))
    hit = positive[:, None] == passage_id[None, :]
    m = jnp.max(logits, axis=1)
    e = jnp.exp(logits - m[:, None])
    stats = jnp.stack(
        [m, jnp.sum(e, 1), jnp.sum(e * logits, 1), jnp.sum(jnp.where(hit, logits, 0.0), 1)]
    )
    for move in ("xnear", "xflip"):
        got = send(stats, move)
        top = jnp.maximum(stats[0], got[0])
        fa, fb = jnp.exp(stats[0] - top), jnp.exp(got[0] - top)
        stats = jnp.stack(
            [
                top,
                stats[1] * fa + got[1] * fb,
                stats[2] * fa + got[2] * fb,
                stats[3] + got[3],
            ]
        )
    log_norm = stats[0] + jnp.log(stats[1])
    loss_rows = log_norm - stats[3]
    scale_rows = stats[2] / stats[1] - stats[3]
    weight_half = jnp.exp(logits - log_norm[:, None]).astype(bf16)
    hot = hit.astype(bf16)
    q_part = jnp.dot(weight_half, p_blk, preferred_element_type=f32) - jnp.dot(
        hot, p_blk, preferred_element_type=f32
    )
    p_part = lax.dot_general(weight_half, q_feat, TN, preferred_element_type=f32) - lax.dot_general(
        hot, q_feat, TN, preferred_element_type=f32
    )
    xh, xl = x // 2, x % 2
    q_sum = pick(q_part, 16 * xh, 16) + send(pick(q_part, 16 * (1 - xh), 16), "xflip")
    q_sum = pick(q_sum, 8 * xl, 8) + send(pick(q_sum, 8 * (1 - xl), 8), "xnear")
    q_sum = logit_scale * q_sum

    a_own, res_own, _ = lax.optimization_barrier((a_own, res_own, q_sum))
    a_par = send(a_own, "core")
    r_par = send(pick(res_own, other_half, 2048, 1), "core")
    low = jnp.concatenate(
        [
            jnp.dot(a_own, adapter_down_weight, preferred_element_type=f32),
            jnp.dot(a_par, adapter_down_weight, preferred_element_type=f32),
        ],
        axis=0,
    ).astype(bf16)
    up_half = pick(adapter_up_weight, half, 2048, 1)
    gain = pick(final_norm_weight, half, 2048)
    q_own = pick(q_sum, 4 * c, 1) * gain[None]
    q_par = pick(q_sum, 4 * (1 - c), 1) * gain[None]
    q_f = jnp.concatenate([q_own, q_par, jnp.zeros((6, 2048), f32)], axis=0)
    q_hi = q_f[:2].astype(bf16)
    q_lo = (q_f[:2] - q_hi.astype(f32)).astype(bf16)
    q_rows = jnp.concatenate([q_hi, q_lo, jnp.zeros((12, 2048), bf16)], axis=0)

    shard_ids = [(x_hi ^ du) * 4 + (z + dz) % 4 for du, dz in REL]
    scal = jnp.stack(shard_ids + [(y + dy) % 4 for dy in (0, -1, 1, 2)] + [half]).astype(jnp.int32)
    srcs, copies = [output_weight], [(0, 0, 12, 512, 0, 0, 0, 2048)]

    def land(value, shards, dst_col, cols, at=0):
        if not any(value is known for known in srcs):
            srcs.append(value)
        index = [value is known for known in srcs].index(True)
        for shard, dst_row, rows in shards:
            copies.append((index, at, None, rows, shard, dst_row, dst_col, cols))
            at += rows

    whole = lambda shard: (shard, 0, 512)
    seven = [whole(shard) for shard in (4, 1, 5, 2, 6, 3, 7)]
    land(y0, seven, (8,), 256)
    land(y_up, seven, (9,), 256)
    land(y_dn, seven, (10,), 256)
    land(y_far0, seven[:3] + [(2, 0, 256)], (11,), 256)
    land(y_far1, [(2, 256, 256)] + seven[4:], (11,), 256)
    land(o_ab, [whole(4)], 1024, 1024)
    land(up0, [whole(1)], 1024, 256, 1024)
    land(dn0, [whole(2)], 1024, 256, 1024)
    land(up1, [(3, 0, 256)], 1024, 256, 512)
    land(dn1, [(3, 256, 256)], 1024, 256, 512)
    land(a_x, [whole(5), whole(6), whole(7)], 1024, 256)
    land(b_up, [whole(1), whole(5)], 1280, 768)
    land(b_dn, [whole(2), whole(6)], 1280, 768)
    land(b_far0, [whole(3)], 1280, 768)
    land(b_far1, [whole(7)], 1280, 768)
    hidden, stats_own, y_own, y_par, y_q = block_call(
        copies, srcs, scal, a_own, a_par, res_own, r_par, low, up_half, q_rows, q_f
    )

    v_own, v_par = y_q[0:1] + y_q[2:3], y_q[1:2] + y_q[3:4]
    packed = jnp.concatenate([stats_own, v_par.reshape(32, 128)], axis=0)
    got = send(packed, "core")
    y_got = send(y_par, "core")
    tok = stats_own[:512] + jnp.concatenate([got[256:512], got[:256]], axis=0)
    qu_own = stats_own[512, :16] + stats_own[514, :16] + got[513, :16] + got[515, :16]
    qu_par = stats_own[513, :16] + stats_own[515, :16] + got[512, :16] + got[514, :16]
    v = v_own + got[528:].reshape(1, 4096)
    position = jnp.arange(256, dtype=jnp.int32).astype(f32)
    len_own = lengths[0].astype(f32)
    w_tok = jnp.concatenate(
        [
            grad_scale * (position < len_own).astype(f32) / len_own,
            grad_scale * (position < len_par).astype(f32) / len_par,
        ]
    )
    inv = lax.rsqrt(tok[:, 16] / 4096 + epsilon)
    lead = inv * w_tok
    back = inv * inv * inv * (w_tok * tok[:, 17] / 4096)
    qu = jnp.concatenate(
        [jnp.broadcast_to(qu_own[None], (256, 16)), jnp.broadcast_to(qu_par[None], (256, 16))], 0
    )
    low_grad = (adapter_scale * (lead[:, None] * qu - back[:, None] * tok[:, :16])).astype(bf16)
    q_tok = jnp.concatenate(
        [jnp.broadcast_to(q_own, (256, 2048)), jnp.broadcast_to(q_par, (256, 2048))], axis=0
    )
    res_grad = (lead[:, None] * q_tok - back[:, None] * hidden).astype(bf16)
    r_got = send(res_grad[256:], "core")
    residual_grad = ordered(c, res_grad[:256], r_got, axis=1)
    attn_grad = (
        lead[:256, None] * v
        - back[:256, None] * (y_own + y_got.astype(f32))
        + lax.dot_general(low_grad[:256], adapter_down_weight, NT, preferred_element_type=f32)
    ).astype(bf16)

    up_part = adapter_scale * lax.dot_general(low, res_grad, TN, preferred_element_type=f32)
    down_part = lax.dot_general(
        low_grad[:256], pick(a_own, half, 2048, 1), TN, preferred_element_type=f32
    ) + lax.dot_general(low_grad[256:], pick(a_par, half, 2048, 1), TN, preferred_element_type=f32)
    my_row = (x * 2 + c) * 4
    sums = jnp.stack([jnp.sum(pick(loss_rows, my_row, 4)), jnp.sum(pick(scale_rows, my_row, 4))])
    tail = jnp.pad(sums[None], ((0, 7), (0, 2046)))
    total = jnp.concatenate([down_part / 128, up_part / 128, tail], axis=0)
    sides = [[i for i in range(128) if coords(i)[3] == side] for side in range(2)]
    swap = lambda value: lax.all_to_all(
        value, AX, 0, 0, axis_index_groups=sides, tiled=True
    )
    part = jnp.sum(swap(total.reshape(64, 1280)), axis=0, keepdims=True)
    total = swap(jnp.broadcast_to(part, (64, 1280))).reshape(40, 2048)
    mate = send(total, "core")
    loss = (total[32, 0] + mate[32, 0]) / 512
    scale_grad = (total[32, 1] + mate[32, 1]) / 512
    lora_down = ordered(c, total[:16], mate[:16], axis=1).T
    lora_up = ordered(c, total[16:32], mate[16:32], axis=1)

    p_sum = p_part
    for bit, n, move, name in (
        (y // 2, 64, "yflip", "r_y0"),
        (y % 2, 32, "ynear", "r_y1"),
        (z // 2, 16, "zflip", "r_z0"),
        (z % 2, 8, "znear", "r_z1"),
    ):
        got = send(pick(p_sum, n * (1 - bit), n), move)
        if name == "r_y0":
            got, p_sum, _ = lax.optimization_barrier((got, p_sum, stats_own))
        p_sum = pick(p_sum, n * bit, n) + got
    p_sum = logit_scale * p_sum
    keep = jnp.concatenate([pick(q_sum, 4 * c, 4), pick(p_sum, 4 * c, 4)], axis=0)
    give = jnp.concatenate([pick(q_sum, 4 * (1 - c), 4), pick(p_sum, 4 * (1 - c), 4)], axis=0)
    grads = ordered(c, keep, send(give, "core"), axis=1)
    return (
        loss,
        scale_grad,
        grads[:4],
        grads[4:],
        attn_grad[None],
        residual_grad[None],
        lora_down,
        lora_up,
    )


def solution(mesh):
    placed = (
        P(AX, None),
        P(AX, None),
        P(AX),
        P(),
        P(AX, None, None),
        P(AX, None, None),
        P("fsdp", None),
        P(),
        P(),
        P(),
        P(AX),
    )
    return jax.shard_map(
        compute,
        mesh=mesh,
        in_specs=placed,
        out_specs=(
            P(),
            P(),
            P(AX, None),
            P(AX, None),
            P(AX, None, None),
            P(AX, None, None),
            P(),
            P(),
        ),
        check_vma=False,
    )
```

```python
import functools

import jax
import jax.numpy as jnp
from jax import lax
from jax.experimental import pallas as pl
from jax.experimental.pallas import tpu as pltpu
from jax.sharding import PartitionSpec as P


grad_scale = 512.0
adapter_scale = 2.0
epsilon = 1e-05
AX = ("group", "fsdp")
NT = (((1,), (1,)), ((), ()))
TN = (((0,), (0,)), ((), ()))
f32 = jnp.float32
bf16 = jnp.bfloat16


def coords(i):
    g, f = divmod(i, 8)
    return (f // 4) * 2 + (g // 2) % 2, g // 4, f % 4, g % 2


def device(x, y, z, c):
    x, y, z = x % 4, y % 4, z % 4
    return ((y * 2 + x % 2) * 2 + c) * 8 + (x // 2) * 4 + z


def table(move):
    return [(i, device(*move(*coords(i)))) for i in range(128)]


MOVES = {
    "core": table(lambda x, y, z, c: (x, y, z, 1 - c)),
    "xnear": table(lambda x, y, z, c: (x ^ 1, y, z, c)),
    "xflip": table(lambda x, y, z, c: (3 - x, y, z, c)),
    "ynear": table(lambda x, y, z, c: (x, y ^ 1, z, c)),
    "yflip": table(lambda x, y, z, c: (x, 3 - y, z, c)),
    "znear": table(lambda x, y, z, c: (x, y, z ^ 1, c)),
    "zflip": table(lambda x, y, z, c: (x, y, 3 - z, c)),
    "yup": table(lambda x, y, z, c: (x, y + 1, z, c)),
    "ydown": table(lambda x, y, z, c: (x, y - 1, z, c)),
    "zup": table(lambda x, y, z, c: (x, y, z + 1, c)),
    "zdown": table(lambda x, y, z, c: (x, y, z - 1, c)),
    "zfar": table(lambda x, y, z, c: (x, y, z + 2, c)),
}


def send(value, move):
    return lax.ppermute(value, AX, MOVES[move])


def ordered(bit, mine, other, axis=0):
    return jnp.where(
        bit == 0,
        jnp.concatenate([mine, other], axis=axis),
        jnp.concatenate([other, mine], axis=axis),
    )


def pick(value, start, size, axis=0):
    return lax.dynamic_slice_in_dim(value, start, size, axis=axis)


def block_kernel(copies, n_src, first, scal, *refs):
    srcs = refs[:n_src]
    a_own, a_par, r_own, r_par, low, up, q_rows, q_f = refs[n_src : n_src + 8]
    rest = refs[n_src + 8 :]
    if first:
        hid_out, st_out, y_out = rest[:3]
        w_s, a_s, r_s, hid, hb_s, y_s, w_sem, in_sem, out_sem = rest[3:]
    else:
        y_in, st_in, _, hid_out, st_out, y_own, y_par, y_q = rest[:8]
        w_s, a_s, r_s, hid, hb_s, y_s, w_sem, in_sem, out_sem, yo_s, yp_s = rest[8:]
    half = pl.multiple_of(scal[12], 2048)
    inputs = [
        pltpu.make_async_copy(a_own, a_s.at[pl.ds(0, 256), :], in_sem.at[0]),
        pltpu.make_async_copy(a_par, a_s.at[pl.ds(256, 256), :], in_sem.at[1]),
    ]
    for j in range(4):
        col = pl.multiple_of(scal[8 + j] * 256, 256)
        here = pl.ds(j * 256, 256)
        far = pl.ds(pl.multiple_of(half + col, 256), 256)
        inputs.append(
            pltpu.make_async_copy(
                r_own.at[:, far], r_s.at[pl.ds(0, 256), here], in_sem.at[2 + 2 * j]
            )
        )
        inputs.append(
            pltpu.make_async_copy(
                r_par.at[:, pl.ds(col, 256)], r_s.at[pl.ds(256, 256), here], in_sem.at[3 + 2 * j]
            )
        )
    for copy in inputs:
        copy.start()
    for src, src_row, src_col, from_half, rows, shard, dst_row, block in copies:
        if from_half:
            col = half + pl.multiple_of(scal[8 + block] * 256, 256)
        else:
            col = src_col
        row = pl.multiple_of(scal[shard] * 512 + dst_row, 256)
        pltpu.make_async_copy(
            srcs[src].at[pl.ds(src_row, rows), pl.ds(col, 256)],
            w_s.at[pl.ds(row, rows), pl.ds(block * 256, 256)],
            w_sem.at[block],
        ).start()
    if not first:
        y_copy = pltpu.make_async_copy(y_in, y_s, in_sem.at[10])
        y_copy.start()
    for copy in inputs:
        copy.wait()
    st_out[...] = jnp.zeros_like(st_out) if first else st_in[...]

    def forward(j, carry):
        here = pl.ds(pl.multiple_of(j * 256, 256), 256)
        col = pl.ds(pl.multiple_of(scal[8 + j] * 256, 256), 256)
        pltpu.make_async_copy(w_s.at[:, here], w_s.at[:, here], w_sem.at[j]).wait()
        value = (
            r_s[:, here].astype(f32)
            + adapter_scale * jnp.dot(low[...], up[:, col], preferred_element_type=f32)
            + jnp.dot(a_s[...], w_s[:, here], preferred_element_type=f32)
        )
        hid[:, here] = value
        pltpu.make_async_copy(hid.at[:, here], hid_out.at[:, col], out_sem.at[2]).start()
        hb_s[pl.ds(0, 512), here] = value.astype(bf16)
        hb_s[pl.ds(512, 16), here] = q_rows[:, col]
        st_out[:, 0:16] += lax.dot_general(
            hb_s[:, here], up[:, col], NT, preferred_element_type=f32
        )
        st_out[0:512, 16:17] += jnp.sum(value * value, axis=1, keepdims=True)
        st_out[0:256, 17:18] += jnp.sum(value[:256] * q_f[0:1, col], axis=1, keepdims=True)
        st_out[256:512, 17:18] += jnp.sum(value[256:] * q_f[1:2, col], axis=1, keepdims=True)
        return carry

    lax.fori_loop(0, 4, forward, 0)
    if not first:
        y_copy.wait()

    def backward(shard, carry):
        columns = pl.ds(pl.multiple_of(scal[shard] * 512, 512), 512)
        part = lax.dot_general(hb_s[...], w_s[columns, :], NT, preferred_element_type=f32)
        if first:
            y_s[:, columns] = part
            pltpu.make_async_copy(y_s.at[:, columns], y_out.at[:, columns], out_sem.at[0]).start()
        else:
            part += y_s[:, columns]
            yo_s[:, columns] = part[:256]
            yp_s[:, columns] = part[256:512].astype(bf16)
            y_q[:, columns] = part[512:]
            pltpu.make_async_copy(yo_s.at[:, columns], y_own.at[:, columns], out_sem.at[0]).start()
            pltpu.make_async_copy(yp_s.at[:, columns], y_par.at[:, columns], out_sem.at[1]).start()
        return carry

    lax.fori_loop(0, 8, backward, 0)
    if first:
        pltpu.make_async_copy(y_s, y_out, out_sem.at[0]).wait()
    else:
        pltpu.make_async_copy(yo_s, y_own, out_sem.at[0]).wait()
        pltpu.make_async_copy(yp_s, y_par, out_sem.at[1]).wait()
    pltpu.make_async_copy(hid, hid, out_sem.at[2]).wait()


def block_call(copies, srcs, scal, a_own, a_par, r_own, r_par, low, up, q_rows, q_f, carry):
    vm = pl.BlockSpec(memory_space=pltpu.VMEM)
    anyspace = pl.BlockSpec(memory_space=pl.ANY)
    first = carry is None
    shapes = [jax.ShapeDtypeStruct((512, 2048), f32), jax.ShapeDtypeStruct((528, 128), f32)]
    args = [scal, *srcs, a_own, a_par, r_own, r_par, low, up, q_rows, q_f]
    in_specs = [pl.BlockSpec(memory_space=pltpu.SMEM)] + [anyspace] * (len(srcs) + 4) + [vm] * 4
    scratch = [
        pltpu.VMEM((4096, 1024), bf16),
        pltpu.VMEM((512, 4096), bf16),
        pltpu.VMEM((512, 1024), bf16),
        pltpu.VMEM((512, 1024), f32),
        pltpu.VMEM((528, 1024), bf16),
        pltpu.VMEM((528, 4096), f32),
        pltpu.SemaphoreType.DMA((4,)),
        pltpu.SemaphoreType.DMA((11,)),
        pltpu.SemaphoreType.DMA((3,)),
    ]
    if first:
        shapes += [jax.ShapeDtypeStruct((528, 4096), f32)]
        out_specs = [anyspace, vm, anyspace]
        aliases = {}
    else:
        shapes += [
            jax.ShapeDtypeStruct((256, 4096), f32),
            jax.ShapeDtypeStruct((256, 4096), bf16),
            jax.ShapeDtypeStruct((16, 4096), f32),
        ]
        out_specs = [anyspace, vm, anyspace, anyspace, vm]
        scratch += [pltpu.VMEM((256, 4096), f32), pltpu.VMEM((256, 4096), bf16)]
        in_specs += [anyspace, vm, anyspace]
        args += [carry[2], carry[1], carry[0]]
        aliases = {len(args) - 1: 0}
    return pl.pallas_call(
        functools.partial(block_kernel, copies, len(srcs), first),
        out_shape=shapes,
        in_specs=in_specs,
        out_specs=out_specs,
        scratch_shapes=scratch,
        input_output_aliases=aliases,
        compiler_params=pltpu.CompilerParams(vmem_limit_bytes=44 * 1024 * 1024),
        cost_estimate=pl.CostEstimate(
            flops=4 * 512 * 4096 * 1024, transcendentals=0, bytes_accessed=24 << 20
        ),
        name="block_first" if first else "block_last",
    )(*args)


REL = [(0, 0), (0, -1), (0, 1), (0, 2), (1, 0), (1, -1), (1, 1), (1, 2)]


def compute(
    query_embeddings,
    passage_embeddings,
    positives,
    logarithm_scale,
    residual_input,
    attention_head_outputs,
    output_weight,
    adapter_down_weight,
    adapter_up_weight,
    final_norm_weight,
    lengths,
):
    group = lax.axis_index("group")
    fsdp = lax.axis_index("fsdp")
    y, x_lo, c = group // 4, (group // 2) % 2, group % 2
    x_hi, z = fsdp // 4, fsdp % 4
    x = x_hi * 2 + x_lo
    half = c * 2048
    other_half = 2048 - half
    logit_scale = jnp.exp(logarithm_scale)
    a_own = attention_head_outputs.reshape(256, 4096)
    res_own = residual_input.reshape(256, 4096)

    extras = jnp.concatenate(
        [
            (positives // 16).astype(bf16)[:, None],
            (positives % 16).astype(bf16)[:, None],
            jnp.broadcast_to(lengths.astype(bf16)[:, None], (4, 1)),
            jnp.zeros((4, 125), bf16),
        ],
        axis=1,
    )
    both = jnp.concatenate([query_embeddings, passage_embeddings], axis=0)
    tags = jnp.concatenate([extras, extras], axis=0)
    mine = jnp.concatenate([pick(both, half, 2048, 1), tags], axis=1)
    theirs = send(jnp.concatenate([pick(both, other_half, 2048, 1), tags], axis=1), "core")
    q_chip = ordered(c, mine[:4], theirs[:4])
    p_chip = ordered(c, mine[4:, :2048], theirs[4:, :2048])
    len_par = theirs[0, 2050].astype(f32)

    s_g = pick(output_weight, half + y * 256, 256, 1)
    s_ab = pick(output_weight, half + 1024, 1024, 1)
    o_g = send(s_g, "xflip")
    o_ab = send(s_ab, "xflip")

    p_blk = ordered(y % 2, p_chip, send(p_chip, "ynear"))
    p_blk = ordered(y // 2, p_blk, send(p_blk, "yflip"))
    p_blk = ordered(z % 2, p_blk, send(p_blk, "znear"))
    p_blk = ordered(z // 2, p_blk, send(p_blk, "zflip"))
    q_blk = ordered(x % 2, q_chip, send(q_chip, "xnear"))
    q_far, q_blk, _ = lax.optimization_barrier((send(q_blk, "xflip"), q_blk, p_blk))
    q_blk = ordered(x // 2, q_blk, q_far)

    ga = jnp.concatenate([s_g, o_g, s_ab[:, :256]], axis=0)
    up0 = send(ga, "zup")
    dn0 = send(ga, "zdown")
    up1 = send(jnp.concatenate([up0[:512], up0[1024:1280]], axis=0), "zup")
    dn1 = send(jnp.concatenate([dn0[512:1024], dn0[1280:]], axis=0), "zdown")
    ya = jnp.concatenate([o_g, up0[:1024], dn0[:1024]], axis=0)
    yb = jnp.concatenate([up1[:512], dn1[:512]], axis=0)
    ya_u, ya_d = send(ya, "yup"), send(ya, "ydown")
    yb_u, yb_d = send(yb, "yup"), send(yb, "ydown")
    y_far0 = send(ya_u[:1792], "yup")
    y_far1 = send(jnp.concatenate([ya_d[1792:], yb_d], axis=0), "ydown")
    a_x = send(jnp.concatenate([up0[1024:], dn0[1024:], up1[512:], dn1[512:]], axis=0), "xflip")
    b0 = jnp.concatenate([s_ab[:, 256:], o_ab[:, 256:]], axis=0)
    b_up = send(b0, "zup")
    b_dn = send(b0, "zdown")
    b_far0 = send(b_up[:512], "zup")
    b_far1 = send(b_dn[512:], "zdown")

    q_feat = q_blk[:, :2048]
    positive = (q_blk[:, 2048].astype(f32) * 16 + q_blk[:, 2049].astype(f32)).astype(jnp.int32)
    row = jnp.arange(128, dtype=jnp.int32)
    row_c, row_y, row_z = (row // 4) % 2, (row // 8) % 4, row // 32
    passage_id = (((row_y * 2 + x_lo) * 2 + row_c) * 8 + x_hi * 4 + row_z) * 4 + row % 4
    partial = lax.dot_general(q_feat, p_blk, NT, preferred_element_type=f32)
    logits = logit_scale * (partial + send(partial, "core"))
    hit = positive[:, None] == passage_id[None, :]
    m = jnp.max(logits, axis=1)
    e = jnp.exp(logits - m[:, None])
    stats = jnp.stack(
        [m, jnp.sum(e, 1), jnp.sum(e * logits, 1), jnp.sum(jnp.where(hit, logits, 0.0), 1)]
    )
    for move in ("xnear", "xflip"):
        got = send(stats, move)
        top = jnp.maximum(stats[0], got[0])
        fa, fb = jnp.exp(stats[0] - top), jnp.exp(got[0] - top)
        stats = jnp.stack(
            [
                top,
                stats[1] * fa + got[1] * fb,
                stats[2] * fa + got[2] * fb,
                stats[3] + got[3],
            ]
        )
    log_norm = stats[0] + jnp.log(stats[1])
    loss_rows = log_norm - stats[3]
    scale_rows = stats[2] / stats[1] - stats[3]
    weight_half = jnp.exp(logits - log_norm[:, None]).astype(bf16)
    hot = hit.astype(bf16)
    q_part = jnp.dot(weight_half, p_blk, preferred_element_type=f32) - jnp.dot(
        hot, p_blk, preferred_element_type=f32
    )
    p_part = lax.dot_general(weight_half, q_feat, TN, preferred_element_type=f32) - lax.dot_general(
        hot, q_feat, TN, preferred_element_type=f32
    )
    xh, xl = x // 2, x % 2
    q_sum = pick(q_part, 16 * xh, 16) + send(pick(q_part, 16 * (1 - xh), 16), "xflip")
    q_sum = pick(q_sum, 8 * xl, 8) + send(pick(q_sum, 8 * (1 - xl), 8), "xnear")
    q_sum = logit_scale * q_sum

    a_own, res_own, _ = lax.optimization_barrier((a_own, res_own, q_sum))
    a_par = send(a_own, "core")
    r_par = send(pick(res_own, other_half, 2048, 1), "core")
    low = jnp.concatenate(
        [
            jnp.dot(a_own, adapter_down_weight, preferred_element_type=f32),
            jnp.dot(a_par, adapter_down_weight, preferred_element_type=f32),
        ],
        axis=0,
    ).astype(bf16)
    up_half = pick(adapter_up_weight, half, 2048, 1)
    gain = pick(final_norm_weight, half, 2048)
    q_own = pick(q_sum, 4 * c, 1) * gain[None]
    q_par = pick(q_sum, 4 * (1 - c), 1) * gain[None]
    q_f = jnp.concatenate([q_own, q_par, jnp.zeros((6, 2048), f32)], axis=0)
    q_hi = q_f[:2].astype(bf16)
    q_lo = (q_f[:2] - q_hi.astype(f32)).astype(bf16)
    q_rows = jnp.concatenate([q_hi, q_lo, jnp.zeros((12, 2048), bf16)], axis=0)

    shard_ids = [(x_hi ^ du) * 4 + (z + dz) % 4 for du, dz in REL]
    ring = [(y + dy) % 4 for dy in (0, -1, 1, 2)]
    numbers = lambda blocks: jnp.stack(
        shard_ids + [jnp.asarray(block, jnp.int32) for block in blocks] + [half]
    ).astype(jnp.int32)

    class Plan:
        def __init__(self):
            self.srcs, self.copies = [output_weight], []
            for block in range(4):
                self.copies.append((0, 0, 0, True, 512, 0, 0, block))

        def land(self, value, pieces, block, at=0, column=0):
            if not any(value is known for known in self.srcs):
                self.srcs.append(value)
            index = [value is known for known in self.srcs].index(True)
            for shard, dst_row, rows in pieces:
                self.copies.append((index, at, column, False, rows, shard, dst_row, block))
                at += rows

    whole = lambda shard: (shard, 0, 512)
    five, two = [whole(shard) for shard in (4, 1, 5, 2, 6)], [whole(3), whole(7)]
    early, late = Plan(), Plan()
    for block, (va, vb) in enumerate(((ya, yb), (ya_u, yb_u), (ya_d, yb_d))):
        early.land(va, five, block)
        early.land(vb, two, block)
    early.land(o_ab, [whole(4)], 3)
    early.land(up0, [whole(1)], 3, 1024)
    early.land(dn0, [whole(2)], 3, 1024)
    early.land(up1, [(3, 0, 256)], 3, 512)
    early.land(dn1, [(3, 256, 256)], 3, 512)
    early.land(a_x, [whole(5), whole(6), whole(7)], 3)
    for k in range(3):
        late.land(o_ab, [whole(4)], 1 + k, 0, 256 + 256 * k)
        late.land(b_up, [whole(1), whole(5)], 1 + k, 0, 256 * k)
        late.land(b_dn, [whole(2), whole(6)], 1 + k, 0, 256 * k)
        late.land(b_far0, [whole(3)], 1 + k, 0, 256 * k)
        late.land(b_far1, [whole(7)], 1 + k, 0, 256 * k)
    late.land(y_far0, five[:3] + [(2, 0, 256)], 0)
    late.land(y_far1, [(2, 256, 256), five[4]] + two, 0)
    shared = (a_own, a_par, res_own, r_par, low, up_half, q_rows, q_f)
    carry = block_call(early.copies, early.srcs, numbers(ring[:3] + [4]), *shared, None)
    hidden, stats_own, y_own, y_par, y_q = block_call(
        late.copies, late.srcs, numbers(ring[3:] + [5, 6, 7]), *shared, carry
    )

    v_own, v_par = y_q[0:1] + y_q[2:3], y_q[1:2] + y_q[3:4]
    packed = jnp.concatenate([stats_own, v_par.reshape(32, 128)], axis=0)
    got = send(packed, "core")
    y_got = send(y_par, "core")
    tok = stats_own[:512] + jnp.concatenate([got[256:512], got[:256]], axis=0)
    qu_own = stats_own[512, :16] + stats_own[514, :16] + got[513, :16] + got[515, :16]
    qu_par = stats_own[513, :16] + stats_own[515, :16] + got[512, :16] + got[514, :16]
    v = v_own + got[528:].reshape(1, 4096)
    position = jnp.arange(256, dtype=jnp.int32).astype(f32)
    len_own = lengths[0].astype(f32)
    w_tok = jnp.concatenate(
        [
            grad_scale * (position < len_own).astype(f32) / len_own,
            grad_scale * (position < len_par).astype(f32) / len_par,
        ]
    )
    inv = lax.rsqrt(tok[:, 16] / 4096 + epsilon)
    lead = inv * w_tok
    back = inv * inv * inv * (w_tok * tok[:, 17] / 4096)
    qu = jnp.concatenate(
        [jnp.broadcast_to(qu_own[None], (256, 16)), jnp.broadcast_to(qu_par[None], (256, 16))], 0
    )
    low_grad = (adapter_scale * (lead[:, None] * qu - back[:, None] * tok[:, :16])).astype(bf16)
    q_tok = jnp.concatenate(
        [jnp.broadcast_to(q_own, (256, 2048)), jnp.broadcast_to(q_par, (256, 2048))], axis=0
    )
    res_grad = (lead[:, None] * q_tok - back[:, None] * hidden).astype(bf16)
    r_got = send(res_grad[256:], "core")
    residual_grad = ordered(c, res_grad[:256], r_got, axis=1)
    attn_grad = (
        lead[:256, None] * v
        - back[:256, None] * (y_own + y_got.astype(f32))
        + lax.dot_general(low_grad[:256], adapter_down_weight, NT, preferred_element_type=f32)
    ).astype(bf16)

    up_part = adapter_scale * lax.dot_general(low, res_grad, TN, preferred_element_type=f32)
    down_part = lax.dot_general(
        low_grad[:256], pick(a_own, half, 2048, 1), TN, preferred_element_type=f32
    ) + lax.dot_general(low_grad[256:], pick(a_par, half, 2048, 1), TN, preferred_element_type=f32)
    my_row = (x * 2 + c) * 4
    sums = jnp.stack([jnp.sum(pick(loss_rows, my_row, 4)), jnp.sum(pick(scale_rows, my_row, 4))])
    tail = jnp.pad(sums[None], ((0, 7), (0, 2046)))
    total = jnp.concatenate([down_part / 128, up_part / 128, tail], axis=0)
    sides = [[i for i in range(128) if coords(i)[3] == side] for side in range(2)]
    swap = lambda value: lax.all_to_all(
        value, AX, 0, 0, axis_index_groups=sides, tiled=True
    )
    packed_total = total
    part = jnp.sum(swap(total.reshape(64, 1280)), axis=0, keepdims=True)
    total = swap(jnp.broadcast_to(part, (64, 1280))).reshape(40, 2048)
    mate = send(total, "core")
    loss = (total[32, 0] + mate[32, 0]) / 512
    scale_grad = (total[32, 1] + mate[32, 1]) / 512
    lora_down = ordered(c, total[:16], mate[:16], axis=1).T
    lora_up = ordered(c, total[16:32], mate[16:32], axis=1)

    p_sum = p_part
    for bit, n, move, until in (
        (z // 2, 64, "zflip", stats_own),
        (z % 2, 32, "znear", packed_total),
        (y // 2, 16, "yflip", part),
        (y % 2, 8, "ynear", attn_grad),
    ):
        got = send(pick(p_sum, n * (1 - bit), n), move)
        got, p_sum, _ = lax.optimization_barrier((got, p_sum, until))
        p_sum = pick(p_sum, n * bit, n) + got
    p_sum = logit_scale * p_sum
    keep = jnp.concatenate([pick(q_sum, 4 * c, 4), pick(p_sum, 4 * c, 4)], axis=0)
    give = jnp.concatenate([pick(q_sum, 4 * (1 - c), 4), pick(p_sum, 4 * (1 - c), 4)], axis=0)
    grads = ordered(c, keep, send(give, "core"), axis=1)
    return (
        loss,
        scale_grad,
        grads[:4],
        grads[4:],
        attn_grad[None],
        residual_grad[None],
        lora_down,
        lora_up,
    )


def solution(mesh):
    placed = (
        P(AX, None),
        P(AX, None),
        P(AX),
        P(),
        P(AX, None, None),
        P(AX, None, None),
        P("fsdp", None),
        P(),
        P(),
        P(),
        P(AX),
    )
    return jax.shard_map(
        compute,
        mesh=mesh,
        in_specs=placed,
        out_specs=(
            P(),
            P(),
            P(AX, None),
            P(AX, None),
            P(AX, None, None),
            P(AX, None, None),
            P(),
            P(),
        ),
        check_vma=False,
    )
```

```python
import functools

import jax
import jax.numpy as jnp
from jax import lax
from jax.experimental import pallas as pl
from jax.experimental.pallas import tpu as pltpu
from jax.sharding import PartitionSpec as P


grad_scale = 512.0
adapter_scale = 2.0
epsilon = 1e-05
AX = ("group", "fsdp")
NT = (((1,), (1,)), ((), ()))
TN = (((0,), (0,)), ((), ()))
f32 = jnp.float32
bf16 = jnp.bfloat16


def coords(i):
    g, f = divmod(i, 8)
    return (f // 4) * 2 + (g // 2) % 2, g // 4, f % 4, g % 2


def device(x, y, z, c):
    x, y, z = x % 4, y % 4, z % 4
    return ((y * 2 + x % 2) * 2 + c) * 8 + (x // 2) * 4 + z


def table(move):
    return [(i, device(*move(*coords(i)))) for i in range(128)]


MOVES = {
    "core": table(lambda x, y, z, c: (x, y, z, 1 - c)),
    "xnear": table(lambda x, y, z, c: (x ^ 1, y, z, c)),
    "xflip": table(lambda x, y, z, c: (3 - x, y, z, c)),
    "ynear": table(lambda x, y, z, c: (x, y ^ 1, z, c)),
    "yflip": table(lambda x, y, z, c: (x, 3 - y, z, c)),
    "znear": table(lambda x, y, z, c: (x, y, z ^ 1, c)),
    "zflip": table(lambda x, y, z, c: (x, y, 3 - z, c)),
    "yup": table(lambda x, y, z, c: (x, y + 1, z, c)),
    "ydown": table(lambda x, y, z, c: (x, y - 1, z, c)),
    "zup": table(lambda x, y, z, c: (x, y, z + 1, c)),
    "zdown": table(lambda x, y, z, c: (x, y, z - 1, c)),
    "zfar": table(lambda x, y, z, c: (x, y, z + 2, c)),
}


def send(value, move):
    return lax.ppermute(value, AX, MOVES[move])


def ordered(bit, mine, other, axis=0):
    return jnp.where(
        bit == 0,
        jnp.concatenate([mine, other], axis=axis),
        jnp.concatenate([other, mine], axis=axis),
    )


def pick(value, start, size, axis=0):
    return lax.dynamic_slice_in_dim(value, start, size, axis=axis)


def block_kernel(copies, n_src, first, scal, *refs):
    srcs = refs[:n_src]
    a_own, a_par, r_own, r_par, low, up, q_rows, q_f = refs[n_src : n_src + 8]
    rest = refs[n_src + 8 :]
    if first:
        hid_out, st_out, y_out = rest[:3]
        w_s, a_s, r_s, hid, hb_s, y_s, w_sem, in_sem, out_sem = rest[3:]
    else:
        y_in, st_in, _, hid_out, st_out, y_own, y_par, y_q = rest[:8]
        w_s, a_s, r_s, hid, hb_s, y_s, w_sem, in_sem, out_sem, yo_s, yp_s = rest[8:]
    half = pl.multiple_of(scal[12], 2048)
    inputs = [
        pltpu.make_async_copy(a_own, a_s.at[pl.ds(0, 256), :], in_sem.at[0]),
        pltpu.make_async_copy(a_par, a_s.at[pl.ds(256, 256), :], in_sem.at[1]),
    ]
    for j in range(4):
        col = pl.multiple_of(scal[8 + j] * 256, 256)
        here = pl.ds(j * 256, 256)
        far = pl.ds(pl.multiple_of(half + col, 256), 256)
        inputs.append(
            pltpu.make_async_copy(
                r_own.at[:, far], r_s.at[pl.ds(0, 256), here], in_sem.at[2 + 2 * j]
            )
        )
        inputs.append(
            pltpu.make_async_copy(
                r_par.at[:, pl.ds(col, 256)], r_s.at[pl.ds(256, 256), here], in_sem.at[3 + 2 * j]
            )
        )
    for copy in inputs:
        copy.start()
    for src, src_row, src_col, from_half, rows, shard, dst_row, block in copies:
        if from_half:
            col = half + pl.multiple_of(scal[8 + block] * 256, 256)
        else:
            col = src_col
        row = pl.multiple_of(scal[shard] * 512 + dst_row, 256)
        pltpu.make_async_copy(
            srcs[src].at[pl.ds(src_row, rows), pl.ds(col, 256)],
            w_s.at[pl.ds(row, rows), pl.ds(block * 256, 256)],
            w_sem.at[block],
        ).start()
    if not first:
        y_copy = pltpu.make_async_copy(y_in, y_s, in_sem.at[10])
        y_copy.start()
    for copy in inputs:
        copy.wait()
    st_out[...] = jnp.zeros_like(st_out) if first else st_in[...]

    def forward(j, carry):
        here = pl.ds(pl.multiple_of(j * 256, 256), 256)
        col = pl.ds(pl.multiple_of(scal[8 + j] * 256, 256), 256)
        pltpu.make_async_copy(w_s.at[:, here], w_s.at[:, here], w_sem.at[j]).wait()
        value = (
            r_s[:, here].astype(f32)
            + adapter_scale * jnp.dot(low[...], up[:, col], preferred_element_type=f32)
            + jnp.dot(a_s[...], w_s[:, here], preferred_element_type=f32)
        )
        hid[:, here] = value
        pltpu.make_async_copy(hid.at[:, here], hid_out.at[:, col], out_sem.at[2]).start()
        hb_s[pl.ds(0, 512), here] = value.astype(bf16)
        hb_s[pl.ds(512, 16), here] = q_rows[:, col]
        st_out[:, 0:16] += lax.dot_general(
            hb_s[:, here], up[:, col], NT, preferred_element_type=f32
        )
        st_out[0:512, 16:17] += jnp.sum(value * value, axis=1, keepdims=True)
        st_out[0:256, 17:18] += jnp.sum(value[:256] * q_f[0:1, col], axis=1, keepdims=True)
        st_out[256:512, 17:18] += jnp.sum(value[256:] * q_f[1:2, col], axis=1, keepdims=True)
        return carry

    lax.fori_loop(0, 4, forward, 0)
    if not first:
        y_copy.wait()

    def backward(shard, carry):
        columns = pl.ds(pl.multiple_of(scal[shard] * 512, 512), 512)
        part = lax.dot_general(hb_s[...], w_s[columns, :], NT, preferred_element_type=f32)
        if first:
            y_s[:, columns] = part
            pltpu.make_async_copy(y_s.at[:, columns], y_out.at[:, columns], out_sem.at[0]).start()
        else:
            part += y_s[:, columns]
            yo_s[:, columns] = part[:256]
            yp_s[:, columns] = part[256:512].astype(bf16)
            y_q[:, columns] = part[512:]
            pltpu.make_async_copy(yo_s.at[:, columns], y_own.at[:, columns], out_sem.at[0]).start()
            pltpu.make_async_copy(yp_s.at[:, columns], y_par.at[:, columns], out_sem.at[1]).start()
        return carry

    lax.fori_loop(0, 8, backward, 0)
    if first:
        pltpu.make_async_copy(y_s, y_out, out_sem.at[0]).wait()
    else:
        pltpu.make_async_copy(yo_s, y_own, out_sem.at[0]).wait()
        pltpu.make_async_copy(yp_s, y_par, out_sem.at[1]).wait()
    pltpu.make_async_copy(hid, hid, out_sem.at[2]).wait()


def block_call(copies, srcs, scal, a_own, a_par, r_own, r_par, low, up, q_rows, q_f, carry):
    vm = pl.BlockSpec(memory_space=pltpu.VMEM)
    anyspace = pl.BlockSpec(memory_space=pltpu.HBM)
    first = carry is None
    shapes = [jax.ShapeDtypeStruct((512, 2048), f32), jax.ShapeDtypeStruct((528, 128), f32)]
    args = [scal, *srcs, a_own, a_par, r_own, r_par, low, up, q_rows, q_f]
    in_specs = [pl.BlockSpec(memory_space=pltpu.SMEM)] + [anyspace] * (len(srcs) + 4) + [vm] * 4
    scratch = [
        pltpu.VMEM((4096, 1024), bf16),
        pltpu.VMEM((512, 4096), bf16),
        pltpu.VMEM((512, 1024), bf16),
        pltpu.VMEM((512, 1024), f32),
        pltpu.VMEM((528, 1024), bf16),
        pltpu.VMEM((528, 4096), f32),
        pltpu.SemaphoreType.DMA((4,)),
        pltpu.SemaphoreType.DMA((11,)),
        pltpu.SemaphoreType.DMA((3,)),
    ]
    if first:
        shapes += [jax.ShapeDtypeStruct((528, 4096), f32)]
        out_specs = [anyspace, vm, anyspace]
        aliases = {}
    else:
        shapes += [
            jax.ShapeDtypeStruct((256, 4096), f32),
            jax.ShapeDtypeStruct((256, 4096), bf16),
            jax.ShapeDtypeStruct((16, 4096), f32),
        ]
        out_specs = [anyspace, vm, anyspace, anyspace, vm]
        scratch += [pltpu.VMEM((256, 4096), f32), pltpu.VMEM((256, 4096), bf16)]
        in_specs += [anyspace, vm, anyspace]
        args += [carry[2], carry[1], carry[0]]
        aliases = {len(args) - 1: 0}
    args = [
        pltpu.with_memory_space_constraint(arg, pltpu.HBM) if spec is anyspace else arg
        for arg, spec in zip(args, in_specs)
    ]
    return pl.pallas_call(
        functools.partial(block_kernel, copies, len(srcs), first),
        out_shape=shapes,
        in_specs=in_specs,
        out_specs=out_specs,
        scratch_shapes=scratch,
        input_output_aliases=aliases,
        compiler_params=pltpu.CompilerParams(vmem_limit_bytes=44 * 1024 * 1024),
        cost_estimate=pl.CostEstimate(
            flops=4 * 512 * 4096 * 1024, transcendentals=0, bytes_accessed=24 << 20
        ),
        name="block_first" if first else "block_last",
    )(*args)


REL = [(0, 0), (0, -1), (0, 1), (0, 2), (1, 0), (1, -1), (1, 1), (1, 2)]


def compute(
    query_embeddings,
    passage_embeddings,
    positives,
    logarithm_scale,
    residual_input,
    attention_head_outputs,
    output_weight,
    adapter_down_weight,
    adapter_up_weight,
    final_norm_weight,
    lengths,
):
    group = lax.axis_index("group")
    fsdp = lax.axis_index("fsdp")
    y, x_lo, c = group // 4, (group // 2) % 2, group % 2
    x_hi, z = fsdp // 4, fsdp % 4
    x = x_hi * 2 + x_lo
    half = c * 2048
    other_half = 2048 - half
    logit_scale = jnp.exp(logarithm_scale)
    a_own = attention_head_outputs.reshape(256, 4096)
    res_own = residual_input.reshape(256, 4096)

    extras = jnp.concatenate(
        [
            (positives // 16).astype(bf16)[:, None],
            (positives % 16).astype(bf16)[:, None],
            jnp.broadcast_to(lengths.astype(bf16)[:, None], (4, 1)),
            jnp.zeros((4, 125), bf16),
        ],
        axis=1,
    )
    both = jnp.concatenate([query_embeddings, passage_embeddings], axis=0)
    tags = jnp.concatenate([extras, extras], axis=0)
    mine = jnp.concatenate([pick(both, half, 2048, 1), tags], axis=1)
    theirs = send(jnp.concatenate([pick(both, other_half, 2048, 1), tags], axis=1), "core")
    q_chip = ordered(c, mine[:4], theirs[:4])
    p_chip = ordered(c, mine[4:, :2048], theirs[4:, :2048])
    len_par = theirs[0, 2050].astype(f32)

    s_g = pick(output_weight, half + y * 256, 256, 1)
    s_ab = pick(output_weight, half + 1024, 1024, 1)
    o_g = send(s_g, "xflip")
    o_ab = send(s_ab, "xflip")

    p_blk = ordered(y % 2, p_chip, send(p_chip, "ynear"))
    p_blk = ordered(y // 2, p_blk, send(p_blk, "yflip"))
    p_half = p_blk
    p_blk = ordered(z % 2, p_blk, send(p_blk, "znear"))
    p_blk = ordered(z // 2, p_blk, send(p_blk, "zflip"))
    q_blk = ordered(x % 2, q_chip, send(q_chip, "xnear"))
    q_far, q_blk, _ = lax.optimization_barrier((send(q_blk, "xflip"), q_blk, p_blk))
    q_blk = ordered(x // 2, q_blk, q_far)

    ga = jnp.concatenate([s_g, o_g, s_ab[:, :256]], axis=0)
    up0 = send(ga, "zup")
    dn0 = send(ga, "zdown")
    up1 = send(jnp.concatenate([up0[:512], up0[1024:1280]], axis=0), "zup")
    dn1 = send(jnp.concatenate([dn0[512:1024], dn0[1280:]], axis=0), "zdown")
    ya = jnp.concatenate([o_g, up0[:1024], dn0[:1024]], axis=0)
    yb = jnp.concatenate([up1[:512], dn1[:512]], axis=0)
    ya_u, ya_d = send(ya, "yup"), send(ya, "ydown")
    yb_u, yb_d = send(yb, "yup"), send(yb, "ydown")
    y_far0 = send(ya_u[:1792], "yup")
    y_far1 = send(jnp.concatenate([ya_d[1792:], yb_d], axis=0), "ydown")
    a_x = send(jnp.concatenate([up0[1024:], dn0[1024:], up1[512:], dn1[512:]], axis=0), "xflip")
    b0 = jnp.concatenate([s_ab[:, 256:], o_ab[:, 256:]], axis=0)
    b_up = send(b0, "zup")
    b_dn = send(b0, "zdown")
    b_far0 = send(b_up[:512], "zup")
    b_far1 = send(b_dn[512:], "zdown")

    q_feat = q_blk[:, :2048]
    positive = (q_blk[:, 2048].astype(f32) * 16 + q_blk[:, 2049].astype(f32)).astype(jnp.int32)
    row = jnp.arange(128, dtype=jnp.int32)
    row_c, row_y, row_z = (row // 4) % 2, (row // 8) % 4, row // 32
    passage_id = (((row_y * 2 + x_lo) * 2 + row_c) * 8 + x_hi * 4 + row_z) * 4 + row % 4
    partial = lax.dot_general(q_feat, p_blk, NT, preferred_element_type=f32)
    logits = logit_scale * (partial + send(partial, "core"))
    hit = positive[:, None] == passage_id[None, :]
    m = jnp.max(logits, axis=1)
    e = jnp.exp(logits - m[:, None])
    stats = jnp.stack(
        [m, jnp.sum(e, 1), jnp.sum(e * logits, 1), jnp.sum(jnp.where(hit, logits, 0.0), 1)]
    )
    for move in ("xnear", "xflip"):
        got = send(stats, move)
        top = jnp.maximum(stats[0], got[0])
        fa, fb = jnp.exp(stats[0] - top), jnp.exp(got[0] - top)
        stats = jnp.stack(
            [
                top,
                stats[1] * fa + got[1] * fb,
                stats[2] * fa + got[2] * fb,
                stats[3] + got[3],
            ]
        )
    log_norm = stats[0] + jnp.log(stats[1])
    loss_rows = log_norm - stats[3]
    scale_rows = stats[2] / stats[1] - stats[3]
    loss_sums = jnp.sum(jnp.stack([loss_rows, scale_rows]), axis=1) / 8
    weight_half = jnp.exp(logits - log_norm[:, None]).astype(bf16)
    hot = hit.astype(bf16)
    q_part = jnp.dot(weight_half, p_blk, preferred_element_type=f32) - jnp.dot(
        hot, p_blk, preferred_element_type=f32
    )
    p_part = lax.dot_general(weight_half, q_feat, TN, preferred_element_type=f32) - lax.dot_general(
        hot, q_feat, TN, preferred_element_type=f32
    )
    xh, xl = x // 2, x % 2
    q_sum = pick(q_part, 16 * xh, 16) + send(pick(q_part, 16 * (1 - xh), 16), "xflip")
    q_sum = pick(q_sum, 8 * xl, 8) + send(pick(q_sum, 8 * (1 - xl), 8), "xnear")
    q_sum = logit_scale * q_sum

    a_own, res_own, _ = lax.optimization_barrier((a_own, res_own, p_half))
    a_par = send(a_own, "core")
    r_par = send(pick(res_own, other_half, 2048, 1), "core")
    low = jnp.concatenate(
        [
            jnp.dot(a_own, adapter_down_weight, preferred_element_type=f32),
            jnp.dot(a_par, adapter_down_weight, preferred_element_type=f32),
        ],
        axis=0,
    ).astype(bf16)
    up_half = pick(adapter_up_weight, half, 2048, 1)
    gain = pick(final_norm_weight, half, 2048)
    q_own = pick(q_sum, 4 * c, 1) * gain[None]
    q_par = pick(q_sum, 4 * (1 - c), 1) * gain[None]
    q_f = jnp.concatenate([q_own, q_par, jnp.zeros((6, 2048), f32)], axis=0)
    q_hi = q_f[:2].astype(bf16)
    q_lo = (q_f[:2] - q_hi.astype(f32)).astype(bf16)
    q_rows = jnp.concatenate([q_hi, q_lo, jnp.zeros((12, 2048), bf16)], axis=0)

    shard_ids = [(x_hi ^ du) * 4 + (z + dz) % 4 for du, dz in REL]
    ring = [(y + dy) % 4 for dy in (0, -1, 1, 2)]
    numbers = lambda blocks: jnp.stack(
        shard_ids + [jnp.asarray(block, jnp.int32) for block in blocks] + [half]
    ).astype(jnp.int32)

    class Plan:
        def __init__(self):
            self.srcs, self.copies = [output_weight], []
            for block in range(4):
                self.copies.append((0, 0, 0, True, 512, 0, 0, block))

        def land(self, value, pieces, block, at=0, column=0):
            if not any(value is known for known in self.srcs):
                self.srcs.append(value)
            index = [value is known for known in self.srcs].index(True)
            for shard, dst_row, rows in pieces:
                self.copies.append((index, at, column, False, rows, shard, dst_row, block))
                at += rows

    whole = lambda shard: (shard, 0, 512)
    five, two = [whole(shard) for shard in (4, 1, 5, 2, 6)], [whole(3), whole(7)]
    early, late = Plan(), Plan()
    for block, (va, vb) in enumerate(((ya, yb), (ya_u, yb_u), (ya_d, yb_d))):
        early.land(va, five, block)
        early.land(vb, two, block)
    early.land(o_ab, [whole(4)], 3)
    early.land(up0, [whole(1)], 3, 1024)
    early.land(dn0, [whole(2)], 3, 1024)
    early.land(up1, [(3, 0, 256)], 3, 512)
    early.land(dn1, [(3, 256, 256)], 3, 512)
    early.land(a_x, [whole(5), whole(6), whole(7)], 3)
    for k in range(3):
        late.land(o_ab, [whole(4)], 1 + k, 0, 256 + 256 * k)
        late.land(b_up, [whole(1), whole(5)], 1 + k, 0, 256 * k)
        late.land(b_dn, [whole(2), whole(6)], 1 + k, 0, 256 * k)
        late.land(b_far0, [whole(3)], 1 + k, 0, 256 * k)
        late.land(b_far1, [whole(7)], 1 + k, 0, 256 * k)
    late.land(y_far0, five[:3] + [(2, 0, 256)], 0)
    late.land(y_far1, [(2, 256, 256), five[4]] + two, 0)
    shared = (a_own, a_par, res_own, r_par, low, up_half, q_rows, q_f)
    carry = block_call(early.copies, early.srcs, numbers(ring[:3] + [4]), *shared, None)
    hidden, stats_own, y_own, y_par, y_q = block_call(
        late.copies, late.srcs, numbers(ring[3:] + [5, 6, 7]), *shared, carry
    )

    v_own, v_par = y_q[0:1] + y_q[2:3], y_q[1:2] + y_q[3:4]
    packed = jnp.concatenate([stats_own, v_par.reshape(32, 128)], axis=0)
    got = send(packed, "core")
    y_got = send(y_par, "core")
    tok = stats_own[:512] + jnp.concatenate([got[256:512], got[:256]], axis=0)
    qu_own = stats_own[512, :16] + stats_own[514, :16] + got[513, :16] + got[515, :16]
    qu_par = stats_own[513, :16] + stats_own[515, :16] + got[512, :16] + got[514, :16]
    v = v_own + got[528:].reshape(1, 4096)
    position = jnp.arange(256, dtype=jnp.int32).astype(f32)
    len_own = lengths[0].astype(f32)
    w_tok = jnp.concatenate(
        [
            grad_scale * (position < len_own).astype(f32) / len_own,
            grad_scale * (position < len_par).astype(f32) / len_par,
        ]
    )
    inv = lax.rsqrt(tok[:, 16] / 4096 + epsilon)
    lead = inv * w_tok
    back = inv * inv * inv * (w_tok * tok[:, 17] / 4096)
    qu = jnp.concatenate(
        [jnp.broadcast_to(qu_own[None], (256, 16)), jnp.broadcast_to(qu_par[None], (256, 16))], 0
    )
    low_grad = (adapter_scale * (lead[:, None] * qu - back[:, None] * tok[:, :16])).astype(bf16)
    q_tok = jnp.concatenate(
        [jnp.broadcast_to(q_own, (256, 2048)), jnp.broadcast_to(q_par, (256, 2048))], axis=0
    )
    res_grad = (lead[:, None] * q_tok - back[:, None] * hidden).astype(bf16)
    r_got = send(res_grad[256:], "core")
    residual_grad = ordered(c, res_grad[:256], r_got, axis=1)
    attn_grad = (
        lead[:256, None] * v
        - back[:256, None] * (y_own + y_got.astype(f32))
        + lax.dot_general(low_grad[:256], adapter_down_weight, NT, preferred_element_type=f32)
    ).astype(bf16)

    up_part = adapter_scale * lax.dot_general(low, res_grad, TN, preferred_element_type=f32)
    down_part = lax.dot_general(
        low_grad[:256], pick(a_own, half, 2048, 1), TN, preferred_element_type=f32
    ) + lax.dot_general(low_grad[256:], pick(a_par, half, 2048, 1), TN, preferred_element_type=f32)
    tail = jnp.pad(loss_sums[None], ((0, 7), (0, 2046)))
    total = jnp.concatenate([down_part / 128, up_part / 128, tail], axis=0)
    sides = [[i for i in range(128) if coords(i)[3] == side] for side in range(2)]
    swap = lambda value: lax.all_to_all(
        value, AX, 0, 0, axis_index_groups=sides, tiled=True
    )
    packed_total = total
    part = jnp.sum(swap(total.reshape(64, 1280)), axis=0, keepdims=True)
    total = swap(jnp.broadcast_to(part, (64, 1280))).reshape(40, 2048)
    mate = send(total, "core")
    loss = (total[32, 0] + mate[32, 0]) / 512
    scale_grad = (total[32, 1] + mate[32, 1]) / 512
    lora_down = ordered(c, total[:16], mate[:16], axis=1).T
    lora_up = ordered(c, total[16:32], mate[16:32], axis=1)

    p_sum = p_part
    for bit, n, move, until in (
        (z // 2, 64, "zflip", stats_own),
        (z % 2, 32, "znear", packed_total),
        (y // 2, 16, "yflip", part),
        (y % 2, 8, "ynear", attn_grad),
    ):
        got = send(pick(p_sum, n * (1 - bit), n), move)
        got, p_sum, _ = lax.optimization_barrier((got, p_sum, until))
        p_sum = pick(p_sum, n * bit, n) + got
    p_sum = logit_scale * p_sum
    keep = jnp.concatenate([pick(q_sum, 4 * c, 4), pick(p_sum, 4 * c, 4)], axis=0)
    give = jnp.concatenate([pick(q_sum, 4 * (1 - c), 4), pick(p_sum, 4 * (1 - c), 4)], axis=0)
    grads = ordered(c, keep, send(give, "core"), axis=1)
    return (
        loss,
        scale_grad,
        grads[:4],
        grads[4:],
        attn_grad[None],
        residual_grad[None],
        lora_down,
        lora_up,
    )


def solution(mesh):
    placed = (
        P(AX, None),
        P(AX, None),
        P(AX),
        P(),
        P(AX, None, None),
        P(AX, None, None),
        P("fsdp", None),
        P(),
        P(),
        P(),
        P(AX),
    )
    return jax.shard_map(
        compute,
        mesh=mesh,
        in_specs=placed,
        out_specs=(
            P(),
            P(),
            P(AX, None),
            P(AX, None),
            P(AX, None, None),
            P(AX, None, None),
            P(),
            P(),
        ),
        check_vma=False,
    )
```

```python
import functools

import jax
import jax.numpy as jnp
from jax import lax
from jax.experimental import pallas as pl
from jax.experimental.pallas import tpu as pltpu
from jax.sharding import PartitionSpec as P


grad_scale = 512.0
adapter_scale = 2.0
epsilon = 1e-05
AX = ("group", "fsdp")
NT = (((1,), (1,)), ((), ()))
TN = (((0,), (0,)), ((), ()))
f32 = jnp.float32
bf16 = jnp.bfloat16


def coords(i):
    g, f = divmod(i, 8)
    return (f // 4) * 2 + (g // 2) % 2, g // 4, f % 4, g % 2


def device(x, y, z, c):
    x, y, z = x % 4, y % 4, z % 4
    return ((y * 2 + x % 2) * 2 + c) * 8 + (x // 2) * 4 + z


def table(move):
    return [(i, device(*move(*coords(i)))) for i in range(128)]


MOVES = {
    "core": table(lambda x, y, z, c: (x, y, z, 1 - c)),
    "xnear": table(lambda x, y, z, c: (x ^ 1, y, z, c)),
    "xflip": table(lambda x, y, z, c: (3 - x, y, z, c)),
    "ynear": table(lambda x, y, z, c: (x, y ^ 1, z, c)),
    "yflip": table(lambda x, y, z, c: (x, 3 - y, z, c)),
    "znear": table(lambda x, y, z, c: (x, y, z ^ 1, c)),
    "zflip": table(lambda x, y, z, c: (x, y, 3 - z, c)),
    "yup": table(lambda x, y, z, c: (x, y + 1, z, c)),
    "ydown": table(lambda x, y, z, c: (x, y - 1, z, c)),
    "zup": table(lambda x, y, z, c: (x, y, z + 1, c)),
    "zdown": table(lambda x, y, z, c: (x, y, z - 1, c)),
    "zfar": table(lambda x, y, z, c: (x, y, z + 2, c)),
}


def send(value, move):
    return lax.ppermute(value, AX, MOVES[move])


def ordered(bit, mine, other, axis=0):
    return jnp.where(
        bit == 0,
        jnp.concatenate([mine, other], axis=axis),
        jnp.concatenate([other, mine], axis=axis),
    )


def pick(value, start, size, axis=0):
    return lax.dynamic_slice_in_dim(value, start, size, axis=axis)


def block_kernel(copies, n_src, first, scal, *refs):
    srcs = refs[:n_src]
    a_own, a_par, r_own, r_par, low, up, q_rows, q_f = refs[n_src : n_src + 8]
    rest = refs[n_src + 8 :]
    if first:
        hid_out, st_out, y_q, y_out = rest[:4]
        scratch = rest[4:]
    else:
        y_in, st_in, vq_in, _, hid_out, st_out, y_q, y_own, y_par = rest[:9]
        scratch = rest[9:]
    w_s, a_s, r_s, hid, ht_s, y_s, up_s, qf_s, qb_s, qt_s, w_sem, in_sem, out_sem = scratch[:13]
    if not first:
        yo_s, yp_s = scratch[13:]
    half = pl.multiple_of(scal[12], 2048)
    inputs = [
        pltpu.make_async_copy(a_own, a_s.at[pl.ds(0, 256), :], in_sem.at[0]),
        pltpu.make_async_copy(a_par, a_s.at[pl.ds(256, 256), :], in_sem.at[1]),
    ]
    for j in range(4):
        col = pl.multiple_of(scal[8 + j] * 256, 256)
        here = pl.ds(j * 256, 256)
        far = pl.ds(pl.multiple_of(half + col, 256), 256)
        inputs.append(
            pltpu.make_async_copy(
                r_own.at[:, far], r_s.at[pl.ds(0, 256), here], in_sem.at[2 + 2 * j]
            )
        )
        inputs.append(
            pltpu.make_async_copy(
                r_par.at[:, pl.ds(col, 256)], r_s.at[pl.ds(256, 256), here], in_sem.at[3 + 2 * j]
            )
        )
    for copy in inputs:
        copy.start()
    for src, src_row, src_col, from_half, rows, shard, dst_row, block in copies:
        if from_half:
            col = half + pl.multiple_of(scal[8 + block] * 256, 256)
        else:
            col = src_col
        row = pl.multiple_of(scal[shard] * 512 + dst_row, 256)
        pltpu.make_async_copy(
            srcs[src].at[pl.ds(src_row, rows), pl.ds(col, 256)],
            w_s.at[pl.ds(row, rows), pl.ds(block * 256, 256)],
            w_sem.at[block],
        ).start()
    if not first:
        y_copy = pltpu.make_async_copy(y_in, y_s, in_sem.at[10])
        y_copy.start()
    for copy in inputs:
        copy.wait()
    st_out[...] = jnp.zeros_like(st_out) if first else st_in[...]
    qb_s[...] = jnp.zeros_like(qb_s)
    for j in range(4):
        here = pl.ds(j * 256, 256)
        col = pl.ds(pl.multiple_of(scal[8 + j] * 256, 256), 256)
        up_s[:, here] = up[:, col]
        qf_s[:, here] = q_f[:, col]
        qb_s[pl.ds(0, 16), here] = q_rows[:, col]
    qt_s[...] = qb_s[...].T

    def forward(j, carry):
        here = pl.ds(pl.multiple_of(j * 512, 512), 512)
        for k in range(2):
            part = pl.ds(pl.multiple_of(j * 512 + k * 256, 256), 256)
            pltpu.make_async_copy(w_s.at[:, part], w_s.at[:, part], w_sem.at[2 * j + k]).wait()
        value = (
            r_s[:, here].astype(f32)
            + adapter_scale * jnp.dot(low[...], up_s[:, here], preferred_element_type=f32)
            + jnp.dot(a_s[...], w_s[:, here], preferred_element_type=f32)
        )
        hid[:, here] = value
        for k in range(2):
            part = pl.ds(pl.multiple_of(j * 512 + k * 256, 256), 256)
            col = pl.ds(pl.multiple_of(scal[8 + 2 * j + k] * 256, 256), 256)
            pltpu.make_async_copy(hid.at[:, part], hid_out.at[:, col], out_sem.at[2]).start()
        short = value.astype(bf16)
        ht_s[here, :] = short.T
        st_out[0:512, 0:16] += lax.dot_general(
            short, up_s[:, here], NT, preferred_element_type=f32
        )
        st_out[512:528, 0:16] += lax.dot_general(
            qb_s[0:16, here], up_s[:, here], NT, preferred_element_type=f32
        )
        st_out[0:512, 16:17] += jnp.sum(value * value, axis=1, keepdims=True)
        st_out[0:256, 17:18] += jnp.sum(value[:256] * qf_s[0:1, here], axis=1, keepdims=True)
        st_out[256:512, 17:18] += jnp.sum(value[256:] * qf_s[1:2, here], axis=1, keepdims=True)
        return carry

    lax.fori_loop(0, 2, forward, 0)
    if not first:
        y_copy.wait()

    def backward(shard, carry):
        columns = pl.ds(pl.multiple_of(scal[shard] * 512, 512), 512)
        rows = w_s[columns, :]
        part = jnp.dot(rows, ht_s[...], preferred_element_type=f32)
        vq = jnp.dot(rows, qt_s[...], preferred_element_type=f32).T[:16]
        if first:
            y_q[:, columns] = vq
            y_s[columns, :] = part
            pltpu.make_async_copy(y_s.at[columns, :], y_out.at[columns, :], out_sem.at[0]).start()
        else:
            y_q[:, columns] = vq + vq_in[:, columns]
            turned = (part + y_s[columns, :]).astype(bf16).T
            yo_s[:, columns] = turned[:256]
            yp_s[:, columns] = turned[256:]
            pltpu.make_async_copy(yo_s.at[:, columns], y_own.at[:, columns], out_sem.at[0]).start()
            pltpu.make_async_copy(yp_s.at[:, columns], y_par.at[:, columns], out_sem.at[1]).start()
        return carry

    lax.fori_loop(0, 8, backward, 0)
    if first:
        pltpu.make_async_copy(y_s, y_out, out_sem.at[0]).wait()
    else:
        pltpu.make_async_copy(yo_s, y_own, out_sem.at[0]).wait()
        pltpu.make_async_copy(yp_s, y_par, out_sem.at[1]).wait()
    pltpu.make_async_copy(hid, hid, out_sem.at[2]).wait()


def block_call(copies, srcs, scal, a_own, a_par, r_own, r_par, low, up, q_rows, q_f, carry):
    vm = pl.BlockSpec(memory_space=pltpu.VMEM)
    anyspace = pl.BlockSpec(memory_space=pltpu.HBM)
    first = carry is None
    shapes = [
        jax.ShapeDtypeStruct((512, 2048), f32),
        jax.ShapeDtypeStruct((528, 128), f32),
        jax.ShapeDtypeStruct((16, 4096), f32),
    ]
    out_specs = [anyspace, vm, vm]
    args = [scal, *srcs, a_own, a_par, r_own, r_par, low, up, q_rows, q_f]
    in_specs = [pl.BlockSpec(memory_space=pltpu.SMEM)] + [anyspace] * (len(srcs) + 4) + [vm] * 4
    scratch = [
        pltpu.VMEM((4096, 1024), bf16),
        pltpu.VMEM((512, 4096), bf16),
        pltpu.VMEM((512, 1024), bf16),
        pltpu.VMEM((512, 1024), f32),
        pltpu.VMEM((1024, 512), bf16),
        pltpu.VMEM((4096, 512), f32),
        pltpu.VMEM((16, 1024), bf16),
        pltpu.VMEM((8, 1024), f32),
        pltpu.VMEM((128, 1024), bf16),
        pltpu.VMEM((1024, 128), bf16),
        pltpu.SemaphoreType.DMA((4,)),
        pltpu.SemaphoreType.DMA((11,)),
        pltpu.SemaphoreType.DMA((3,)),
    ]
    if first:
        shapes += [jax.ShapeDtypeStruct((4096, 512), f32)]
        out_specs += [anyspace]
        aliases = {}
    else:
        shapes += [jax.ShapeDtypeStruct((256, 4096), bf16)] * 2
        out_specs += [anyspace, anyspace]
        scratch += [pltpu.VMEM((256, 4096), bf16)] * 2
        in_specs += [anyspace, vm, vm, anyspace]
        args += [carry[3], carry[1], carry[2], carry[0]]
        aliases = {len(args) - 1: 0}
    args = [
        pltpu.with_memory_space_constraint(arg, pltpu.HBM) if spec is anyspace else arg
        for arg, spec in zip(args, in_specs)
    ]
    return pl.pallas_call(
        functools.partial(block_kernel, copies, len(srcs), first),
        out_shape=shapes,
        in_specs=in_specs,
        out_specs=out_specs,
        scratch_shapes=scratch,
        input_output_aliases=aliases,
        compiler_params=pltpu.CompilerParams(vmem_limit_bytes=44 * 1024 * 1024),
        cost_estimate=pl.CostEstimate(
            flops=4 * 512 * 4096 * 1024, transcendentals=0, bytes_accessed=24 << 20
        ),
        name="block_first" if first else "block_last",
    )(*args)


REL = [(0, 0), (0, -1), (0, 1), (0, 2), (1, 0), (1, -1), (1, 1), (1, 2)]


def compute(
    query_embeddings,
    passage_embeddings,
    positives,
    logarithm_scale,
    residual_input,
    attention_head_outputs,
    output_weight,
    adapter_down_weight,
    adapter_up_weight,
    final_norm_weight,
    lengths,
):
    group = lax.axis_index("group")
    fsdp = lax.axis_index("fsdp")
    y, x_lo, c = group // 4, (group // 2) % 2, group % 2
    x_hi, z = fsdp // 4, fsdp % 4
    x = x_hi * 2 + x_lo
    half = c * 2048
    other_half = 2048 - half
    logit_scale = jnp.exp(logarithm_scale)
    a_own = attention_head_outputs.reshape(256, 4096)
    res_own = residual_input.reshape(256, 4096)

    extras = jnp.concatenate(
        [
            (positives // 16).astype(bf16)[:, None],
            (positives % 16).astype(bf16)[:, None],
            jnp.broadcast_to(lengths.astype(bf16)[:, None], (4, 1)),
            jnp.zeros((4, 125), bf16),
        ],
        axis=1,
    )
    both = jnp.concatenate([query_embeddings, passage_embeddings], axis=0)
    tags = jnp.concatenate([extras, extras], axis=0)
    mine = jnp.concatenate([pick(both, half, 2048, 1), tags], axis=1)
    theirs = send(jnp.concatenate([pick(both, other_half, 2048, 1), tags], axis=1), "core")
    q_chip = ordered(c, mine[:4], theirs[:4])
    p_chip = ordered(c, mine[4:, :2048], theirs[4:, :2048])
    len_par = theirs[0, 2050].astype(f32)

    s_g = pick(output_weight, half + y * 256, 256, 1)
    s_ab = pick(output_weight, half + 1024, 1024, 1)
    o_g = send(s_g, "xflip")
    o_ab = send(s_ab, "xflip")

    p_blk = ordered(y % 2, p_chip, send(p_chip, "ynear"))
    p_blk = ordered(y // 2, p_blk, send(p_blk, "yflip"))
    p_half = p_blk
    p_blk = ordered(z % 2, p_blk, send(p_blk, "znear"))
    p_blk = ordered(z // 2, p_blk, send(p_blk, "zflip"))
    q_blk = ordered(x % 2, q_chip, send(q_chip, "xnear"))
    q_far, q_blk, _ = lax.optimization_barrier((send(q_blk, "xflip"), q_blk, p_blk))
    q_blk = ordered(x // 2, q_blk, q_far)

    ga = jnp.concatenate([s_g, o_g, s_ab[:, :256]], axis=0)
    up0 = send(ga, "zup")
    dn0 = send(ga, "zdown")
    up1 = send(jnp.concatenate([up0[:512], up0[1024:1280]], axis=0), "zup")
    dn1 = send(jnp.concatenate([dn0[512:1024], dn0[1280:]], axis=0), "zdown")
    ya = jnp.concatenate([o_g, up0[:1024], dn0[:1024]], axis=0)
    yb = jnp.concatenate([up1[:512], dn1[:512]], axis=0)
    ya_u, ya_d = send(ya, "yup"), send(ya, "ydown")
    yb_u, yb_d = send(yb, "yup"), send(yb, "ydown")
    y_far0 = send(ya_u[:1792], "yup")
    y_far1 = send(jnp.concatenate([ya_d[1792:], yb_d], axis=0), "ydown")
    a_x = send(jnp.concatenate([up0[1024:], dn0[1024:], up1[512:], dn1[512:]], axis=0), "xflip")
    b0 = jnp.concatenate([s_ab[:, 256:], o_ab[:, 256:]], axis=0)
    b_up = send(b0, "zup")
    b_dn = send(b0, "zdown")
    b_far0 = send(b_up[:512], "zup")
    b_far1 = send(b_dn[512:], "zdown")

    q_feat = q_blk[:, :2048]
    positive = (q_blk[:, 2048].astype(f32) * 16 + q_blk[:, 2049].astype(f32)).astype(jnp.int32)
    row = jnp.arange(128, dtype=jnp.int32)
    row_c, row_y, row_z = (row // 4) % 2, (row // 8) % 4, row // 32
    passage_id = (((row_y * 2 + x_lo) * 2 + row_c) * 8 + x_hi * 4 + row_z) * 4 + row % 4
    partial = lax.dot_general(q_feat, p_blk, NT, preferred_element_type=f32)
    logits = logit_scale * (partial + send(partial, "core"))
    hit = positive[:, None] == passage_id[None, :]
    m = jnp.max(logits, axis=1)
    e = jnp.exp(logits - m[:, None])
    stats = jnp.stack(
        [m, jnp.sum(e, 1), jnp.sum(e * logits, 1), jnp.sum(jnp.where(hit, logits, 0.0), 1)]
    )
    for move in ("xnear", "xflip"):
        got = send(stats, move)
        top = jnp.maximum(stats[0], got[0])
        fa, fb = jnp.exp(stats[0] - top), jnp.exp(got[0] - top)
        stats = jnp.stack(
            [
                top,
                stats[1] * fa + got[1] * fb,
                stats[2] * fa + got[2] * fb,
                stats[3] + got[3],
            ]
        )
    log_norm = stats[0] + jnp.log(stats[1])
    loss_rows = log_norm - stats[3]
    scale_rows = stats[2] / stats[1] - stats[3]
    loss_sums = jnp.sum(jnp.stack([loss_rows, scale_rows]), axis=1) / 8
    weight_half = jnp.exp(logits - log_norm[:, None]).astype(bf16)
    hot = hit.astype(bf16)
    q_part = jnp.dot(weight_half, p_blk, preferred_element_type=f32) - jnp.dot(
        hot, p_blk, preferred_element_type=f32
    )
    p_part = lax.dot_general(weight_half, q_feat, TN, preferred_element_type=f32) - lax.dot_general(
        hot, q_feat, TN, preferred_element_type=f32
    )
    xh, xl = x // 2, x % 2
    q_sum = pick(q_part, 16 * xh, 16) + send(pick(q_part, 16 * (1 - xh), 16), "xflip")
    q_sum = pick(q_sum, 8 * xl, 8) + send(pick(q_sum, 8 * (1 - xl), 8), "xnear")
    q_sum = logit_scale * q_sum

    a_own, res_own, _ = lax.optimization_barrier((a_own, res_own, p_half))
    a_par = send(a_own, "core")
    r_par = send(pick(res_own, other_half, 2048, 1), "core")
    low = jnp.concatenate(
        [
            jnp.dot(a_own, adapter_down_weight, preferred_element_type=f32),
            jnp.dot(a_par, adapter_down_weight, preferred_element_type=f32),
        ],
        axis=0,
    ).astype(bf16)
    up_half = pick(adapter_up_weight, half, 2048, 1)
    gain = pick(final_norm_weight, half, 2048)
    q_own = pick(q_sum, 4 * c, 1) * gain[None]
    q_par = pick(q_sum, 4 * (1 - c), 1) * gain[None]
    q_f = jnp.concatenate([q_own, q_par, jnp.zeros((6, 2048), f32)], axis=0)
    q_hi = q_f[:2].astype(bf16)
    q_lo = (q_f[:2] - q_hi.astype(f32)).astype(bf16)
    q_rows = jnp.concatenate([q_hi, q_lo, jnp.zeros((12, 2048), bf16)], axis=0)

    shard_ids = [(x_hi ^ du) * 4 + (z + dz) % 4 for du, dz in REL]
    ring = [(y + dy) % 4 for dy in (0, -1, 1, 2)]
    numbers = lambda blocks: jnp.stack(
        shard_ids + [jnp.asarray(block, jnp.int32) for block in blocks] + [half]
    ).astype(jnp.int32)

    class Plan:
        def __init__(self):
            self.srcs, self.copies = [output_weight], []
            for block in range(4):
                self.copies.append((0, 0, 0, True, 512, 0, 0, block))

        def land(self, value, pieces, block, at=0, column=0):
            if not any(value is known for known in self.srcs):
                self.srcs.append(value)
            index = [value is known for known in self.srcs].index(True)
            for shard, dst_row, rows in pieces:
                self.copies.append((index, at, column, False, rows, shard, dst_row, block))
                at += rows

    whole = lambda shard: (shard, 0, 512)
    five, two = [whole(shard) for shard in (4, 1, 5, 2, 6)], [whole(3), whole(7)]
    early, late = Plan(), Plan()
    for block, (va, vb) in enumerate(((ya, yb), (ya_u, yb_u), (ya_d, yb_d))):
        early.land(va, five, block)
        early.land(vb, two, block)
    early.land(o_ab, [whole(4)], 3)
    early.land(up0, [whole(1)], 3, 1024)
    early.land(dn0, [whole(2)], 3, 1024)
    early.land(up1, [(3, 0, 256)], 3, 512)
    early.land(dn1, [(3, 256, 256)], 3, 512)
    early.land(a_x, [whole(5), whole(6), whole(7)], 3)
    for k in range(3):
        late.land(o_ab, [whole(4)], 1 + k, 0, 256 + 256 * k)
        late.land(b_up, [whole(1), whole(5)], 1 + k, 0, 256 * k)
        late.land(b_dn, [whole(2), whole(6)], 1 + k, 0, 256 * k)
        late.land(b_far0, [whole(3)], 1 + k, 0, 256 * k)
        late.land(b_far1, [whole(7)], 1 + k, 0, 256 * k)
    late.land(y_far0, five[:3] + [(2, 0, 256)], 0)
    late.land(y_far1, [(2, 256, 256), five[4]] + two, 0)
    shared = (a_own, a_par, res_own, r_par, low, up_half, q_rows, q_f)
    carry = block_call(early.copies, early.srcs, numbers(ring[:3] + [4]), *shared, None)
    hidden, stats_own, y_q, y_own, y_par = block_call(
        late.copies, late.srcs, numbers(ring[3:] + [5, 6, 7]), *shared, carry
    )

    v_own, v_par = y_q[0:1] + y_q[2:3], y_q[1:2] + y_q[3:4]
    packed = jnp.concatenate([stats_own, v_par.reshape(32, 128)], axis=0)
    got = send(packed, "core")
    y_got = send(y_par, "core")
    tok = stats_own[:512] + jnp.concatenate([got[256:512], got[:256]], axis=0)
    qu_own = stats_own[512, :16] + stats_own[514, :16] + got[513, :16] + got[515, :16]
    qu_par = stats_own[513, :16] + stats_own[515, :16] + got[512, :16] + got[514, :16]
    v = v_own + got[528:].reshape(1, 4096)
    position = jnp.arange(256, dtype=jnp.int32).astype(f32)
    len_own = lengths[0].astype(f32)
    w_tok = jnp.concatenate(
        [
            grad_scale * (position < len_own).astype(f32) / len_own,
            grad_scale * (position < len_par).astype(f32) / len_par,
        ]
    )
    inv = lax.rsqrt(tok[:, 16] / 4096 + epsilon)
    lead = inv * w_tok
    back = inv * inv * inv * (w_tok * tok[:, 17] / 4096)
    qu = jnp.concatenate(
        [jnp.broadcast_to(qu_own[None], (256, 16)), jnp.broadcast_to(qu_par[None], (256, 16))], 0
    )
    low_grad = (adapter_scale * (lead[:, None] * qu - back[:, None] * tok[:, :16])).astype(bf16)
    q_tok = jnp.concatenate(
        [jnp.broadcast_to(q_own, (256, 2048)), jnp.broadcast_to(q_par, (256, 2048))], axis=0
    )
    res_grad = (lead[:, None] * q_tok - back[:, None] * hidden).astype(bf16)
    r_got = send(res_grad[256:], "core")
    residual_grad = ordered(c, res_grad[:256], r_got, axis=1)
    attn_grad = (
        lead[:256, None] * v
        - back[:256, None] * (y_own.astype(f32) + y_got.astype(f32))
        + lax.dot_general(low_grad[:256], adapter_down_weight, NT, preferred_element_type=f32)
    ).astype(bf16)

    up_part = adapter_scale * lax.dot_general(low, res_grad, TN, preferred_element_type=f32)
    down_part = lax.dot_general(
        low_grad[:256], pick(a_own, half, 2048, 1), TN, preferred_element_type=f32
    ) + lax.dot_general(low_grad[256:], pick(a_par, half, 2048, 1), TN, preferred_element_type=f32)
    tail = jnp.pad(loss_sums[None], ((0, 7), (0, 2046)))
    total = jnp.concatenate([down_part / 128, up_part / 128, tail], axis=0)
    sides = [[i for i in range(128) if coords(i)[3] == side] for side in range(2)]
    swap = lambda value: lax.all_to_all(
        value, AX, 0, 0, axis_index_groups=sides, tiled=True
    )
    packed_total = total
    part = jnp.sum(swap(total.reshape(64, 1280)), axis=0, keepdims=True)
    total = swap(jnp.broadcast_to(part, (64, 1280))).reshape(40, 2048)
    mate = send(total, "core")
    loss = (total[32, 0] + mate[32, 0]) / 512
    scale_grad = (total[32, 1] + mate[32, 1]) / 512
    lora_down = ordered(c, total[:16], mate[:16], axis=1).T
    lora_up = ordered(c, total[16:32], mate[16:32], axis=1)

    p_sum = p_part
    for bit, n, move, until in (
        (z // 2, 64, "zflip", stats_own),
        (z % 2, 32, "znear", packed_total),
        (y // 2, 16, "yflip", part),
        (y % 2, 8, "ynear", attn_grad),
    ):
        got = send(pick(p_sum, n * (1 - bit), n), move)
        got, p_sum, _ = lax.optimization_barrier((got, p_sum, until))
        p_sum = pick(p_sum, n * bit, n) + got
    p_sum = logit_scale * p_sum
    keep = jnp.concatenate([pick(q_sum, 4 * c, 4), pick(p_sum, 4 * c, 4)], axis=0)
    give = jnp.concatenate([pick(q_sum, 4 * (1 - c), 4), pick(p_sum, 4 * (1 - c), 4)], axis=0)
    grads = ordered(c, keep, send(give, "core"), axis=1)
    return (
        loss,
        scale_grad,
        grads[:4],
        grads[4:],
        attn_grad[None],
        residual_grad[None],
        lora_down,
        lora_up,
    )


def solution(mesh):
    placed = (
        P(AX, None),
        P(AX, None),
        P(AX),
        P(),
        P(AX, None, None),
        P(AX, None, None),
        P("fsdp", None),
        P(),
        P(),
        P(),
        P(AX),
    )
    return jax.shard_map(
        compute,
        mesh=mesh,
        in_specs=placed,
        out_specs=(
            P(),
            P(),
            P(AX, None),
            P(AX, None),
            P(AX, None, None),
            P(AX, None, None),
            P(),
            P(),
        ),
        check_vma=False,
    )
```

```python
import functools

import jax
import jax.numpy as jnp
from jax import lax
from jax.experimental import pallas as pl
from jax.experimental.pallas import tpu as pltpu
from jax.sharding import PartitionSpec as P


grad_scale = 512.0
adapter_scale = 2.0
epsilon = 1e-05
AX = ("group", "fsdp")
NT = (((1,), (1,)), ((), ()))
TN = (((0,), (0,)), ((), ()))
f32 = jnp.float32
bf16 = jnp.bfloat16


def coords(i):
    g, f = divmod(i, 8)
    return (f // 4) * 2 + (g // 2) % 2, g // 4, f % 4, g % 2


def device(x, y, z, c):
    x, y, z = x % 4, y % 4, z % 4
    return ((y * 2 + x % 2) * 2 + c) * 8 + (x // 2) * 4 + z


def table(move):
    return [(i, device(*move(*coords(i)))) for i in range(128)]


MOVES = {
    "core": table(lambda x, y, z, c: (x, y, z, 1 - c)),
    "xnear": table(lambda x, y, z, c: (x ^ 1, y, z, c)),
    "xflip": table(lambda x, y, z, c: (3 - x, y, z, c)),
    "ynear": table(lambda x, y, z, c: (x, y ^ 1, z, c)),
    "yflip": table(lambda x, y, z, c: (x, 3 - y, z, c)),
    "znear": table(lambda x, y, z, c: (x, y, z ^ 1, c)),
    "zflip": table(lambda x, y, z, c: (x, y, 3 - z, c)),
    "yup": table(lambda x, y, z, c: (x, y + 1, z, c)),
    "ydown": table(lambda x, y, z, c: (x, y - 1, z, c)),
    "zup": table(lambda x, y, z, c: (x, y, z + 1, c)),
    "zdown": table(lambda x, y, z, c: (x, y, z - 1, c)),
    "zfar": table(lambda x, y, z, c: (x, y, z + 2, c)),
}


def send(value, move):
    return lax.ppermute(value, AX, MOVES[move])


def ordered(bit, mine, other, axis=0):
    return jnp.where(
        bit == 0,
        jnp.concatenate([mine, other], axis=axis),
        jnp.concatenate([other, mine], axis=axis),
    )


def pick(value, start, size, axis=0):
    return lax.dynamic_slice_in_dim(value, start, size, axis=axis)


def block_kernel(copies, n_src, first, scal, *refs):
    srcs = refs[:n_src]
    a_own, a_par, r_own, r_par, low, up, q_rows, q_f = refs[n_src : n_src + 8]
    rest = refs[n_src + 8 :]
    if first:
        hid_out, st_out = rest[:2]
        scratch = rest[2:]
    else:
        st_in, _, hid_out, st_out = rest[:4]
        scratch = rest[4:]
    w_s, a_s, r_s, hid, up_s, qf_s, w_sem, in_sem, out_sem = scratch
    half = pl.multiple_of(scal[12], 2048)
    inputs = [
        pltpu.make_async_copy(a_own, a_s.at[pl.ds(0, 256), :], in_sem.at[0]),
        pltpu.make_async_copy(a_par, a_s.at[pl.ds(256, 256), :], in_sem.at[1]),
    ]
    for j in range(4):
        col = pl.multiple_of(scal[8 + j] * 256, 256)
        here = pl.ds(j * 256, 256)
        far = pl.ds(pl.multiple_of(half + col, 256), 256)
        inputs.append(
            pltpu.make_async_copy(
                r_own.at[:, far], r_s.at[pl.ds(0, 256), here], in_sem.at[2 + 2 * j]
            )
        )
        inputs.append(
            pltpu.make_async_copy(
                r_par.at[:, pl.ds(col, 256)], r_s.at[pl.ds(256, 256), here], in_sem.at[3 + 2 * j]
            )
        )
    for copy in inputs:
        copy.start()
    for src, src_row, src_col, from_half, rows, shard, dst_row, block in copies:
        if from_half:
            col = half + pl.multiple_of(scal[8 + block] * 256, 256)
        else:
            col = src_col
        row = pl.multiple_of(scal[shard] * 512 + dst_row, 256)
        pltpu.make_async_copy(
            srcs[src].at[pl.ds(src_row, rows), pl.ds(col, 256)],
            w_s.at[pl.ds(row, rows), pl.ds(block * 256, 256)],
            w_sem.at[block],
        ).start()
    for copy in inputs:
        copy.wait()
    st_out[...] = jnp.zeros_like(st_out) if first else st_in[...]
    for j in range(4):
        here = pl.ds(j * 256, 256)
        col = pl.ds(pl.multiple_of(scal[8 + j] * 256, 256), 256)
        up_s[:, here] = up[:, col]
        qf_s[:, here] = q_f[:, col]

    def forward(j, carry):
        here = pl.ds(pl.multiple_of(j * 512, 512), 512)
        for k in range(2):
            part = pl.ds(pl.multiple_of(j * 512 + k * 256, 256), 256)
            pltpu.make_async_copy(w_s.at[:, part], w_s.at[:, part], w_sem.at[2 * j + k]).wait()
        hid[:, here] = jnp.dot(a_s[...], w_s[:, here], preferred_element_type=f32)

        def finish(i, carry):
            some = pl.ds(pl.multiple_of(i * 128, 128), 128)
            value = (
                hid[some, here]
                + r_s[some, here].astype(f32)
                + adapter_scale * jnp.dot(low[some, :], up_s[:, here], preferred_element_type=f32)
            )
            hid[some, here] = value
            short = value.astype(bf16)
            st_out[some, 0:16] += lax.dot_general(
                short, up_s[:, here], NT, preferred_element_type=f32
            )
            q_row = qf_s[pl.ds(i // 2, 1), here]
            st_out[some, 16:17] += jnp.sum(value * value, axis=1, keepdims=True)
            st_out[some, 17:18] += jnp.sum(value * q_row, axis=1, keepdims=True)
            return carry

        lax.fori_loop(0, 4, finish, 0)
        for k in range(2):
            part = pl.ds(pl.multiple_of(j * 512 + k * 256, 256), 256)
            col = pl.ds(pl.multiple_of(scal[8 + 2 * j + k] * 256, 256), 256)
            pltpu.make_async_copy(hid.at[:, part], hid_out.at[:, col], out_sem.at[2]).start()
        return carry

    lax.fori_loop(0, 2, forward, 0)
    if first:
        st_out[512:528, 0:16] = lax.dot_general(
            q_rows[...], up[...], NT, preferred_element_type=f32
        )
    pltpu.make_async_copy(hid, hid, out_sem.at[2]).wait()


def back_kernel(copies, n_src, scal, *refs):
    srcs = refs[:n_src]
    grad, low_t, down, y_own, y_par, w_s, t_s, y_s, yo_s, yp_s, w_sem, out_sem = refs[n_src:]
    half = pl.multiple_of(scal[16], 2048)
    for wanted in range(8):
        for src, src_row, src_col, from_half, rows, shard, dst_row, block in copies:
            if shard != wanted:
                continue
            at = pl.multiple_of(scal[8 + block] * 256, 256)
            row = pl.multiple_of(scal[shard] * 512 + dst_row, 256)
            pltpu.make_async_copy(
                srcs[src].at[pl.ds(src_row, rows), pl.ds(half + at if from_half else src_col, 256)],
                w_s.at[pl.ds(row, rows), pl.ds(at, 256)],
                w_sem.at[shard],
            ).start()

    def flip(i, carry):
        some = pl.ds(pl.multiple_of(i * 256, 256), 256)
        t_s[some, :] = grad[:, some].T
        return carry

    lax.fori_loop(0, 8, flip, 0)

    def backward(shard, carry):
        columns = pl.ds(pl.multiple_of(scal[shard] * 512, 512), 512)
        pltpu.make_async_copy(w_s.at[columns, :], w_s.at[columns, :], w_sem.at[shard]).wait()
        y_s[...] = jnp.dot(w_s[columns, :], t_s[...], preferred_element_type=f32)

        def turn(i, carry):
            part = pl.ds(pl.multiple_of(i * 128, 128), 128)
            some = pl.ds(pl.multiple_of(scal[shard] * 512 + i * 128, 128), 128)
            full = y_s[part, :] + lax.dot_general(
                down[:, some], low_t[...], TN, preferred_element_type=f32
            )
            turned = full.astype(bf16).T
            yo_s[:, some] = turned[:256]
            yp_s[:, some] = turned[256:]
            return carry

        lax.fori_loop(0, 4, turn, 0)
        pltpu.make_async_copy(yo_s.at[:, columns], y_own.at[:, columns], out_sem.at[0]).start()
        pltpu.make_async_copy(yp_s.at[:, columns], y_par.at[:, columns], out_sem.at[1]).start()
        return carry

    lax.fori_loop(0, 8, backward, 0)
    pltpu.make_async_copy(yo_s, y_own, out_sem.at[0]).wait()
    pltpu.make_async_copy(yp_s, y_par, out_sem.at[1]).wait()


def back_call(copies, srcs, scal, grad, low_t, down):
    vm = pl.BlockSpec(memory_space=pltpu.VMEM)
    anyspace = pl.BlockSpec(memory_space=pltpu.HBM)
    srcs = [pltpu.with_memory_space_constraint(src, pltpu.HBM) for src in srcs]
    return pl.pallas_call(
        functools.partial(back_kernel, copies, len(srcs)),
        out_shape=[jax.ShapeDtypeStruct((256, 4096), bf16)] * 2,
        in_specs=[pl.BlockSpec(memory_space=pltpu.SMEM)] + [anyspace] * len(srcs) + [vm] * 3,
        out_specs=[anyspace, anyspace],
        scratch_shapes=[
            pltpu.VMEM((4096, 2048), bf16),
            pltpu.VMEM((2048, 512), bf16),
            pltpu.VMEM((512, 512), f32),
            pltpu.VMEM((256, 4096), bf16),
            pltpu.VMEM((256, 4096), bf16),
            pltpu.SemaphoreType.DMA((8,)),
            pltpu.SemaphoreType.DMA((2,)),
        ],
        compiler_params=pltpu.CompilerParams(vmem_limit_bytes=40 * 1024 * 1024),
        cost_estimate=pl.CostEstimate(
            flops=2 * 512 * 4096 * 2048, transcendentals=0, bytes_accessed=24 << 20
        ),
        name="back",
    )(scal, *srcs, grad, low_t, down)


def block_call(copies, srcs, scal, a_own, a_par, r_own, r_par, low, up, q_rows, q_f, carry):
    vm = pl.BlockSpec(memory_space=pltpu.VMEM)
    anyspace = pl.BlockSpec(memory_space=pltpu.HBM)
    first = carry is None
    shapes = [jax.ShapeDtypeStruct((512, 2048), f32), jax.ShapeDtypeStruct((528, 128), f32)]
    out_specs = [anyspace, vm]
    args = [scal, *srcs, a_own, a_par, r_own, r_par, low, up, q_rows, q_f]
    in_specs = [pl.BlockSpec(memory_space=pltpu.SMEM)] + [anyspace] * (len(srcs) + 4) + [vm] * 4
    aliases = {}
    if not first:
        in_specs += [vm, anyspace]
        args += [carry[1], carry[0]]
        aliases = {len(args) - 1: 0}
    scratch = [
        pltpu.VMEM((4096, 1024), bf16),
        pltpu.VMEM((512, 4096), bf16),
        pltpu.VMEM((512, 1024), bf16),
        pltpu.VMEM((512, 1024), f32),
        pltpu.VMEM((16, 1024), bf16),
        pltpu.VMEM((8, 1024), f32),
        pltpu.SemaphoreType.DMA((4,)),
        pltpu.SemaphoreType.DMA((10,)),
        pltpu.SemaphoreType.DMA((3,)),
    ]
    args = [
        pltpu.with_memory_space_constraint(arg, pltpu.HBM) if spec is anyspace else arg
        for arg, spec in zip(args, in_specs)
    ]
    return pl.pallas_call(
        functools.partial(block_kernel, copies, len(srcs), first),
        out_shape=shapes,
        in_specs=in_specs,
        out_specs=out_specs,
        scratch_shapes=scratch,
        input_output_aliases=aliases,
        compiler_params=pltpu.CompilerParams(vmem_limit_bytes=28 * 1024 * 1024),
        cost_estimate=pl.CostEstimate(
            flops=2 * 512 * 4096 * 1024, transcendentals=0, bytes_accessed=16 << 20
        ),
        name="block_first" if first else "block_last",
    )(*args)


REL = [(0, 0), (0, -1), (0, 1), (0, 2), (1, 0), (1, -1), (1, 1), (1, 2)]


def compute(
    query_embeddings,
    passage_embeddings,
    positives,
    logarithm_scale,
    residual_input,
    attention_head_outputs,
    output_weight,
    adapter_down_weight,
    adapter_up_weight,
    final_norm_weight,
    lengths,
):
    group = lax.axis_index("group")
    fsdp = lax.axis_index("fsdp")
    y, x_lo, c = group // 4, (group // 2) % 2, group % 2
    x_hi, z = fsdp // 4, fsdp % 4
    x = x_hi * 2 + x_lo
    half = c * 2048
    other_half = 2048 - half
    logit_scale = jnp.exp(logarithm_scale)
    a_own = attention_head_outputs.reshape(256, 4096)
    res_own = residual_input.reshape(256, 4096)

    extras = jnp.concatenate(
        [
            (positives // 16).astype(bf16)[:, None],
            (positives % 16).astype(bf16)[:, None],
            jnp.broadcast_to(lengths.astype(bf16)[:, None], (4, 1)),
            jnp.zeros((4, 125), bf16),
        ],
        axis=1,
    )
    both = jnp.concatenate([query_embeddings, passage_embeddings], axis=0)
    tags = jnp.concatenate([extras, extras], axis=0)
    mine = jnp.concatenate([pick(both, half, 2048, 1), tags], axis=1)
    theirs = send(jnp.concatenate([pick(both, other_half, 2048, 1), tags], axis=1), "core")
    q_chip = ordered(c, mine[:4], theirs[:4])
    p_chip = ordered(c, mine[4:, :2048], theirs[4:, :2048])
    len_par = theirs[0, 2050].astype(f32)

    s_g = pick(output_weight, half + y * 256, 256, 1)
    s_ab = pick(output_weight, half + 1024, 1024, 1)
    o_g = send(s_g, "xflip")
    o_ab = send(s_ab, "xflip")

    p_blk = ordered(y % 2, p_chip, send(p_chip, "ynear"))
    p_blk = ordered(y // 2, p_blk, send(p_blk, "yflip"))
    p_half = p_blk
    p_blk = ordered(z % 2, p_blk, send(p_blk, "znear"))
    p_blk = ordered(z // 2, p_blk, send(p_blk, "zflip"))
    q_blk = ordered(x % 2, q_chip, send(q_chip, "xnear"))
    q_far, q_blk, _ = lax.optimization_barrier((send(q_blk, "xflip"), q_blk, p_blk))
    q_blk = ordered(x // 2, q_blk, q_far)

    ga = jnp.concatenate([s_g, o_g, s_ab[:, :256]], axis=0)
    up0 = send(ga, "zup")
    dn0 = send(ga, "zdown")
    up1 = send(jnp.concatenate([up0[:512], up0[1024:1280]], axis=0), "zup")
    dn1 = send(jnp.concatenate([dn0[512:1024], dn0[1280:]], axis=0), "zdown")
    ya = jnp.concatenate([o_g, up0[:1024], dn0[:1024]], axis=0)
    yb = jnp.concatenate([up1[:512], dn1[:512]], axis=0)
    ya_u, ya_d = send(ya, "yup"), send(ya, "ydown")
    yb_u, yb_d = send(yb, "yup"), send(yb, "ydown")
    y_far0 = send(ya_u[:1792], "yup")
    y_far1 = send(jnp.concatenate([ya_d[1792:], yb_d], axis=0), "ydown")
    a_x = send(jnp.concatenate([up0[1024:], dn0[1024:], up1[512:], dn1[512:]], axis=0), "xflip")
    b0 = jnp.concatenate([s_ab[:, 256:], o_ab[:, 256:]], axis=0)
    b_up = send(b0, "zup")
    b_dn = send(b0, "zdown")
    b_far0 = send(b_up[:512], "zup")
    b_far1 = send(b_dn[512:], "zdown")

    q_feat = q_blk[:, :2048]
    positive = (q_blk[:, 2048].astype(f32) * 16 + q_blk[:, 2049].astype(f32)).astype(jnp.int32)
    row = jnp.arange(128, dtype=jnp.int32)
    row_c, row_y, row_z = (row // 4) % 2, (row // 8) % 4, row // 32
    passage_id = (((row_y * 2 + x_lo) * 2 + row_c) * 8 + x_hi * 4 + row_z) * 4 + row % 4
    partial = lax.dot_general(q_feat, p_blk, NT, preferred_element_type=f32)
    logits = logit_scale * (partial + send(partial, "core"))
    hit = positive[:, None] == passage_id[None, :]
    m = jnp.max(logits, axis=1)
    e = jnp.exp(logits - m[:, None])
    stats = jnp.stack(
        [m, jnp.sum(e, 1), jnp.sum(e * logits, 1), jnp.sum(jnp.where(hit, logits, 0.0), 1)]
    )
    for move in ("xnear", "xflip"):
        got = send(stats, move)
        top = jnp.maximum(stats[0], got[0])
        fa, fb = jnp.exp(stats[0] - top), jnp.exp(got[0] - top)
        stats = jnp.stack(
            [
                top,
                stats[1] * fa + got[1] * fb,
                stats[2] * fa + got[2] * fb,
                stats[3] + got[3],
            ]
        )
    log_norm = stats[0] + jnp.log(stats[1])
    loss_rows = log_norm - stats[3]
    scale_rows = stats[2] / stats[1] - stats[3]
    loss_sums = jnp.sum(jnp.stack([loss_rows, scale_rows]), axis=1) / 8
    weight_half = jnp.exp(logits - log_norm[:, None]).astype(bf16)
    hot = hit.astype(bf16)
    q_part = jnp.dot(weight_half, p_blk, preferred_element_type=f32) - jnp.dot(
        hot, p_blk, preferred_element_type=f32
    )
    p_part = lax.dot_general(weight_half, q_feat, TN, preferred_element_type=f32) - lax.dot_general(
        hot, q_feat, TN, preferred_element_type=f32
    )
    xh, xl = x // 2, x % 2
    q_sum = pick(q_part, 16 * xh, 16) + send(pick(q_part, 16 * (1 - xh), 16), "xflip")
    q_sum = pick(q_sum, 8 * xl, 8) + send(pick(q_sum, 8 * (1 - xl), 8), "xnear")
    q_sum = logit_scale * q_sum

    a_own, res_own, _ = lax.optimization_barrier((a_own, res_own, p_half))
    a_par = send(a_own, "core")
    r_par = send(pick(res_own, other_half, 2048, 1), "core")
    low = jnp.concatenate(
        [
            jnp.dot(a_own, adapter_down_weight, preferred_element_type=f32),
            jnp.dot(a_par, adapter_down_weight, preferred_element_type=f32),
        ],
        axis=0,
    ).astype(bf16)
    up_half = pick(adapter_up_weight, half, 2048, 1)
    gain = pick(final_norm_weight, half, 2048)
    q_own = pick(q_sum, 4 * c, 1) * gain[None]
    q_par = pick(q_sum, 4 * (1 - c), 1) * gain[None]
    q_f = jnp.concatenate([q_own, q_par, jnp.zeros((6, 2048), f32)], axis=0)
    q_hi = q_f[:2].astype(bf16)
    q_lo = (q_f[:2] - q_hi.astype(f32)).astype(bf16)
    q_rows = jnp.concatenate([q_hi, q_lo, jnp.zeros((12, 2048), bf16)], axis=0)

    shard_ids = [(x_hi ^ du) * 4 + (z + dz) % 4 for du, dz in REL]
    ring = [(y + dy) % 4 for dy in (0, -1, 1, 2)]
    numbers = lambda blocks: jnp.stack(
        shard_ids + [jnp.asarray(block, jnp.int32) for block in blocks] + [half]
    ).astype(jnp.int32)

    class Plan:
        def __init__(self):
            self.srcs, self.copies = [output_weight], []
            for block in range(4):
                self.copies.append((0, 0, 0, True, 512, 0, 0, block))

        def land(self, value, pieces, block, at=0, column=0):
            if not any(value is known for known in self.srcs):
                self.srcs.append(value)
            index = [value is known for known in self.srcs].index(True)
            for shard, dst_row, rows in pieces:
                self.copies.append((index, at, column, False, rows, shard, dst_row, block))
                at += rows

    whole = lambda shard: (shard, 0, 512)
    five, two = [whole(shard) for shard in (4, 1, 5, 2, 6)], [whole(3), whole(7)]
    early, late = Plan(), Plan()
    for block, (va, vb) in enumerate(((ya, yb), (ya_u, yb_u), (ya_d, yb_d))):
        early.land(va, five, block)
        early.land(vb, two, block)
    early.land(o_ab, [whole(4)], 3)
    early.land(up0, [whole(1)], 3, 1024)
    early.land(dn0, [whole(2)], 3, 1024)
    early.land(up1, [(3, 0, 256)], 3, 512)
    early.land(dn1, [(3, 256, 256)], 3, 512)
    early.land(a_x, [whole(5), whole(6), whole(7)], 3)
    for k in range(3):
        late.land(o_ab, [whole(4)], 1 + k, 0, 256 + 256 * k)
        late.land(b_up, [whole(1), whole(5)], 1 + k, 0, 256 * k)
        late.land(b_dn, [whole(2), whole(6)], 1 + k, 0, 256 * k)
        late.land(b_far0, [whole(3)], 1 + k, 0, 256 * k)
        late.land(b_far1, [whole(7)], 1 + k, 0, 256 * k)
    late.land(y_far0, five[:3] + [(2, 0, 256)], 0)
    late.land(y_far1, [(2, 256, 256), five[4]] + two, 0)
    shared = (a_own, a_par, res_own, r_par, low, up_half, q_rows, q_f)
    carry = block_call(early.copies, early.srcs, numbers(ring[:3] + [4]), *shared, None)
    hidden, stats_own = block_call(
        late.copies, late.srcs, numbers(ring[3:] + [5, 6, 7]), *shared, carry
    )

    got = send(stats_own, "core")
    tok = stats_own[:512] + jnp.concatenate([got[256:512], got[:256]], axis=0)
    qu_own = stats_own[512, :16] + stats_own[514, :16] + got[513, :16] + got[515, :16]
    qu_par = stats_own[513, :16] + stats_own[515, :16] + got[512, :16] + got[514, :16]
    position = jnp.arange(256, dtype=jnp.int32).astype(f32)
    len_own = lengths[0].astype(f32)
    w_tok = jnp.concatenate(
        [
            grad_scale * (position < len_own).astype(f32) / len_own,
            grad_scale * (position < len_par).astype(f32) / len_par,
        ]
    )
    inv = lax.rsqrt(tok[:, 16] / 4096 + epsilon)
    lead = inv * w_tok
    back = inv * inv * inv * (w_tok * tok[:, 17] / 4096)
    qu = jnp.concatenate(
        [jnp.broadcast_to(qu_own[None], (256, 16)), jnp.broadcast_to(qu_par[None], (256, 16))], 0
    )
    low_grad = (adapter_scale * (lead[:, None] * qu - back[:, None] * tok[:, :16])).astype(bf16)
    q_tok = jnp.concatenate(
        [jnp.broadcast_to(q_own, (256, 2048)), jnp.broadcast_to(q_par, (256, 2048))], axis=0
    )
    res_grad = (lead[:, None] * q_tok - back[:, None] * hidden).astype(bf16)
    r_got = send(res_grad[256:], "core")
    residual_grad = ordered(c, res_grad[:256], r_got, axis=1)
    srcs, copies = [], []
    for plan, shift in ((early, 0), (late, 4)):
        for index, at, column, from_half, rows, shard, dst_row, block in plan.copies:
            value = plan.srcs[index]
            if not any(value is known for known in srcs):
                srcs.append(value)
            index = [value is known for known in srcs].index(True)
            copies.append((index, at, column, from_half, rows, shard, dst_row, block + shift))
    low_t = jnp.concatenate([low_grad[:256], jnp.zeros((256, 16), bf16)], axis=0).T
    y_own, y_par = back_call(
        copies,
        srcs,
        numbers(ring[:3] + [4] + ring[3:] + [5, 6, 7]),
        res_grad,
        low_t,
        adapter_down_weight.T,
    )
    y_got = send(y_par, "core")
    attn_grad = (y_own.astype(f32) + y_got.astype(f32)).astype(bf16)

    up_part = adapter_scale * lax.dot_general(low, res_grad, TN, preferred_element_type=f32)
    down_part = lax.dot_general(
        low_grad[:256], pick(a_own, half, 2048, 1), TN, preferred_element_type=f32
    ) + lax.dot_general(low_grad[256:], pick(a_par, half, 2048, 1), TN, preferred_element_type=f32)
    tail = jnp.pad(loss_sums[None], ((0, 7), (0, 2046)))
    total = jnp.concatenate([down_part / 128, up_part / 128, tail], axis=0)
    sides = [[i for i in range(128) if coords(i)[3] == side] for side in range(2)]
    swap = lambda value: lax.all_to_all(
        value, AX, 0, 0, axis_index_groups=sides, tiled=True
    )
    packed_total = total
    part = jnp.sum(swap(total.reshape(64, 1280)), axis=0, keepdims=True)
    total = swap(jnp.broadcast_to(part, (64, 1280))).reshape(40, 2048)
    mate = send(total, "core")
    loss = (total[32, 0] + mate[32, 0]) / 512
    scale_grad = (total[32, 1] + mate[32, 1]) / 512
    lora_down = ordered(c, total[:16], mate[:16], axis=1).T
    lora_up = ordered(c, total[16:32], mate[16:32], axis=1)

    p_sum = p_part
    for bit, n, move, until in (
        (z // 2, 64, "zflip", stats_own),
        (z % 2, 32, "znear", packed_total),
        (y // 2, 16, "yflip", part),
        (y % 2, 8, "ynear", attn_grad),
    ):
        got = send(pick(p_sum, n * (1 - bit), n), move)
        got, p_sum, _ = lax.optimization_barrier((got, p_sum, until))
        p_sum = pick(p_sum, n * bit, n) + got
    p_sum = logit_scale * p_sum
    keep = jnp.concatenate([pick(q_sum, 4 * c, 4), pick(p_sum, 4 * c, 4)], axis=0)
    give = jnp.concatenate([pick(q_sum, 4 * (1 - c), 4), pick(p_sum, 4 * (1 - c), 4)], axis=0)
    grads = ordered(c, keep, send(give, "core"), axis=1)
    return (
        loss,
        scale_grad,
        grads[:4],
        grads[4:],
        attn_grad[None],
        residual_grad[None],
        lora_down,
        lora_up,
    )


def solution(mesh):
    placed = (
        P(AX, None),
        P(AX, None),
        P(AX),
        P(),
        P(AX, None, None),
        P(AX, None, None),
        P("fsdp", None),
        P(),
        P(),
        P(),
        P(AX),
    )
    return jax.shard_map(
        compute,
        mesh=mesh,
        in_specs=placed,
        out_specs=(
            P(),
            P(),
            P(AX, None),
            P(AX, None),
            P(AX, None, None),
            P(AX, None, None),
            P(),
            P(),
        ),
        check_vma=False,
    )
```

```python
import functools

import jax
import jax.numpy as jnp
from jax import lax
from jax.experimental import pallas as pl
from jax.experimental.pallas import tpu as pltpu
from jax.sharding import PartitionSpec as P


grad_scale = 512.0
adapter_scale = 2.0
epsilon = 1e-05
AX = ("group", "fsdp")
NT = (((1,), (1,)), ((), ()))
TN = (((0,), (0,)), ((), ()))
f32 = jnp.float32
bf16 = jnp.bfloat16


def coords(i):
    g, f = divmod(i, 8)
    return (f // 4) * 2 + (g // 2) % 2, g // 4, f % 4, g % 2


def device(x, y, z, c):
    x, y, z = x % 4, y % 4, z % 4
    return ((y * 2 + x % 2) * 2 + c) * 8 + (x // 2) * 4 + z


def table(move):
    return [(i, device(*move(*coords(i)))) for i in range(128)]


MOVES = {
    "core": table(lambda x, y, z, c: (x, y, z, 1 - c)),
    "xnear": table(lambda x, y, z, c: (x ^ 1, y, z, c)),
    "xflip": table(lambda x, y, z, c: (3 - x, y, z, c)),
    "ynear": table(lambda x, y, z, c: (x, y ^ 1, z, c)),
    "yflip": table(lambda x, y, z, c: (x, 3 - y, z, c)),
    "znear": table(lambda x, y, z, c: (x, y, z ^ 1, c)),
    "zflip": table(lambda x, y, z, c: (x, y, 3 - z, c)),
    "yup": table(lambda x, y, z, c: (x, y + 1, z, c)),
    "ydown": table(lambda x, y, z, c: (x, y - 1, z, c)),
    "zup": table(lambda x, y, z, c: (x, y, z + 1, c)),
    "zdown": table(lambda x, y, z, c: (x, y, z - 1, c)),
    "zfar": table(lambda x, y, z, c: (x, y, z + 2, c)),
}


def send(value, move):
    return lax.ppermute(value, AX, MOVES[move])


def ordered(bit, mine, other, axis=0):
    return jnp.where(
        bit == 0,
        jnp.concatenate([mine, other], axis=axis),
        jnp.concatenate([other, mine], axis=axis),
    )


def pick(value, start, size, axis=0):
    return lax.dynamic_slice_in_dim(value, start, size, axis=axis)


def block_kernel(copies, n_src, first, scal, *refs):
    srcs = refs[:n_src]
    a_own, a_par, r_own, r_par, low, up, q_rows, q_f = refs[n_src : n_src + 8]
    rest = refs[n_src + 8 :]
    if first:
        hid_out, st_out = rest[:2]
        scratch = rest[2:]
    else:
        st_in, _, hid_out, st_out = rest[:4]
        scratch = rest[4:]
    w_s, a_s, r_s, hid, up_s, qf_s, w_sem, in_sem, out_sem = scratch
    half = pl.multiple_of(scal[12], 2048)
    inputs = [
        pltpu.make_async_copy(a_own, a_s.at[pl.ds(0, 256), :], in_sem.at[0]),
        pltpu.make_async_copy(a_par, a_s.at[pl.ds(256, 256), :], in_sem.at[1]),
    ]
    for j in range(4):
        col = pl.multiple_of(scal[8 + j] * 256, 256)
        here = pl.ds(j * 256, 256)
        far = pl.ds(pl.multiple_of(half + col, 256), 256)
        inputs.append(
            pltpu.make_async_copy(
                r_own.at[:, far], r_s.at[pl.ds(0, 256), here], in_sem.at[2 + 2 * j]
            )
        )
        inputs.append(
            pltpu.make_async_copy(
                r_par.at[:, pl.ds(col, 256)], r_s.at[pl.ds(256, 256), here], in_sem.at[3 + 2 * j]
            )
        )
    for copy in inputs:
        copy.start()
    for src, src_row, src_col, from_half, rows, shard, dst_row, block in copies:
        if from_half:
            col = half + pl.multiple_of(scal[8 + block] * 256, 256)
        else:
            col = src_col
        row = pl.multiple_of(scal[shard] * 512 + dst_row, 256)
        pltpu.make_async_copy(
            srcs[src].at[pl.ds(src_row, rows), pl.ds(col, 256)],
            w_s.at[pl.ds(row, rows), pl.ds(block * 256, 256)],
            w_sem.at[block],
        ).start()
    for copy in inputs:
        copy.wait()
    st_out[...] = jnp.zeros_like(st_out) if first else st_in[...]
    for j in range(4):
        here = pl.ds(j * 256, 256)
        col = pl.ds(pl.multiple_of(scal[8 + j] * 256, 256), 256)
        up_s[:, here] = up[:, col]
        qf_s[:, here] = q_f[:, col]

    def forward(j, carry):
        here = pl.ds(pl.multiple_of(j * 512, 512), 512)
        for k in range(2):
            part = pl.ds(pl.multiple_of(j * 512 + k * 256, 256), 256)
            pltpu.make_async_copy(w_s.at[:, part], w_s.at[:, part], w_sem.at[2 * j + k]).wait()
        hid[:, here] = jnp.dot(a_s[...], w_s[:, here], preferred_element_type=f32)

        def finish(i, carry):
            some = pl.ds(pl.multiple_of(i * 128, 128), 128)
            value = (
                hid[some, here]
                + r_s[some, here].astype(f32)
                + adapter_scale * jnp.dot(low[some, :], up_s[:, here], preferred_element_type=f32)
            )
            hid[some, here] = value
            short = value.astype(bf16)
            st_out[some, 0:16] += lax.dot_general(
                short, up_s[:, here], NT, preferred_element_type=f32
            )
            q_row = qf_s[pl.ds(i // 2, 1), here]
            st_out[some, 16:17] += jnp.sum(value * value, axis=1, keepdims=True)
            st_out[some, 17:18] += jnp.sum(value * q_row, axis=1, keepdims=True)
            return carry

        lax.fori_loop(0, 4, finish, 0)
        for k in range(2):
            part = pl.ds(pl.multiple_of(j * 512 + k * 256, 256), 256)
            col = pl.ds(pl.multiple_of(scal[8 + 2 * j + k] * 256, 256), 256)
            pltpu.make_async_copy(hid.at[:, part], hid_out.at[:, col], out_sem.at[2]).start()
        return carry

    lax.fori_loop(0, 2, forward, 0)
    if first:
        st_out[512:528, 0:16] = lax.dot_general(
            q_rows[...], up[...], NT, preferred_element_type=f32
        )
    pltpu.make_async_copy(hid, hid, out_sem.at[2]).wait()


def back_kernel(copies, n_src, scal, *refs):
    srcs = refs[:n_src]
    grad, low, down, y_own, y_par, w_s, y_s, yo_s, yp_s, w_sem, out_sem = refs[n_src:]
    half = pl.multiple_of(scal[16], 2048)
    for wanted in range(8):
        for src, src_row, src_col, from_half, rows, shard, dst_row, block in copies:
            if shard != wanted:
                continue
            at = pl.multiple_of(scal[8 + block] * 256, 256)
            row = pl.multiple_of(scal[shard] * 512 + dst_row, 256)
            pltpu.make_async_copy(
                srcs[src].at[pl.ds(src_row, rows), pl.ds(half + at if from_half else src_col, 256)],
                w_s.at[pl.ds(row, rows), pl.ds(at, 256)],
                w_sem.at[shard],
            ).start()

    def backward(shard, carry):
        columns = pl.ds(pl.multiple_of(scal[shard] * 512, 512), 512)
        pltpu.make_async_copy(w_s.at[columns, :], w_s.at[columns, :], w_sem.at[shard]).wait()
        y_s[...] = lax.dot_general(grad[...], w_s[columns, :], NT, preferred_element_type=f32)
        for i in range(2):
            some = pl.ds(i * 128, 128)
            yo_s[some, columns] = (
                y_s[some, :] + jnp.dot(low[some, :], down[:, columns], preferred_element_type=f32)
            ).astype(bf16)
            yp_s[some, columns] = y_s[pl.ds(256 + i * 128, 128), :].astype(bf16)
        pltpu.make_async_copy(yo_s.at[:, columns], y_own.at[:, columns], out_sem.at[0]).start()
        pltpu.make_async_copy(yp_s.at[:, columns], y_par.at[:, columns], out_sem.at[1]).start()
        return carry

    lax.fori_loop(0, 8, backward, 0)
    pltpu.make_async_copy(yo_s, y_own, out_sem.at[0]).wait()
    pltpu.make_async_copy(yp_s, y_par, out_sem.at[1]).wait()


def back_call(copies, srcs, scal, grad, low, down):
    vm = pl.BlockSpec(memory_space=pltpu.VMEM)
    anyspace = pl.BlockSpec(memory_space=pltpu.HBM)
    srcs = [pltpu.with_memory_space_constraint(src, pltpu.HBM) for src in srcs]
    return pl.pallas_call(
        functools.partial(back_kernel, copies, len(srcs)),
        out_shape=[jax.ShapeDtypeStruct((256, 4096), bf16)] * 2,
        in_specs=[pl.BlockSpec(memory_space=pltpu.SMEM)] + [anyspace] * len(srcs) + [vm] * 3,
        out_specs=[anyspace, anyspace],
        scratch_shapes=[
            pltpu.VMEM((4096, 2048), bf16),
            pltpu.VMEM((512, 512), f32),
            pltpu.VMEM((256, 4096), bf16),
            pltpu.VMEM((256, 4096), bf16),
            pltpu.SemaphoreType.DMA((8,)),
            pltpu.SemaphoreType.DMA((2,)),
        ],
        compiler_params=pltpu.CompilerParams(vmem_limit_bytes=40 * 1024 * 1024),
        cost_estimate=pl.CostEstimate(
            flops=2 * 512 * 4096 * 2048, transcendentals=0, bytes_accessed=24 << 20
        ),
        name="back",
    )(scal, *srcs, grad, low, down)


def block_call(copies, srcs, scal, a_own, a_par, r_own, r_par, low, up, q_rows, q_f, carry):
    vm = pl.BlockSpec(memory_space=pltpu.VMEM)
    anyspace = pl.BlockSpec(memory_space=pltpu.HBM)
    first = carry is None
    shapes = [jax.ShapeDtypeStruct((512, 2048), f32), jax.ShapeDtypeStruct((528, 128), f32)]
    out_specs = [anyspace, vm]
    args = [scal, *srcs, a_own, a_par, r_own, r_par, low, up, q_rows, q_f]
    in_specs = [pl.BlockSpec(memory_space=pltpu.SMEM)] + [anyspace] * (len(srcs) + 4) + [vm] * 4
    aliases = {}
    if not first:
        in_specs += [vm, anyspace]
        args += [carry[1], carry[0]]
        aliases = {len(args) - 1: 0}
    scratch = [
        pltpu.VMEM((4096, 1024), bf16),
        pltpu.VMEM((512, 4096), bf16),
        pltpu.VMEM((512, 1024), bf16),
        pltpu.VMEM((512, 1024), f32),
        pltpu.VMEM((16, 1024), bf16),
        pltpu.VMEM((8, 1024), f32),
        pltpu.SemaphoreType.DMA((4,)),
        pltpu.SemaphoreType.DMA((10,)),
        pltpu.SemaphoreType.DMA((3,)),
    ]
    args = [
        pltpu.with_memory_space_constraint(arg, pltpu.HBM) if spec is anyspace else arg
        for arg, spec in zip(args, in_specs)
    ]
    return pl.pallas_call(
        functools.partial(block_kernel, copies, len(srcs), first),
        out_shape=shapes,
        in_specs=in_specs,
        out_specs=out_specs,
        scratch_shapes=scratch,
        input_output_aliases=aliases,
        compiler_params=pltpu.CompilerParams(vmem_limit_bytes=28 * 1024 * 1024),
        cost_estimate=pl.CostEstimate(
            flops=2 * 512 * 4096 * 1024, transcendentals=0, bytes_accessed=16 << 20
        ),
        name="block_first" if first else "block_last",
    )(*args)


REL = [(0, 0), (0, -1), (0, 1), (0, 2), (1, 0), (1, -1), (1, 1), (1, 2)]


def compute(
    query_embeddings,
    passage_embeddings,
    positives,
    logarithm_scale,
    residual_input,
    attention_head_outputs,
    output_weight,
    adapter_down_weight,
    adapter_up_weight,
    final_norm_weight,
    lengths,
):
    group = lax.axis_index("group")
    fsdp = lax.axis_index("fsdp")
    y, x_lo, c = group // 4, (group // 2) % 2, group % 2
    x_hi, z = fsdp // 4, fsdp % 4
    x = x_hi * 2 + x_lo
    half = c * 2048
    other_half = 2048 - half
    logit_scale = jnp.exp(logarithm_scale)
    a_own = attention_head_outputs.reshape(256, 4096)
    res_own = residual_input.reshape(256, 4096)

    extras = jnp.concatenate(
        [
            (positives // 16).astype(bf16)[:, None],
            (positives % 16).astype(bf16)[:, None],
            jnp.broadcast_to(lengths.astype(bf16)[:, None], (4, 1)),
            jnp.zeros((4, 125), bf16),
        ],
        axis=1,
    )
    both = jnp.concatenate([query_embeddings, passage_embeddings], axis=0)
    tags = jnp.concatenate([extras, extras], axis=0)
    mine = jnp.concatenate([pick(both, half, 2048, 1), tags], axis=1)
    theirs = send(jnp.concatenate([pick(both, other_half, 2048, 1), tags], axis=1), "core")
    q_chip = ordered(c, mine[:4], theirs[:4])
    p_chip = ordered(c, mine[4:, :2048], theirs[4:, :2048])
    len_par = theirs[0, 2050].astype(f32)

    s_g = pick(output_weight, half + y * 256, 256, 1)
    s_ab = pick(output_weight, half + 1024, 1024, 1)
    o_g = send(s_g, "xflip")
    o_ab = send(s_ab, "xflip")

    p_blk = ordered(z % 2, p_chip, send(p_chip, "znear"))
    p_blk = ordered(z // 2, p_blk, send(p_blk, "zflip"))
    p_half = p_blk
    p_blk = ordered(y % 2, p_blk, send(p_blk, "ynear"))
    p_blk = ordered(y // 2, p_blk, send(p_blk, "yflip"))
    q_blk = ordered(x % 2, q_chip, send(q_chip, "xnear"))
    q_far, q_blk, _ = lax.optimization_barrier((send(q_blk, "xflip"), q_blk, p_blk))
    q_blk = ordered(x // 2, q_blk, q_far)

    ga = jnp.concatenate([s_g, o_g, s_ab[:, :256]], axis=0)
    up0 = send(ga, "zup")
    dn0 = send(ga, "zdown")
    up1 = send(jnp.concatenate([up0[:512], up0[1024:1280]], axis=0), "zup")
    dn1 = send(jnp.concatenate([dn0[512:1024], dn0[1280:]], axis=0), "zdown")
    ya = jnp.concatenate([o_g, up0[:1024], dn0[:1024]], axis=0)
    yb = jnp.concatenate([up1[:512], dn1[:512]], axis=0)
    ya_u, ya_d = send(ya, "yup"), send(ya, "ydown")
    yb_u, yb_d = send(yb, "yup"), send(yb, "ydown")
    y_far0 = send(ya_u[:1792], "yup")
    y_far1 = send(jnp.concatenate([ya_d[1792:], yb_d], axis=0), "ydown")
    a_x = send(jnp.concatenate([up0[1024:], dn0[1024:], up1[512:], dn1[512:]], axis=0), "xflip")
    b0 = jnp.concatenate([s_ab[:, 256:], o_ab[:, 256:]], axis=0)
    b_up = send(b0, "zup")
    b_dn = send(b0, "zdown")
    b_far0 = send(b_up[:512], "zup")
    b_far1 = send(b_dn[512:], "zdown")

    q_feat = q_blk[:, :2048]
    positive = (q_blk[:, 2048].astype(f32) * 16 + q_blk[:, 2049].astype(f32)).astype(jnp.int32)
    row = jnp.arange(128, dtype=jnp.int32)
    row_c, row_z, row_y = (row // 4) % 2, (row // 8) % 4, row // 32
    passage_id = (((row_y * 2 + x_lo) * 2 + row_c) * 8 + x_hi * 4 + row_z) * 4 + row % 4
    partial = lax.dot_general(q_feat, p_blk, NT, preferred_element_type=f32)
    logits = logit_scale * (partial + send(partial, "core"))
    hit = positive[:, None] == passage_id[None, :]
    m = jnp.max(logits, axis=1)
    e = jnp.exp(logits - m[:, None])
    stats = jnp.stack(
        [m, jnp.sum(e, 1), jnp.sum(e * logits, 1), jnp.sum(jnp.where(hit, logits, 0.0), 1)]
    )
    for move in ("xnear", "xflip"):
        got = send(stats, move)
        top = jnp.maximum(stats[0], got[0])
        fa, fb = jnp.exp(stats[0] - top), jnp.exp(got[0] - top)
        stats = jnp.stack(
            [
                top,
                stats[1] * fa + got[1] * fb,
                stats[2] * fa + got[2] * fb,
                stats[3] + got[3],
            ]
        )
    log_norm = stats[0] + jnp.log(stats[1])
    loss_rows = log_norm - stats[3]
    scale_rows = stats[2] / stats[1] - stats[3]
    loss_sums = jnp.sum(jnp.stack([loss_rows, scale_rows]), axis=1) / 8
    weight_half = jnp.exp(logits - log_norm[:, None]).astype(bf16)
    hot = hit.astype(bf16)
    q_part = jnp.dot(weight_half, p_blk, preferred_element_type=f32) - jnp.dot(
        hot, p_blk, preferred_element_type=f32
    )
    p_part = lax.dot_general(weight_half, q_feat, TN, preferred_element_type=f32) - lax.dot_general(
        hot, q_feat, TN, preferred_element_type=f32
    )
    xh, xl = x // 2, x % 2
    q_sum = pick(q_part, 16 * xh, 16) + send(pick(q_part, 16 * (1 - xh), 16), "xflip")
    q_sum = pick(q_sum, 8 * xl, 8) + send(pick(q_sum, 8 * (1 - xl), 8), "xnear")
    q_sum = logit_scale * q_sum

    a_own, res_own, _ = lax.optimization_barrier((a_own, res_own, p_half))
    a_par = send(a_own, "core")
    r_par = send(pick(res_own, other_half, 2048, 1), "core")
    low = jnp.concatenate(
        [
            jnp.dot(a_own, adapter_down_weight, preferred_element_type=f32),
            jnp.dot(a_par, adapter_down_weight, preferred_element_type=f32),
        ],
        axis=0,
    ).astype(bf16)
    up_half = pick(adapter_up_weight, half, 2048, 1)
    gain = pick(final_norm_weight, half, 2048)
    q_own = pick(q_sum, 4 * c, 1) * gain[None]
    q_par = pick(q_sum, 4 * (1 - c), 1) * gain[None]
    q_f = jnp.concatenate([q_own, q_par, jnp.zeros((6, 2048), f32)], axis=0)
    q_hi = q_f[:2].astype(bf16)
    q_lo = (q_f[:2] - q_hi.astype(f32)).astype(bf16)
    q_rows = jnp.concatenate([q_hi, q_lo, jnp.zeros((12, 2048), bf16)], axis=0)

    shard_ids = [(x_hi ^ du) * 4 + (z + dz) % 4 for du, dz in REL]
    ring = [(y + dy) % 4 for dy in (0, -1, 1, 2)]
    numbers = lambda blocks: jnp.stack(
        shard_ids + [jnp.asarray(block, jnp.int32) for block in blocks] + [half]
    ).astype(jnp.int32)

    class Plan:
        def __init__(self):
            self.srcs, self.copies = [output_weight], []
            for block in range(4):
                self.copies.append((0, 0, 0, True, 512, 0, 0, block))

        def land(self, value, pieces, block, at=0, column=0):
            if not any(value is known for known in self.srcs):
                self.srcs.append(value)
            index = [value is known for known in self.srcs].index(True)
            for shard, dst_row, rows in pieces:
                self.copies.append((index, at, column, False, rows, shard, dst_row, block))
                at += rows

    whole = lambda shard: (shard, 0, 512)
    five, two = [whole(shard) for shard in (4, 1, 5, 2, 6)], [whole(3), whole(7)]
    early, late = Plan(), Plan()
    for block, (va, vb) in enumerate(((ya, yb), (ya_u, yb_u), (ya_d, yb_d))):
        early.land(va, five, block)
        early.land(vb, two, block)
    early.land(o_ab, [whole(4)], 3)
    early.land(up0, [whole(1)], 3, 1024)
    early.land(dn0, [whole(2)], 3, 1024)
    early.land(up1, [(3, 0, 256)], 3, 512)
    early.land(dn1, [(3, 256, 256)], 3, 512)
    early.land(a_x, [whole(5), whole(6), whole(7)], 3)
    for k in range(3):
        late.land(o_ab, [whole(4)], 1 + k, 0, 256 + 256 * k)
        late.land(b_up, [whole(1), whole(5)], 1 + k, 0, 256 * k)
        late.land(b_dn, [whole(2), whole(6)], 1 + k, 0, 256 * k)
        late.land(b_far0, [whole(3)], 1 + k, 0, 256 * k)
        late.land(b_far1, [whole(7)], 1 + k, 0, 256 * k)
    late.land(y_far0, five[:3] + [(2, 0, 256)], 0)
    late.land(y_far1, [(2, 256, 256), five[4]] + two, 0)
    shared = (a_own, a_par, res_own, r_par, low, up_half, q_rows, q_f)
    carry = block_call(early.copies, early.srcs, numbers(ring[:3] + [4]), *shared, None)
    hidden, stats_own = block_call(
        late.copies, late.srcs, numbers(ring[3:] + [5, 6, 7]), *shared, carry
    )

    got = send(stats_own, "core")
    tok = stats_own[:512] + jnp.concatenate([got[256:512], got[:256]], axis=0)
    qu_own = stats_own[512, :16] + stats_own[514, :16] + got[513, :16] + got[515, :16]
    qu_par = stats_own[513, :16] + stats_own[515, :16] + got[512, :16] + got[514, :16]
    position = jnp.arange(256, dtype=jnp.int32).astype(f32)
    len_own = lengths[0].astype(f32)
    w_tok = jnp.concatenate(
        [
            grad_scale * (position < len_own).astype(f32) / len_own,
            grad_scale * (position < len_par).astype(f32) / len_par,
        ]
    )
    inv = lax.rsqrt(tok[:, 16] / 4096 + epsilon)
    lead = inv * w_tok
    back = inv * inv * inv * (w_tok * tok[:, 17] / 4096)
    qu = jnp.concatenate(
        [jnp.broadcast_to(qu_own[None], (256, 16)), jnp.broadcast_to(qu_par[None], (256, 16))], 0
    )
    low_grad = (adapter_scale * (lead[:, None] * qu - back[:, None] * tok[:, :16])).astype(bf16)
    q_tok = jnp.concatenate(
        [jnp.broadcast_to(q_own, (256, 2048)), jnp.broadcast_to(q_par, (256, 2048))], axis=0
    )
    res_grad = (lead[:, None] * q_tok - back[:, None] * hidden).astype(bf16)
    r_got = send(res_grad[256:], "core")
    residual_grad = ordered(c, res_grad[:256], r_got, axis=1)
    srcs, copies = [], []
    for plan, shift in ((early, 0), (late, 4)):
        for index, at, column, from_half, rows, shard, dst_row, block in plan.copies:
            value = plan.srcs[index]
            if not any(value is known for known in srcs):
                srcs.append(value)
            index = [value is known for known in srcs].index(True)
            copies.append((index, at, column, from_half, rows, shard, dst_row, block + shift))
    y_own, y_par = back_call(
        copies,
        srcs,
        numbers(ring[:3] + [4] + ring[3:] + [5, 6, 7]),
        res_grad,
        low_grad[:256],
        adapter_down_weight.T,
    )
    y_got = send(y_par, "core")
    attn_grad = (y_own.astype(f32) + y_got.astype(f32)).astype(bf16)

    up_part = adapter_scale * lax.dot_general(low, res_grad, TN, preferred_element_type=f32)
    down_part = lax.dot_general(
        low_grad[:256], pick(a_own, half, 2048, 1), TN, preferred_element_type=f32
    ) + lax.dot_general(low_grad[256:], pick(a_par, half, 2048, 1), TN, preferred_element_type=f32)
    tail = jnp.pad(loss_sums[None], ((0, 7), (0, 2046)))
    total = jnp.concatenate([down_part / 128, up_part / 128, tail], axis=0)
    sides = [[i for i in range(128) if coords(i)[3] == side] for side in range(2)]
    swap = lambda value: lax.all_to_all(
        value, AX, 0, 0, axis_index_groups=sides, tiled=True
    )
    packed_total = total
    part = jnp.sum(swap(total.reshape(64, 1280)), axis=0, keepdims=True)
    total = swap(jnp.broadcast_to(part, (64, 1280))).reshape(40, 2048)
    mate = send(total, "core")
    loss = (total[32, 0] + mate[32, 0]) / 512
    scale_grad = (total[32, 1] + mate[32, 1]) / 512
    lora_down = ordered(c, total[:16], mate[:16], axis=1).T
    lora_up = ordered(c, total[16:32], mate[16:32], axis=1)

    p_sum = p_part
    for bit, n, move, until in (
        (y // 2, 64, "yflip", stats_own),
        (y % 2, 32, "ynear", packed_total),
        (z // 2, 16, "zflip", y_par),
        (z % 2, 8, "znear", attn_grad),
    ):
        got = send(pick(p_sum, n * (1 - bit), n), move)
        got, p_sum, _ = lax.optimization_barrier((got, p_sum, until))
        p_sum = pick(p_sum, n * bit, n) + got
    p_sum = logit_scale * p_sum
    keep = jnp.concatenate([pick(q_sum, 4 * c, 4), pick(p_sum, 4 * c, 4)], axis=0)
    give = jnp.concatenate([pick(q_sum, 4 * (1 - c), 4), pick(p_sum, 4 * (1 - c), 4)], axis=0)
    grads = ordered(c, keep, send(give, "core"), axis=1)
    return (
        loss,
        scale_grad,
        grads[:4],
        grads[4:],
        attn_grad[None],
        residual_grad[None],
        lora_down,
        lora_up,
    )


def solution(mesh):
    placed = (
        P(AX, None),
        P(AX, None),
        P(AX),
        P(),
        P(AX, None, None),
        P(AX, None, None),
        P("fsdp", None),
        P(),
        P(),
        P(),
        P(AX),
    )
    return jax.shard_map(
        compute,
        mesh=mesh,
        in_specs=placed,
        out_specs=(
            P(),
            P(),
            P(AX, None),
            P(AX, None),
            P(AX, None, None),
            P(AX, None, None),
            P(),
            P(),
        ),
        check_vma=False,
    )
```

```python
import functools

import jax
import jax.numpy as jnp
from jax import lax
from jax.experimental import pallas as pl
from jax.experimental.pallas import tpu as pltpu
from jax.sharding import PartitionSpec as P


grad_scale = 512.0
adapter_scale = 2.0
epsilon = 1e-05
AX = ("group", "fsdp")
NT = (((1,), (1,)), ((), ()))
TN = (((0,), (0,)), ((), ()))
f32 = jnp.float32
bf16 = jnp.bfloat16


def coords(i):
    g, f = divmod(i, 8)
    return (f // 4) * 2 + (g // 2) % 2, g // 4, f % 4, g % 2


def device(x, y, z, c):
    x, y, z = x % 4, y % 4, z % 4
    return ((y * 2 + x % 2) * 2 + c) * 8 + (x // 2) * 4 + z


def table(move):
    return [(i, device(*move(*coords(i)))) for i in range(128)]


MOVES = {
    "core": table(lambda x, y, z, c: (x, y, z, 1 - c)),
    "xnear": table(lambda x, y, z, c: (x ^ 1, y, z, c)),
    "xflip": table(lambda x, y, z, c: (3 - x, y, z, c)),
    "ynear": table(lambda x, y, z, c: (x, y ^ 1, z, c)),
    "yflip": table(lambda x, y, z, c: (x, 3 - y, z, c)),
    "znear": table(lambda x, y, z, c: (x, y, z ^ 1, c)),
    "zflip": table(lambda x, y, z, c: (x, y, 3 - z, c)),
    "yup": table(lambda x, y, z, c: (x, y + 1, z, c)),
    "ydown": table(lambda x, y, z, c: (x, y - 1, z, c)),
    "zup": table(lambda x, y, z, c: (x, y, z + 1, c)),
    "zdown": table(lambda x, y, z, c: (x, y, z - 1, c)),
    "zfar": table(lambda x, y, z, c: (x, y, z + 2, c)),
}


def send(value, move):
    return lax.ppermute(value, AX, MOVES[move])


def ordered(bit, mine, other, axis=0):
    return jnp.where(
        bit == 0,
        jnp.concatenate([mine, other], axis=axis),
        jnp.concatenate([other, mine], axis=axis),
    )


def pick(value, start, size, axis=0):
    return lax.dynamic_slice_in_dim(value, start, size, axis=axis)


def block_kernel(copies, n_src, first, scal, *refs):
    srcs = refs[:n_src]
    a_own, a_par, r_own, r_par, low, up, q_rows, q_f = refs[n_src : n_src + 8]
    rest = refs[n_src + 8 :]
    if first:
        hid_out, st_out = rest[:2]
        scratch = rest[2:]
    else:
        st_in, _, hid_out, st_out = rest[:4]
        scratch = rest[4:]
    w_s, a_s, r_s, hid, up_s, qf_s, w_sem, in_sem, out_sem = scratch
    half = pl.multiple_of(scal[12], 2048)
    inputs = [
        pltpu.make_async_copy(a_own, a_s.at[pl.ds(0, 256), :], in_sem.at[0]),
        pltpu.make_async_copy(a_par, a_s.at[pl.ds(256, 256), :], in_sem.at[1]),
    ]
    for j in range(4):
        col = pl.multiple_of(scal[8 + j] * 256, 256)
        here = pl.ds(j * 256, 256)
        far = pl.ds(pl.multiple_of(half + col, 256), 256)
        inputs.append(
            pltpu.make_async_copy(
                r_own.at[:, far], r_s.at[pl.ds(0, 256), here], in_sem.at[2 + 2 * j]
            )
        )
        inputs.append(
            pltpu.make_async_copy(
                r_par.at[:, pl.ds(col, 256)], r_s.at[pl.ds(256, 256), here], in_sem.at[3 + 2 * j]
            )
        )
    for copy in inputs:
        copy.start()
    for src, src_row, src_col, from_half, rows, shard, dst_row, block in copies:
        if from_half:
            col = half + pl.multiple_of(scal[8 + block] * 256, 256)
        else:
            col = src_col
        row = pl.multiple_of(scal[shard] * 512 + dst_row, 256)
        pltpu.make_async_copy(
            srcs[src].at[pl.ds(src_row, rows), pl.ds(col, 256)],
            w_s.at[pl.ds(row, rows), pl.ds(block * 256, 256)],
            w_sem.at[block],
        ).start()
    for copy in inputs:
        copy.wait()
    st_out[...] = jnp.zeros_like(st_out) if first else st_in[...]
    for j in range(4):
        here = pl.ds(j * 256, 256)
        col = pl.ds(pl.multiple_of(scal[8 + j] * 256, 256), 256)
        up_s[:, here] = up[:, col]
        qf_s[:, here] = q_f[:, col]

    def forward(j, carry):
        here = pl.ds(pl.multiple_of(j * 512, 512), 512)
        for k in range(2):
            part = pl.ds(pl.multiple_of(j * 512 + k * 256, 256), 256)
            pltpu.make_async_copy(w_s.at[:, part], w_s.at[:, part], w_sem.at[2 * j + k]).wait()
        hid[:, here] = jnp.dot(a_s[...], w_s[:, here], preferred_element_type=f32)

        def finish(i, carry):
            some = pl.ds(pl.multiple_of(i * 128, 128), 128)
            value = (
                hid[some, here]
                + r_s[some, here].astype(f32)
                + adapter_scale * jnp.dot(low[some, :], up_s[:, here], preferred_element_type=f32)
            )
            hid[some, here] = value
            short = value.astype(bf16)
            st_out[some, 0:16] += lax.dot_general(
                short, up_s[:, here], NT, preferred_element_type=f32
            )
            q_row = qf_s[pl.ds(i // 2, 1), here]
            st_out[some, 16:17] += jnp.sum(value * value, axis=1, keepdims=True)
            st_out[some, 17:18] += jnp.sum(value * q_row, axis=1, keepdims=True)
            return carry

        lax.fori_loop(0, 4, finish, 0)
        for k in range(2):
            part = pl.ds(pl.multiple_of(j * 512 + k * 256, 256), 256)
            col = pl.ds(pl.multiple_of(scal[8 + 2 * j + k] * 256, 256), 256)
            pltpu.make_async_copy(hid.at[:, part], hid_out.at[:, col], out_sem.at[2]).start()
        return carry

    lax.fori_loop(0, 2, forward, 0)
    if first:
        st_out[512:528, 0:16] = lax.dot_general(
            q_rows[...], up[...], NT, preferred_element_type=f32
        )
    pltpu.make_async_copy(hid, hid, out_sem.at[2]).wait()


def back_kernel(copies, n_src, scal, *refs):
    srcs = refs[:n_src]
    grad, low, down, y_own, y_par, w_s, y_s, yo_s, yp_s, w_sem, out_sem = refs[n_src:]
    half = pl.multiple_of(scal[16], 2048)
    for wanted in range(8):
        for src, src_row, src_col, from_half, rows, shard, dst_row, block in copies:
            if shard != wanted:
                continue
            at = pl.multiple_of(scal[8 + block] * 256, 256)
            row = pl.multiple_of(scal[shard] * 512 + dst_row, 256)
            pltpu.make_async_copy(
                srcs[src].at[pl.ds(src_row, rows), pl.ds(half + at if from_half else src_col, 256)],
                w_s.at[pl.ds(row, rows), pl.ds(at, 256)],
                w_sem.at[shard],
            ).start()

    def backward(shard, carry):
        columns = pl.ds(pl.multiple_of(scal[shard] * 512, 512), 512)
        pltpu.make_async_copy(w_s.at[columns, :], w_s.at[columns, :], w_sem.at[shard]).wait()
        y_s[...] = lax.dot_general(grad[...], w_s[columns, :], NT, preferred_element_type=f32)
        for i in range(2):
            some = pl.ds(i * 128, 128)
            yo_s[some, columns] = (
                y_s[some, :] + jnp.dot(low[some, :], down[:, columns], preferred_element_type=f32)
            ).astype(bf16)
            yp_s[some, columns] = y_s[pl.ds(256 + i * 128, 128), :].astype(bf16)
        pltpu.make_async_copy(yo_s.at[:, columns], y_own.at[:, columns], out_sem.at[0]).start()
        pltpu.make_async_copy(yp_s.at[:, columns], y_par.at[:, columns], out_sem.at[1]).start()
        return carry

    lax.fori_loop(0, 8, backward, 0)
    pltpu.make_async_copy(yo_s, y_own, out_sem.at[0]).wait()
    pltpu.make_async_copy(yp_s, y_par, out_sem.at[1]).wait()


def back_call(copies, srcs, scal, grad, low, down):
    vm = pl.BlockSpec(memory_space=pltpu.VMEM)
    anyspace = pl.BlockSpec(memory_space=pltpu.HBM)
    srcs = [pltpu.with_memory_space_constraint(src, pltpu.HBM) for src in srcs]
    return pl.pallas_call(
        functools.partial(back_kernel, copies, len(srcs)),
        out_shape=[jax.ShapeDtypeStruct((256, 4096), bf16)] * 2,
        in_specs=[pl.BlockSpec(memory_space=pltpu.SMEM)] + [anyspace] * len(srcs) + [vm] * 3,
        out_specs=[anyspace, anyspace],
        scratch_shapes=[
            pltpu.VMEM((4096, 2048), bf16),
            pltpu.VMEM((512, 512), f32),
            pltpu.VMEM((256, 4096), bf16),
            pltpu.VMEM((256, 4096), bf16),
            pltpu.SemaphoreType.DMA((8,)),
            pltpu.SemaphoreType.DMA((2,)),
        ],
        compiler_params=pltpu.CompilerParams(vmem_limit_bytes=40 * 1024 * 1024),
        cost_estimate=pl.CostEstimate(
            flops=2 * 512 * 4096 * 2048, transcendentals=0, bytes_accessed=24 << 20
        ),
        name="back",
    )(scal, *srcs, grad, low, down)


def block_call(copies, srcs, scal, a_own, a_par, r_own, r_par, low, up, q_rows, q_f, carry):
    vm = pl.BlockSpec(memory_space=pltpu.VMEM)
    anyspace = pl.BlockSpec(memory_space=pltpu.HBM)
    first = carry is None
    shapes = [jax.ShapeDtypeStruct((512, 2048), f32), jax.ShapeDtypeStruct((528, 128), f32)]
    out_specs = [anyspace, vm]
    args = [scal, *srcs, a_own, a_par, r_own, r_par, low, up, q_rows, q_f]
    in_specs = [pl.BlockSpec(memory_space=pltpu.SMEM)] + [anyspace] * (len(srcs) + 4) + [vm] * 4
    aliases = {}
    if not first:
        in_specs += [vm, anyspace]
        args += [carry[1], carry[0]]
        aliases = {len(args) - 1: 0}
    scratch = [
        pltpu.VMEM((4096, 1024), bf16),
        pltpu.VMEM((512, 4096), bf16),
        pltpu.VMEM((512, 1024), bf16),
        pltpu.VMEM((512, 1024), f32),
        pltpu.VMEM((16, 1024), bf16),
        pltpu.VMEM((8, 1024), f32),
        pltpu.SemaphoreType.DMA((4,)),
        pltpu.SemaphoreType.DMA((10,)),
        pltpu.SemaphoreType.DMA((3,)),
    ]
    args = [
        pltpu.with_memory_space_constraint(arg, pltpu.HBM) if spec is anyspace else arg
        for arg, spec in zip(args, in_specs)
    ]
    return pl.pallas_call(
        functools.partial(block_kernel, copies, len(srcs), first),
        out_shape=shapes,
        in_specs=in_specs,
        out_specs=out_specs,
        scratch_shapes=scratch,
        input_output_aliases=aliases,
        compiler_params=pltpu.CompilerParams(vmem_limit_bytes=28 * 1024 * 1024),
        cost_estimate=pl.CostEstimate(
            flops=2 * 512 * 4096 * 1024, transcendentals=0, bytes_accessed=16 << 20
        ),
        name="block_first" if first else "block_last",
    )(*args)


REL = [(0, 0), (0, -1), (0, 1), (0, 2), (1, 0), (1, -1), (1, 1), (1, 2)]


def compute(
    query_embeddings,
    passage_embeddings,
    positives,
    logarithm_scale,
    residual_input,
    attention_head_outputs,
    output_weight,
    adapter_down_weight,
    adapter_up_weight,
    final_norm_weight,
    lengths,
):
    group = lax.axis_index("group")
    fsdp = lax.axis_index("fsdp")
    y, x_lo, c = group // 4, (group // 2) % 2, group % 2
    x_hi, z = fsdp // 4, fsdp % 4
    x = x_hi * 2 + x_lo
    half = c * 2048
    other_half = 2048 - half
    logit_scale = jnp.exp(logarithm_scale)
    a_own = attention_head_outputs.reshape(256, 4096)
    res_own = residual_input.reshape(256, 4096)

    extras = jnp.concatenate(
        [
            (positives // 16).astype(bf16)[:, None],
            (positives % 16).astype(bf16)[:, None],
            jnp.broadcast_to(lengths.astype(bf16)[:, None], (4, 1)),
            jnp.zeros((4, 125), bf16),
        ],
        axis=1,
    )
    both = jnp.concatenate([query_embeddings, passage_embeddings], axis=0)
    tags = jnp.concatenate([extras, extras], axis=0)
    mine = jnp.concatenate([pick(both, half, 2048, 1), tags], axis=1)
    theirs = send(jnp.concatenate([pick(both, other_half, 2048, 1), tags], axis=1), "core")
    q_chip = ordered(c, mine[:4], theirs[:4])
    p_chip = ordered(c, mine[4:, :2048], theirs[4:, :2048])
    len_par = theirs[0, 2050].astype(f32)

    s_g = pick(output_weight, half + y * 256, 256, 1)
    s_ab = pick(output_weight, half + 1024, 1024, 1)
    o_g = send(s_g, "xflip")
    o_ab = send(s_ab, "xflip")

    p_blk = ordered(y % 2, p_chip, send(p_chip, "ynear"))
    p_blk = ordered(y // 2, p_blk, send(p_blk, "yflip"))
    p_half = p_blk
    p_blk = ordered(z % 2, p_blk, send(p_blk, "znear"))
    p_blk = ordered(z // 2, p_blk, send(p_blk, "zflip"))
    q_blk = ordered(x % 2, q_chip, send(q_chip, "xnear"))
    q_far, q_blk, _ = lax.optimization_barrier((send(q_blk, "xflip"), q_blk, p_blk))
    q_blk = ordered(x // 2, q_blk, q_far)

    ga = jnp.concatenate([s_g, o_g, s_ab[:, :256]], axis=0)
    up0 = send(ga, "zup")
    dn0 = send(ga, "zdown")
    up1 = send(jnp.concatenate([up0[:512], up0[1024:1280]], axis=0), "zup")
    dn1 = send(jnp.concatenate([dn0[512:1024], dn0[1280:]], axis=0), "zdown")
    ya = jnp.concatenate([o_g, up0[:1024], dn0[:1024]], axis=0)
    yb = jnp.concatenate([up1[:512], dn1[:512]], axis=0)
    ya_u, ya_d = send(ya, "yup"), send(ya, "ydown")
    yb_u, yb_d = send(yb, "yup"), send(yb, "ydown")
    y_far0 = send(ya_u[:1792], "yup")
    y_far1 = send(jnp.concatenate([ya_d[1792:], yb_d], axis=0), "ydown")
    a_x = send(jnp.concatenate([up0[1024:], dn0[1024:], up1[512:], dn1[512:]], axis=0), "xflip")
    b0 = jnp.concatenate([s_ab[:, 256:], o_ab[:, 256:]], axis=0)
    b_up = send(b0, "zup")
    b_dn = send(b0, "zdown")
    b_far0 = send(b_up[:512], "zup")
    b_far1 = send(b_dn[512:], "zdown")

    q_feat = q_blk[:, :2048]
    positive = (q_blk[:, 2048].astype(f32) * 16 + q_blk[:, 2049].astype(f32)).astype(jnp.int32)
    row = jnp.arange(128, dtype=jnp.int32)
    row_c, row_y, row_z = (row // 4) % 2, (row // 8) % 4, row // 32
    passage_id = (((row_y * 2 + x_lo) * 2 + row_c) * 8 + x_hi * 4 + row_z) * 4 + row % 4
    partial = lax.dot_general(q_feat, p_blk, NT, preferred_element_type=f32)
    logits = logit_scale * (partial + send(partial, "core"))
    hit = positive[:, None] == passage_id[None, :]
    m = jnp.max(logits, axis=1)
    e = jnp.exp(logits - m[:, None])
    stats = jnp.stack(
        [m, jnp.sum(e, 1), jnp.sum(e * logits, 1), jnp.sum(jnp.where(hit, logits, 0.0), 1)]
    )
    for move in ("xnear", "xflip"):
        got = send(stats, move)
        top = jnp.maximum(stats[0], got[0])
        fa, fb = jnp.exp(stats[0] - top), jnp.exp(got[0] - top)
        stats = jnp.stack(
            [
                top,
                stats[1] * fa + got[1] * fb,
                stats[2] * fa + got[2] * fb,
                stats[3] + got[3],
            ]
        )
    log_norm = stats[0] + jnp.log(stats[1])
    loss_rows = log_norm - stats[3]
    scale_rows = stats[2] / stats[1] - stats[3]
    loss_sums = jnp.sum(jnp.stack([loss_rows, scale_rows]), axis=1) / 8
    weight_half = jnp.exp(logits - log_norm[:, None]).astype(bf16)
    hot = hit.astype(bf16)
    q_part = jnp.dot(weight_half, p_blk, preferred_element_type=f32) - jnp.dot(
        hot, p_blk, preferred_element_type=f32
    )
    p_part = lax.dot_general(weight_half, q_feat, TN, preferred_element_type=f32) - lax.dot_general(
        hot, q_feat, TN, preferred_element_type=f32
    )
    xh, xl = x // 2, x % 2
    q_sum = pick(q_part, 16 * xh, 16) + send(pick(q_part, 16 * (1 - xh), 16), "xflip")
    q_sum = pick(q_sum, 8 * xl, 8) + send(pick(q_sum, 8 * (1 - xl), 8), "xnear")
    q_sum = logit_scale * q_sum

    a_own, res_own, _ = lax.optimization_barrier((a_own, res_own, p_half))
    a_par = send(a_own, "core")
    r_par = send(pick(res_own, other_half, 2048, 1), "core")
    low = jnp.concatenate(
        [
            jnp.dot(a_own, adapter_down_weight, preferred_element_type=f32),
            jnp.dot(a_par, adapter_down_weight, preferred_element_type=f32),
        ],
        axis=0,
    ).astype(bf16)
    up_half = pick(adapter_up_weight, half, 2048, 1)
    gain = pick(final_norm_weight, half, 2048)
    q_own = pick(q_sum, 4 * c, 1) * gain[None]
    q_par = pick(q_sum, 4 * (1 - c), 1) * gain[None]
    q_f = jnp.concatenate([q_own, q_par, jnp.zeros((6, 2048), f32)], axis=0)
    q_hi = q_f[:2].astype(bf16)
    q_lo = (q_f[:2] - q_hi.astype(f32)).astype(bf16)
    q_rows = jnp.concatenate([q_hi, q_lo, jnp.zeros((12, 2048), bf16)], axis=0)

    shard_ids = [(x_hi ^ du) * 4 + (z + dz) % 4 for du, dz in REL]
    ring = [(y + dy) % 4 for dy in (0, -1, 1, 2)]
    numbers = lambda blocks: jnp.stack(
        shard_ids + [jnp.asarray(block, jnp.int32) for block in blocks] + [half]
    ).astype(jnp.int32)

    class Plan:
        def __init__(self):
            self.srcs, self.copies = [output_weight], []
            for block in range(4):
                self.copies.append((0, 0, 0, True, 512, 0, 0, block))

        def land(self, value, pieces, block, at=0, column=0):
            if not any(value is known for known in self.srcs):
                self.srcs.append(value)
            index = [value is known for known in self.srcs].index(True)
            for shard, dst_row, rows in pieces:
                self.copies.append((index, at, column, False, rows, shard, dst_row, block))
                at += rows

    whole = lambda shard: (shard, 0, 512)
    five, two = [whole(shard) for shard in (4, 1, 5, 2, 6)], [whole(3), whole(7)]
    early, late = Plan(), Plan()
    for block, (va, vb) in enumerate(((ya, yb), (ya_u, yb_u), (ya_d, yb_d))):
        early.land(va, five, block)
        early.land(vb, two, block)
    early.land(o_ab, [whole(4)], 3)
    early.land(up0, [whole(1)], 3, 1024)
    early.land(dn0, [whole(2)], 3, 1024)
    early.land(up1, [(3, 0, 256)], 3, 512)
    early.land(dn1, [(3, 256, 256)], 3, 512)
    early.land(a_x, [whole(5), whole(6), whole(7)], 3)
    for k in range(3):
        late.land(o_ab, [whole(4)], 1 + k, 0, 256 + 256 * k)
        late.land(b_up, [whole(1), whole(5)], 1 + k, 0, 256 * k)
        late.land(b_dn, [whole(2), whole(6)], 1 + k, 0, 256 * k)
        late.land(b_far0, [whole(3)], 1 + k, 0, 256 * k)
        late.land(b_far1, [whole(7)], 1 + k, 0, 256 * k)
    late.land(y_far0, five[:3] + [(2, 0, 256)], 0)
    late.land(y_far1, [(2, 256, 256), five[4]] + two, 0)
    shared = (a_own, a_par, res_own, r_par, low, up_half, q_rows, q_f)
    carry = block_call(early.copies, early.srcs, numbers(ring[:3] + [4]), *shared, None)
    hidden, stats_own = block_call(
        late.copies, late.srcs, numbers(ring[3:] + [5, 6, 7]), *shared, carry
    )

    got = send(stats_own, "core")
    tok = stats_own[:512] + jnp.concatenate([got[256:512], got[:256]], axis=0)
    qu_own = stats_own[512, :16] + stats_own[514, :16] + got[513, :16] + got[515, :16]
    qu_par = stats_own[513, :16] + stats_own[515, :16] + got[512, :16] + got[514, :16]
    position = jnp.arange(256, dtype=jnp.int32).astype(f32)
    len_own = lengths[0].astype(f32)
    w_tok = jnp.concatenate(
        [
            grad_scale * (position < len_own).astype(f32) / len_own,
            grad_scale * (position < len_par).astype(f32) / len_par,
        ]
    )
    inv = lax.rsqrt(tok[:, 16] / 4096 + epsilon)
    lead = inv * w_tok
    back = inv * inv * inv * (w_tok * tok[:, 17] / 4096)
    qu = jnp.concatenate(
        [jnp.broadcast_to(qu_own[None], (256, 16)), jnp.broadcast_to(qu_par[None], (256, 16))], 0
    )
    low_grad = (adapter_scale * (lead[:, None] * qu - back[:, None] * tok[:, :16])).astype(bf16)
    q_tok = jnp.concatenate(
        [jnp.broadcast_to(q_own, (256, 2048)), jnp.broadcast_to(q_par, (256, 2048))], axis=0
    )
    res_grad = (lead[:, None] * q_tok - back[:, None] * hidden).astype(bf16)
    r_got = send(res_grad[256:], "core")
    residual_grad = ordered(c, res_grad[:256], r_got, axis=1)
    srcs, copies = [], []
    for plan, shift in ((early, 0), (late, 4)):
        for index, at, column, from_half, rows, shard, dst_row, block in plan.copies:
            value = plan.srcs[index]
            if not any(value is known for known in srcs):
                srcs.append(value)
            index = [value is known for known in srcs].index(True)
            copies.append((index, at, column, from_half, rows, shard, dst_row, block + shift))
    y_own, y_par = back_call(
        copies,
        srcs,
        numbers(ring[:3] + [4] + ring[3:] + [5, 6, 7]),
        res_grad,
        low_grad[:256],
        adapter_down_weight.T,
    )
    y_got = send(y_par, "core")
    attn_grad = (y_own.astype(f32) + y_got.astype(f32)).astype(bf16)

    up_part = adapter_scale * lax.dot_general(low, res_grad, TN, preferred_element_type=f32)
    down_part = lax.dot_general(
        low_grad[:256], pick(a_own, half, 2048, 1), TN, preferred_element_type=f32
    ) + lax.dot_general(low_grad[256:], pick(a_par, half, 2048, 1), TN, preferred_element_type=f32)
    tail = jnp.pad(loss_sums[None], ((0, 7), (0, 2046)))
    total = jnp.concatenate([down_part / 128, up_part / 128, tail], axis=0)
    sides = [[i for i in range(128) if coords(i)[3] == side] for side in range(2)]
    swap = lambda value: lax.all_to_all(
        value, AX, 0, 0, axis_index_groups=sides, tiled=True
    )
    packed_total = total
    part = jnp.sum(swap(total.reshape(64, 1280)), axis=0, keepdims=True)
    total = swap(jnp.broadcast_to(part, (64, 1280))).reshape(40, 2048)
    mate = send(total, "core")
    loss = (total[32, 0] + mate[32, 0]) / 512
    scale_grad = (total[32, 1] + mate[32, 1]) / 512
    lora_down = ordered(c, total[:16], mate[:16], axis=1).T
    lora_up = ordered(c, total[16:32], mate[16:32], axis=1)

    p_sum = p_part
    for bit, n, move, until in (
        (z // 2, 64, "zflip", stats_own),
        (z % 2, 32, "znear", packed_total),
        (y // 2, 16, "yflip", y_par),
        (y % 2, 8, "ynear", attn_grad),
    ):
        got = send(pick(p_sum, n * (1 - bit), n), move)
        got, p_sum, _ = lax.optimization_barrier((got, p_sum, until))
        p_sum = pick(p_sum, n * bit, n) + got
    p_sum = logit_scale * p_sum
    keep = jnp.concatenate([pick(q_sum, 4 * c, 4), pick(p_sum, 4 * c, 4)], axis=0)
    give = jnp.concatenate([pick(q_sum, 4 * (1 - c), 4), pick(p_sum, 4 * (1 - c), 4)], axis=0)
    grads = ordered(c, keep, send(give, "core"), axis=1)
    return (
        loss,
        scale_grad,
        grads[:4],
        grads[4:],
        attn_grad[None],
        residual_grad[None],
        lora_down,
        lora_up,
    )


def solution(mesh):
    placed = (
        P(AX, None),
        P(AX, None),
        P(AX),
        P(),
        P(AX, None, None),
        P(AX, None, None),
        P("fsdp", None),
        P(),
        P(),
        P(),
        P(AX),
    )
    return jax.shard_map(
        compute,
        mesh=mesh,
        in_specs=placed,
        out_specs=(
            P(),
            P(),
            P(AX, None),
            P(AX, None),
            P(AX, None, None),
            P(AX, None, None),
            P(),
            P(),
        ),
        check_vma=False,
    )
```
